32 devices in a mesh: dp: 8 (over y, x, core), seq: 4 (over z).
Axes of the slice: x: 2, y: 2, z: 4, core: 2. Of those that a mesh axis runs over, the one named last changes fastest.
Arguments:
- tokens: bfloat16 [8192, 1152], P(('dp', 'seq')), may hold values from -6 to 6
- modulation: bfloat16 [32, 6912], P('dp'), may hold values from -4 to 4
- image_ids: int32 [8192], P('dp'), may hold values from 0 to 3, as said below
- w_qkv: bfloat16 [1152, 3456], replicated, may hold values from -0.1875 to 0.1875
- w_out: bfloat16 [1152, 1152], replicated, may hold values from -3 to 3
- w_fc1: bfloat16 [1152, 4608], replicated, may hold values from -0.1875 to 0.1875
- w_fc2: bfloat16 [4608, 1152], replicated, may hold values from -0.09375 to 0.09375
- w_proj1: bfloat16 [1152, 2048], replicated, may hold values from -0.1875 to 0.1875
- w_proj2: bfloat16 [2048, 2048], replicated, may hold values from -0.125 to 0.125
- w_proj3: bfloat16 [2048, 768], replicated, may hold values from -0.125 to 0.125
- dino: bfloat16 [8192, 768], P(('dp', 'seq')), may hold values from -6 to 6
- cotangent: bfloat16 [8192, 1152], P(('dp', 'seq')), may hold values from -6 to 6
Outputs:
- block_out: bfloat16 [8192, 1152], P(('dp', 'seq'))
- grad_tokens: bfloat16 [8192, 1152], P(('dp', 'seq'))
- grad_modulation: float32 [32, 6912], P('dp', 'seq')
- grad_qkv: float32 [1152, 3456], P('dp', 'seq')
- grad_out: float32 [1152, 1152], P('dp', 'seq')
- grad_fc1: float32 [1152, 4608], P('dp', 'seq')
- grad_fc2: float32 [4608, 1152], P('dp', 'seq')
- grad_proj1: float32 [1152, 2048], P('dp', 'seq')
- grad_proj2: float32 [2048, 2048], P('dp', 'seq')
- grad_proj3: float32 [2048, 768], P('dp', 'seq')
The draws below stay inside these ranges and needn't reach their ends.
Inputs may be any that keep to these rules, and one draw needn't show every extreme that they name: `image_ids`: each aligned run of 1024 tokens is either one image, all its tokens with id 4 * r, or four images of 256 tokens in order with ids 4 * r to 4 * r + 3, where r (0 to 0) is the run's place within its group; the groups of 1024 tokens lie one to an index of dp.
All inputs are finite; a program needn't handle non-finite values.
Results may differ from the reference program's by a relative error of at most 0.022.
Values may be sent and summed in bfloat16 or wider, within the bound.
No kernel may reach another device: no remote copies, remote signals or barrier semaphores. Data moves between devices by JAX's collectives and lax.ppermute only.
A program may use at most 320 MiB of HBM per device.

```python
import jax
import jax.numpy as jnp
from jax import lax

D = 1152
H = 16
HD = 72
FF = 4608
P1 = 2048
ZD = 768
LEN = 1024
ROWS = 1
TOKENS = 8192
IMAGES = 32
N_DP = 8


def draw_image_ids(key, part):
    runs = TOKENS // LEN
    kinds = jax.random.randint(key, (runs,), 0, 2)
    kinds = jnp.where(jnp.arange(runs, dtype=jnp.int32) == runs - 1, 1, kinds)
    place = jnp.arange(TOKENS, dtype=jnp.int32)
    run_index = place // LEN
    within = place % LEN
    local_run = run_index % ROWS
    image_slot = local_run * 4 + kinds[run_index] * (within // (LEN // 4))
    return image_slot.astype(jnp.int32)


def with_spikes(drawn, rng, source, target, shards_of, factor):
    def block_of(axis_at):
        return (jnp.arange(drawn.shape[axis_at]) // (drawn.shape[axis_at] // shards_of)).reshape((-1,) + (1,) * (drawn.ndim - 1 - axis_at))

    one_side = jax.random.permutation(rng, shards_of)[block_of(target)]
    second = (block_of(target) + shards_of // 2) % shards_of
    return jnp.where((block_of(source) == one_side) | (block_of(source) == second), factor * drawn, drawn)


def shard_levels(own_key, shape, pieces, least, high):
    gain, own = 1.0, jax.random.fold_in(own_key, 6)
    for position, shards_of in pieces:
        heights = jnp.exp(jax.random.uniform(jax.random.fold_in(own, position), (shards_of,), jnp.float32, least / len(pieces), high / len(pieces)))
        gain = gain * jnp.repeat(heights, shape[position] // shards_of).reshape([-1 if axis == position else 1 for axis in range(len(shape))])
    return gain


def bell_draw(stream_key, shape, scale, reach, cuts=(), held_as=jnp.bfloat16):
    array = jax.random.normal(stream_key, shape, jnp.float32) * scale
    if len(cuts) > 0:
        array = shard_levels(stream_key, shape, cuts, -0.22, 0.18) * array
    return jnp.clip(array, min=-reach, max=reach).astype(held_as)


def bell_draw_with(rng, extent, scale, limit, shards, heavy, kind=jnp.bfloat16):
    drawn = scale * jax.random.normal(rng, extent, jnp.float32)
    if shards:
        drawn = drawn * shard_levels(rng, extent, shards, -0.22, 0.18)
    return jnp.clip(with_spikes(drawn, jax.random.fold_in(rng, 3), *heavy), -limit, limit).astype(kind)


def setup_inputs(seed: int = 0) -> dict:
    splits = jax.random.split(jax.random.key(seed), 13)
    tokens = bell_draw(splits[0], (TOKENS, D), 1.0, 6.0, ((0, 32),))
    modulation = bell_draw(splits[1], (IMAGES, 6 * D), 0.7, 4.0, ((0, 8),))
    image_ids = draw_image_ids(jax.random.fold_in(splits[12], 71), 0)
    w_qkv = bell_draw(splits[3], (D, 3 * D), D ** -0.5, 0.1875)
    w_out = bell_draw(splits[4], (D, D), (max(D // 256, 1)) ** -0.5, 3.0)
    w_fc1 = bell_draw(splits[5], (D, FF), D ** -0.5, 0.1875)
    w_fc2 = bell_draw(splits[6], (FF, D), FF ** -0.5, 0.09375)
    w_proj1 = bell_draw(splits[7], (D, P1), D ** -0.5, 0.1875)
    w_proj2 = bell_draw(splits[8], (P1, P1), P1 ** -0.5, 0.125)
    w_proj3 = bell_draw(splits[9], (P1, ZD), P1 ** -0.5, 0.125)
    dino = bell_draw(splits[10], (TOKENS, ZD), 1.0, 6.0, ((0, 32),))
    cotangent = bell_draw_with(splits[11], (TOKENS, D), 1.0, 6.0, ((0, 32),), (0, 1, 32, 2.75))
    return {"tokens": tokens, "modulation": modulation, "image_ids": image_ids, "w_qkv": w_qkv, "w_out": w_out, "w_fc1": w_fc1, "w_fc2": w_fc2, "w_proj1": w_proj1, "w_proj2": w_proj2, "w_proj3": w_proj3, "dino": dino, "cotangent": cotangent}


@jax.custom_vjp
def low(v):
    return lax.optimization_barrier(v.astype(jnp.bfloat16)).astype(jnp.float32)

@jax.custom_vjp
def low_back(v):
    return v

def low_keep(v):
    return (low(v), None)

def low_pass(kept, grad):
    return (grad,)

def back_keep(v):
    return (v, None)

def back_low(kept, grad):
    return (low(grad),)
low.defvjp(low_keep, low_pass)
low_back.defvjp(back_keep, back_low)
EPS_NORM = 1e-06
HIGH = lax.Precision.HIGHEST

def matmul(left, right):
    return jnp.dot(left, right, precision=HIGH, preferred_element_type=jnp.float32)

def normalize(v):
    centre = v - lax.optimization_barrier(jnp.mean(v, axis=-1, keepdims=True))
    return centre * lax.rsqrt(lax.optimization_barrier(jnp.mean(centre * centre, axis=-1, keepdims=True)) + EPS_NORM)

def attend_row(block):
    queries, keys, values, ids_row = block
    raw = jnp.einsum('qhd,khd->hqk', queries, keys, precision=HIGH) * HD ** (-0.5)
    same = ids_row[:, None] == ids_row[None, :]
    scores = jnp.where(same[None], low_back(raw), -1e+30)
    probs = jax.nn.softmax(scores, axis=-1)
    return jnp.einsum('hqk,khd->qhd', low(probs), values, precision=HIGH)
attend = jax.checkpoint(attend_row)

def group_forward(xg, mg, idg, targets, weights):
    w_qkv, w_out, w_fc1, w_fc2, w_proj1, w_proj2, w_proj3 = weights
    mods = jnp.take(mg, idg, axis=0)
    shift1 = mods[:, 0:D]
    scale1 = mods[:, D:2 * D]
    gate1 = mods[:, 2 * D:3 * D]
    shift2 = mods[:, 3 * D:4 * D]
    scale2 = mods[:, 4 * D:5 * D]
    gate2 = mods[:, 5 * D:6 * D]
    first = low(normalize(xg) * (1.0 + scale1) + shift1)
    qkv = low(low_back(matmul(first, w_qkv)))
    split = qkv.reshape(ROWS, LEN, 3, H, HD)
    ids_rows = idg.reshape(ROWS, LEN)
    attended = lax.map(attend, (split[:, :, 0], split[:, :, 1], split[:, :, 2], ids_rows))
    heads_out = low(low_back(attended.reshape(ROWS * LEN, D)))
    attn = low_back(matmul(heads_out, w_out))
    hidden1 = xg + gate1 * attn
    second = low(normalize(hidden1) * (1.0 + scale2) + shift2)
    upper = low_back(matmul(second, w_fc1))
    active = low(jax.nn.gelu(upper, approximate=True))
    mlp = low_back(matmul(active, w_fc2))
    out_y = hidden1 + gate2 * mlp
    rounded = low(out_y)
    proj_r1 = low_back(matmul(rounded, w_proj1))
    proj_a1 = low(jax.nn.silu(proj_r1))
    proj_r2 = low_back(matmul(proj_a1, w_proj2))
    proj_a2 = low(jax.nn.silu(proj_r2))
    latent = low_back(matmul(proj_a2, w_proj3))
    cosine = lax.optimization_barrier(jnp.sum(latent * targets, axis=-1)) * lax.rsqrt(lax.optimization_barrier(jnp.sum(latent * latent, axis=-1)) + EPS_NORM) * lax.rsqrt(lax.optimization_barrier(jnp.sum(targets * targets, axis=-1)) + EPS_NORM)
    return (out_y, -0.5 * jnp.sum(cosine))

def reference(tokens, modulation, image_ids, w_qkv, w_out, w_fc1, w_fc2, w_proj1, w_proj2, w_proj3, dino, cotangent):
    weights = (w_qkv.astype(jnp.float32), w_out.astype(jnp.float32), w_fc1.astype(jnp.float32), w_fc2.astype(jnp.float32), w_proj1.astype(jnp.float32), w_proj2.astype(jnp.float32), w_proj3.astype(jnp.float32))
    group_x = tokens.astype(jnp.float32).reshape(N_DP, ROWS * LEN, D)
    group_m = modulation.astype(jnp.float32).reshape(N_DP, 4 * ROWS, 6 * D)
    group_ids = image_ids.reshape(N_DP, ROWS * LEN)
    group_t = dino.astype(jnp.float32).reshape(N_DP, ROWS * LEN, ZD)
    group_c = cotangent.astype(jnp.float32).reshape(N_DP, ROWS * LEN, D)

    def step(totals, group):
        xg, mg, idg, targets, cots = group

        def forward(xin, modin, wq, wo, wf1, wf2, wp1, wp2, wp3):
            return group_forward(xin, modin, idg, targets, (wq, wo, wf1, wf2, wp1, wp2, wp3))
        (out_y, loss), pull = jax.vjp(forward, xg, mg, *weights)
        grads = pull((cots, jnp.ones_like(loss)))
        totals = tuple((acc + new for acc, new in zip(totals, grads[2:])))
        return (totals, (out_y.astype(jnp.bfloat16), grads[0].astype(jnp.bfloat16), grads[1]))
    zeros = tuple((jnp.zeros_like(weight) for weight in weights))
    totals, (outs_y, outs_dx, outs_dm) = lax.scan(step, zeros, (group_x, group_m, group_ids, group_t, group_c))
    return (outs_y.reshape(TOKENS, D), outs_dx.reshape(TOKENS, D), outs_dm.reshape(IMAGES, 6 * D), totals[0], totals[1], totals[2], totals[3], totals[4], totals[5], totals[6])
```

```python
import functools

import jax
import jax.numpy as jnp
from jax import lax
from jax.experimental import pallas as pl
from jax.experimental.pallas import tpu as pltpu
from jax.sharding import PartitionSpec as P

H = 16
HD = 72
HP = 80
LEN = 1024
EPS_NORM = 1e-06
SCALE = HD ** (-0.5)
EXP2_SCALE = SCALE * 1.4426950408889634
GELU_A = 0.7978845608028654
GELU_B = 0.044715
BF = jnp.bfloat16
F32 = jnp.float32
ANY = pl.BlockSpec(memory_space=pl.ANY)
VMEM = pl.BlockSpec(memory_space=pltpu.VMEM)
SMEM = pl.BlockSpec(memory_space=pltpu.SMEM)
ROOM = 60 << 20


def matmul(left, right):
    return jnp.dot(left, right, preferred_element_type=F32)


def times_trans(left, right):
    return lax.dot_general(left, right, (((1,), (1,)), ((), ())), preferred_element_type=F32)


def trans_times(left, right):
    return lax.dot_general(left, right, (((0,), (0,)), ((), ())), preferred_element_type=F32)


def row_mean(v):
    return jnp.mean(v, axis=-1, keepdims=True)


def normalize(v):
    centre = v - row_mean(v)
    inv = lax.rsqrt(row_mean(centre * centre) + EPS_NORM)
    return centre * inv, inv


def norm_back(e, normed, inv):
    return (e - row_mean(e) - normed * row_mean(e * normed)) * inv


def col_sum(v):
    return jnp.sum(v, axis=0, keepdims=True)


def sigmoid(v):
    return 1.0 / (1.0 + jnp.exp(-v))


def shape(dims, kind=BF):
    return jax.ShapeDtypeStruct(dims, kind)


def params(**more):
    return pltpu.CompilerParams(vmem_limit_bytes=ROOM, **more)


def enter_kernel(slot_ref, tokens_ref, mod_ref, mods_ref, out_ref):
    width = tokens_ref.shape[1]
    table = mod_ref[...].astype(F32)
    mine = lax.broadcasted_iota(jnp.int32, table.shape, 0) == slot_ref[0]
    mods = col_sum(jnp.where(mine, table, 0.0))
    mods_ref[...] = jnp.zeros_like(mods_ref)
    for i in range(6):
        mods_ref[i : i + 1, :] = mods[:, i * width : (i + 1) * width]
    normed, _ = normalize(tokens_ref[...].astype(F32))
    first = normed * (1.0 + mods[:, width : 2 * width]) + mods[:, 0:width]
    out_ref[...] = jnp.transpose(first.astype(BF))


def enter(slot, tokens, modulation):
    tok, width = tokens.shape
    return pl.pallas_call(
        enter_kernel,
        out_shape=(shape((8, width), F32), shape((width, tok))),
        in_specs=[SMEM, VMEM, VMEM],
        out_specs=(VMEM, VMEM),
        compiler_params=params(),
        name="enter",
    )(slot, tokens, modulation)


def attend_forward_kernel(size, heads, tile, diagonal, one_ref, *refs):
    pieces = refs[: 2 * size - 1]
    w_ref, idk_ref, idq_ref, x_ref, o_ref, qkv_ref, lse_ref, k_ref, o_all_ref = refs[2 * size - 1 :]
    tok = pieces[0].shape[1]
    total = x_ref.shape[1]
    x_ref[:, 0:tok] = pieces[0][...]
    for d in range(1, size):
        x_ref[:, d * tok : (d + 1) * tok] = pieces[2 * d - 1][...] + pieces[2 * d][...]

    def project(i, carry):
        at = pl.ds(pl.multiple_of(i * tile, tile), tile)
        qkv_ref[:, at] = matmul(w_ref[...], x_ref[:, at]).astype(BF)
        return carry

    lax.fori_loop(0, total // tile, project, 0)

    def head_step(head, carry):
        q_at = pl.ds(pl.multiple_of(head * HP, HP), HP)
        k_at = pl.ds(pl.multiple_of((heads + head) * HP, HP), HP)
        v_at = pl.ds(pl.multiple_of((2 * heads + head) * HP, HP), HP)
        o_at = pl.ds(pl.multiple_of(head * HD, 8), HD)
        k_ref[...] = jnp.transpose(qkv_ref[k_at, :])

        def block(at, keys, masked):
            s = matmul(k_ref[keys, :], qkv_ref[q_at, at]) * EXP2_SCALE
            if masked:
                s = jnp.where(idk_ref[...] == idq_ref[:, at], s, -1e30)
            top = jnp.max(s, axis=0, keepdims=True)
            e = jnp.exp2(s - top)
            tot = col_sum(e)
            o = matmul(qkv_ref[v_at, keys], e.astype(BF)) * (1.0 / tot)
            o_all_ref[o_at, at] = o[0:HD, :]
            lse_ref[pl.ds(head, 1), at] = top + jnp.log2(tot)

        def full(masked):
            def step(i, inner):
                block(pl.ds(pl.multiple_of(i * tile, tile), tile), pl.ds(0, total), masked)
                return inner

            lax.fori_loop(0, total // tile, step, 0)

        @pl.when(one_ref[0] == 1)
        def _():
            full(False)

        @pl.when(one_ref[0] == 0)
        def _():
            if diagonal:

                def step(i, inner):
                    at = pl.ds(pl.multiple_of(i * tile, tile), tile)
                    block(at, at, False)
                    return inner

                lax.fori_loop(0, total // tile, step, 0)
            else:
                full(True)

        return carry

    lax.fori_loop(0, heads, head_step, 0)
    for d in range(size):
        o_ref[d] = o_all_ref[:, d * tok : (d + 1) * tok].astype(BF)


def attend_forward(one, pieces, w, idk, idq, heads, tile, diagonal):
    width, tok = pieces[0].shape
    size = (len(pieces) + 1) // 2
    total = size * tok
    return pl.pallas_call(
        functools.partial(attend_forward_kernel, size, heads, tile, diagonal),
        out_shape=(
            shape((width, total)),
            shape((size, heads * HD, tok)),
            shape((3 * heads * HP, total)),
            shape((heads, total), F32),
        ),
        in_specs=[SMEM] + [VMEM] * (len(pieces) + 3),
        out_specs=(VMEM,) * 4,
        scratch_shapes=[pltpu.VMEM((total, HP), BF), pltpu.VMEM((heads * HD, total), F32)],
        compiler_params=params(),
        name="attend_forward",
    )(one, *pieces, w, idk, idq)


def attend_backward_kernel(size, heads, tile, diagonal, one_ref, *refs):
    do_refs = refs[:size]
    qkv_ref, o_ref, lse_ref, w_ref, idk_ref, idq_ref = refs[size : size + 6]
    dqkv_ref, dx_ref, k_ref, v_ref, do_ref, dk_ref, dv_ref, acc_ref, delta_ref = refs[size + 6 :]
    tok = do_refs[0].shape[1]
    total = qkv_ref.shape[1]
    local = heads * HD
    for d in range(size):
        at = slice(d * tok, (d + 1) * tok)
        do = do_refs[d][...].astype(F32)
        do_ref[0:local, at] = do
        do_ref[local : local + HP - HD, at] = jnp.zeros((HP - HD, tok), F32)
        prod = do * o_ref[d].astype(F32)
        for head in range(heads):
            delta_ref[head : head + 1, at] = col_sum(prod[head * HD : (head + 1) * HD, :])

    def head_step(head, carry):
        q_at = pl.ds(pl.multiple_of(head * HP, HP), HP)
        k_at = pl.ds(pl.multiple_of((heads + head) * HP, HP), HP)
        v_at = pl.ds(pl.multiple_of((2 * heads + head) * HP, HP), HP)
        o_at = pl.ds(pl.multiple_of(head * HD, 8), HP)
        k_ref[...] = jnp.transpose(qkv_ref[k_at, :])
        v_ref[...] = jnp.transpose(qkv_ref[v_at, :])

        def out_at(part):
            return pl.ds(pl.multiple_of(part * local + head * HD, 8), HD)

        def block(at, keys, masked, fresh):
            q = qkv_ref[q_at, at]
            do = do_ref[o_at, at].astype(BF)
            p = jnp.exp2(matmul(k_ref[keys, :], q) * EXP2_SCALE - lse_ref[pl.ds(head, 1), at])
            if masked:
                p = jnp.where(idk_ref[...] == idq_ref[:, at], p, 0.0)
            ds = (p * (matmul(v_ref[keys, :], do) - delta_ref[pl.ds(head, 1), at])).astype(BF)
            dv = times_trans(do, p.astype(BF))
            dk = times_trans(q, ds)
            if fresh:
                dv_ref[:, keys] = dv
                dk_ref[:, keys] = dk
            else:
                dv_ref[:, keys] += dv
                dk_ref[:, keys] += dk
            dq = matmul(qkv_ref[k_at, keys], ds) * SCALE
            acc_ref[out_at(0), at] = dq[0:HD, :]

        def full(masked):
            dk_ref[...] = jnp.zeros_like(dk_ref)
            dv_ref[...] = jnp.zeros_like(dv_ref)

            def step(i, inner):
                block(pl.ds(pl.multiple_of(i * tile, tile), tile), pl.ds(0, total), masked, False)
                return inner

            lax.fori_loop(0, total // tile, step, 0)

        @pl.when(one_ref[0] == 1)
        def _():
            full(False)

        @pl.when(one_ref[0] == 0)
        def _():
            if diagonal:

                def step(i, inner):
                    at = pl.ds(pl.multiple_of(i * tile, tile), tile)
                    block(at, at, False, True)
                    return inner

                lax.fori_loop(0, total // tile, step, 0)
            else:
                full(True)

        acc_ref[out_at(1), :] = dk_ref[0:HD, :] * SCALE
        acc_ref[out_at(2), :] = dv_ref[0:HD, :]
        return carry

    lax.fori_loop(0, heads, head_step, 0)
    dqkv_ref[...] = acc_ref[...].astype(BF)
    for d in range(size):
        dx_ref[d] = trans_times(dqkv_ref[:, d * tok : (d + 1) * tok], w_ref[...]).astype(BF)


def attend_backward(one, dos, qkv, o, lse, w, idk, idq, heads, tile, diagonal):
    size = len(dos)
    local, tok = dos[0].shape
    total = size * tok
    width = w.shape[1]
    return pl.pallas_call(
        functools.partial(attend_backward_kernel, size, heads, tile, diagonal),
        out_shape=(shape((3 * local, total)), shape((size, tok, width))),
        in_specs=[SMEM] + [VMEM] * (size + 6),
        out_specs=(VMEM, VMEM),
        scratch_shapes=[
            pltpu.VMEM((total, HP), BF),
            pltpu.VMEM((total, HP), BF),
            pltpu.VMEM((local + HP - HD, total), F32),
            pltpu.VMEM((HP, total), F32),
            pltpu.VMEM((HP, total), F32),
            pltpu.VMEM((3 * local, total), F32),
            pltpu.VMEM((heads, total), F32),
        ],
        compiler_params=params(),
        name="attend_backward",
    )(one, *dos, qkv, o, lse, w, idk, idq)


STEP = 512


def fetch_rows(rank, size, w_ref, held_ref, sems):
    local = w_ref.shape[0] // size
    copies = []
    for d in range(size):
        block = lax.rem(rank - d + size, size)
        copies.append(
            pltpu.make_async_copy(
                w_ref.at[pl.ds(pl.multiple_of(block * local, local), local), :],
                held_ref.at[pl.ds(d * local, local), :],
                sems.at[d],
            )
        )
    return copies


def middle_kernel(size, rank_ref, *refs):
    o_refs = refs[:size]
    (tokens_ref, mods_ref, dino_ref, cot_ref, wo_any, w1_any, w2_any, p1_any, p2_any, p3_any) = refs[size : size + 10]
    (out_ref, b_ref, g_ref, y_ref, a1_ref, a2_ref, gp_ref, dz_ref, dr2_ref, dr1_ref,
     dmlp_ref, dy_ref, normed_ref, inv_ref, attn_ref, gate_ref) = refs[size + 10 : size + 26]
    (wo_ref, w1_ref, w2_ref, p1_ref, p2_ref, p3_ref, act_ref, o_ref, wo_sem, w1_sem, sems) = refs[size + 26 :]
    local, tok = o_refs[0].shape
    hidden = w1_any.shape[1]
    steps = hidden // STEP
    slots = w1_ref.shape[0]
    wo_copies = fetch_rows(rank_ref[0], size, wo_any, wo_ref, wo_sem)
    for copy in wo_copies:
        copy.start()

    def w1_copy(i):
        at = pl.ds(pl.multiple_of(i * STEP, STEP), STEP)
        slot = lax.rem(i, slots)
        return pltpu.make_async_copy(w1_any.at[:, at], w1_ref.at[slot], w1_sem.at[slot])

    for i in range(slots):
        w1_copy(i).start()
    w2_copy = pltpu.make_async_copy(w2_any, w2_ref, sems.at[0])
    p1_copy = pltpu.make_async_copy(p1_any, p1_ref, sems.at[1])
    p2_copy = pltpu.make_async_copy(p2_any, p2_ref, sems.at[2])
    p3_copy = pltpu.make_async_copy(p3_any, p3_ref, sems.at[3])
    for copy in (w2_copy, p1_copy, p2_copy, p3_copy):
        copy.start()

    gate1, shift2, scale2, gate2 = [mods_ref[i : i + 1, :] for i in (2, 3, 4, 5)]
    for d in range(size):
        o_ref[d * local : (d + 1) * local, :] = o_refs[d][...]
    for copy in wo_copies:
        copy.wait()
    attn = trans_times(o_ref[...], wo_ref[...])
    attn_ref[...] = attn
    h1 = tokens_ref[...].astype(F32) + gate1 * attn
    normed, inv = normalize(h1)
    normed_ref[...] = normed
    inv_ref[...] = inv
    b = (normed * (1.0 + scale2) + shift2).astype(BF)
    b_ref[...] = jnp.transpose(b)

    def up(i, carry):
        at = pl.ds(pl.multiple_of(i * STEP, STEP), STEP)
        w1_copy(i).wait()
        u = matmul(b, w1_ref[lax.rem(i, slots)])

        @pl.when(i + slots < steps)
        def _():
            w1_copy(i + slots).start()

        sq = u * u
        t = jnp.tanh(u * (GELU_A + (GELU_A * GELU_B) * sq))
        half = 0.5 * (1.0 + t)
        g = (u * half).astype(BF)
        gp_ref[:, at] = (half + u * (1.0 - t * t) * (0.5 * GELU_A + (1.5 * GELU_A * GELU_B) * sq)).astype(BF)
        act_ref[:, at] = g
        g_ref[at, :] = jnp.transpose(g)
        return carry

    lax.fori_loop(0, steps, up, 0)
    w2_copy.wait()
    mlp = matmul(act_ref[...], w2_ref[...])
    y = (h1 + gate2 * mlp).astype(BF)
    out_ref[...] = y
    y_ref[...] = jnp.transpose(y)
    wide = p1_ref.shape[1]

    def project(source, w_ref, held, out_t_ref, slope_ref):
        def step(i, carry):
            at = pl.ds(pl.multiple_of(i * STEP, STEP), STEP)
            r = matmul(source, w_ref[:, at])
            sig = sigmoid(r)
            act = (r * sig).astype(BF)
            act_ref[:, pl.ds(pl.multiple_of(held + i * STEP, STEP), STEP)] = act
            out_t_ref[at, :] = jnp.transpose(act)
            slope_ref[:, at] = (sig * (1.0 + r * (1.0 - sig))).astype(BF)
            return carry

        lax.fori_loop(0, wide // STEP, step, 0)
        return act_ref[:, held : held + wide]

    def project_back(source, w_ref, slope_ref):
        def step(i, carry):
            at = pl.ds(pl.multiple_of(i * STEP, STEP), STEP)
            slope_ref[:, at] = (times_trans(source, w_ref[at, :]) * slope_ref[:, at].astype(F32)).astype(BF)
            return carry

        lax.fori_loop(0, wide // STEP, step, 0)
        return slope_ref[...]

    p1_copy.wait()
    a1 = project(y, p1_ref, 0, a1_ref, dr1_ref)
    p2_copy.wait()
    a2 = project(a1, p2_ref, wide, a2_ref, dr2_ref)
    p3_copy.wait()
    z = matmul(a2, p3_ref[...])
    t = dino_ref[...].astype(F32)
    nz = lax.rsqrt(jnp.sum(z * z, axis=-1, keepdims=True) + EPS_NORM)
    nt = lax.rsqrt(jnp.sum(t * t, axis=-1, keepdims=True) + EPS_NORM)
    cosine = jnp.sum(z * t, axis=-1, keepdims=True) * nz * nt
    dz = (-0.5 * (t * (nz * nt) - (cosine * nz * nz) * z)).astype(BF)
    dz_ref[...] = dz
    dr2 = project_back(dz, p3_ref, dr2_ref)
    dr1 = project_back(dr2, p2_ref, dr1_ref)
    dy = cot_ref[...].astype(F32) + times_trans(dr1, p1_ref[...])
    dy_ref[...] = dy
    dmlp_ref[...] = (gate2 * dy).astype(BF)
    gate_ref[...] = col_sum(dy * mlp)


def middle(rank, os, tokens, mods, dino, cot, wo, w1, w2, p1, p2, p3):
    size = len(os)
    tok, width = tokens.shape
    hidden, wide, narrow = w1.shape[1], p1.shape[1], p3.shape[1]
    return pl.pallas_call(
        functools.partial(middle_kernel, size),
        out_shape=(
            shape((tok, width)), shape((width, tok)), shape((hidden, tok)), shape((width, tok)),
            shape((wide, tok)), shape((wide, tok)), shape((tok, hidden)), shape((tok, narrow)),
            shape((tok, wide)), shape((tok, wide)), shape((tok, width)), shape((tok, width), F32),
            shape((tok, width), F32), shape((tok, 1), F32), shape((tok, width), F32), shape((1, width), F32),
        ),
        in_specs=[SMEM] + [VMEM] * (size + 4) + [ANY] * 6,
        out_specs=(VMEM,) * 16,
        scratch_shapes=[pltpu.VMEM(dims, BF) for dims in (wo.shape, (4, width, STEP), w2.shape, p1.shape, p2.shape, p3.shape)]
        + [
            pltpu.VMEM((tok, hidden), BF),
            pltpu.VMEM((width, tok), BF),
            pltpu.SemaphoreType.DMA((size,)),
            pltpu.SemaphoreType.DMA((4,)),
            pltpu.SemaphoreType.DMA((4,)),
        ],
        compiler_params=params(),
        name="middle",
    )(rank, *os, tokens, mods, dino, cot, wo, w1, w2, p1, p2, p3)


def descend_kernel(size, rank_ref, *refs):
    (dmlp_ref, gp_ref, dy_ref, normed_ref, inv_ref, attn_ref, mods_ref, w2_any, w1_any, wo_any) = refs[:10]
    (du_ref, dh1_ref, dattn_ref, do_ref, sums_ref) = refs[10:15]
    (w2_ref, w1_ref, wo_ref, w2_sem, w1_sem, wo_sem) = refs[15:]
    hidden = w1_ref.shape[1]
    local = do_ref.shape[1]
    steps = hidden // STEP

    def w2_copy(i):
        at = pl.ds(pl.multiple_of(i * STEP, STEP), STEP)
        return pltpu.make_async_copy(w2_any.at[at, :], w2_ref.at[at, :], w2_sem.at[i])

    for i in range(steps):
        w2_copy(i).start()
    w1_copy = pltpu.make_async_copy(w1_any, w1_ref, w1_sem.at[0])
    w1_copy.start()
    wo_copies = fetch_rows(rank_ref[0], size, wo_any, wo_ref, wo_sem)
    for copy in wo_copies:
        copy.start()
    dmlp = dmlp_ref[...]

    def down(i, carry):
        at = pl.ds(pl.multiple_of(i * STEP, STEP), STEP)
        w2_copy(i).wait()
        du_ref[:, at] = (times_trans(dmlp, w2_ref[at, :]) * gp_ref[:, at].astype(F32)).astype(BF)
        return carry

    lax.fori_loop(0, steps, down, 0)
    w1_copy.wait()
    db = times_trans(du_ref[...], w1_ref[...])
    gate1, scale2 = mods_ref[2:3, :], mods_ref[4:5, :]
    normed = normed_ref[...]
    dh1 = dy_ref[...] + norm_back(db * (1.0 + scale2), normed, inv_ref[...])
    dh1_ref[...] = dh1
    dattn = (gate1 * dh1).astype(BF)
    dattn_ref[...] = dattn
    sums_ref[...] = jnp.zeros_like(sums_ref)
    sums_ref[0:1, :] = col_sum(dh1 * attn_ref[...])
    sums_ref[1:2, :] = col_sum(db)
    sums_ref[2:3, :] = col_sum(db * normed)
    for copy in wo_copies:
        copy.wait()
    for d in range(size):
        do_ref[d] = times_trans(wo_ref[d * local : (d + 1) * local, :], dattn).astype(BF)


def descend(rank, size, dmlp, gp, dy, normed, inv, attn, mods, w2, w1, wo):
    tok, width = dmlp.shape
    hidden = w1.shape[1]
    return pl.pallas_call(
        functools.partial(descend_kernel, size),
        out_shape=(
            shape((tok, hidden)), shape((tok, width), F32), shape((tok, width)),
            shape((size, width // size, tok)), shape((8, width), F32),
        ),
        in_specs=[SMEM] + [VMEM] * 7 + [ANY] * 3,
        out_specs=(VMEM,) * 5,
        scratch_shapes=[pltpu.VMEM(w.shape, BF) for w in (w2, w1, wo)]
        + [
            pltpu.SemaphoreType.DMA((hidden // STEP,)),
            pltpu.SemaphoreType.DMA((1,)),
            pltpu.SemaphoreType.DMA((size,)),
        ],
        compiler_params=params(),
        name="descend",
    )(rank, dmlp, gp, dy, normed, inv, attn, mods, w2, w1, wo)


def leave_kernel(part_ref, left_ref, right_ref, tokens_ref, dh1_ref, mods_ref, out_ref, sums_ref):
    da = part_ref[...].astype(F32) + left_ref[...].astype(F32) + right_ref[...].astype(F32)
    normed, inv = normalize(tokens_ref[...].astype(F32))
    out_ref[...] = (dh1_ref[...] + norm_back(da * (1.0 + mods_ref[1:2, :]), normed, inv)).astype(BF)
    sums_ref[...] = jnp.zeros_like(sums_ref)
    sums_ref[0:1, :] = col_sum(da)
    sums_ref[1:2, :] = col_sum(da * normed)


def leave(part, from_left, from_right, tokens, dh1, mods):
    return pl.pallas_call(
        leave_kernel,
        out_shape=(shape(tokens.shape), shape((8, tokens.shape[1]), F32)),
        in_specs=[VMEM] * 6,
        out_specs=(VMEM, VMEM),
        compiler_params=params(),
        name="leave",
    )(part, from_left, from_right, tokens, dh1, mods)


def weight_grad_kernel(count, flat, rows_ref, *refs):
    lefts, rights = refs[:count], refs[count : 2 * count]
    send_ref, keep_ref, held_ref = refs[2 * count :]
    half, rows, wide = send_ref.shape
    part = lefts[0].shape[1]

    @pl.when(pl.program_id(0) == 0)
    def _():
        for i in range(2 * half):
            at = pl.ds(pl.multiple_of(rows_ref[i], 16), rows)
            for j in range(count):
                held_ref[i * rows : (i + 1) * rows, j * part : (j + 1) * part] = lefts[j][at, :]

    dot = times_trans if flat else matmul
    for out_ref, base in ((send_ref, 0), (keep_ref, half * rows)):
        total = None
        for j in range(count):
            term = dot(held_ref[base : base + half * rows, j * part : (j + 1) * part], rights[j][...])
            total = term if total is None else total + term
        out_ref[...] = total.reshape(half, rows, wide).astype(BF)


def weight_grad(lefts, rights, row_starts, rows, step, flat=False):
    count = len(lefts)
    half = row_starts.shape[0] // 2
    part = lefts[0].shape[1]
    wide = rights[0].shape[0 if flat else 1]
    right_spec = (
        pl.BlockSpec((step, part), lambda i, b: (i, 0)) if flat else pl.BlockSpec((part, step), lambda i, b: (0, i))
    )
    out_spec = pl.BlockSpec((half, rows, step), lambda i, b: (0, 0, i))
    return pl.pallas_call(
        functools.partial(weight_grad_kernel, count, flat),
        out_shape=(shape((half, rows, wide)), shape((half, rows, wide))),
        grid_spec=pltpu.PrefetchScalarGridSpec(
            num_scalar_prefetch=1,
            grid=(wide // step,),
            in_specs=[pl.BlockSpec(a.shape, lambda i, b: (0, 0)) for a in lefts] + [right_spec] * count,
            out_specs=(out_spec, out_spec),
            scratch_shapes=[pltpu.VMEM((2 * half * rows, part * count), BF)],
        ),
        compiler_params=params(dimension_semantics=("arbitrary",)),
        name="weight_grad",
    )(row_starts, *lefts, *rights)


def flip(x, axis, size, bit):
    return lax.ppermute(x, axis, [(i, i ^ bit) for i in range(size)])


def add(a, b):
    return (a.astype(F32) + b.astype(F32)).astype(BF)


def after(x, *others):
    return lax.optimization_barrier((x,) + others)[0]


def masks_of(bits):
    out = []
    for i in range(2 ** len(bits)):
        mask = 0
        for spot, bit in enumerate(bits):
            if not (i >> (len(bits) - 1 - spot)) & 1:
                mask |= bit
        out.append(mask)
    return out


def halve(send, keep, axis, size, bits):
    for bit in bits[:-1]:
        got = flip(send, axis, size, bit)
        half = keep.shape[0] // 2
        send = add(keep[:half], got[:half])
        keep = add(keep[half:], got[half:])
    got = flip(send, axis, size, bits[-1])
    return add(keep, got)


def scatter_columns(share, rank, size):
    rows, cols = share.shape
    blocks = jnp.transpose(share.reshape(rows, size, cols // size), (1, 0, 2))
    bits = [1 << i for i in range(size.bit_length() - 1)]
    order = [lax.dynamic_slice_in_dim(blocks, rank ^ m, 1, 0) for m in masks_of(bits)]
    half = size // 2
    send = jnp.concatenate(order[:half], axis=0)
    keep = jnp.concatenate(order[half:], axis=0)
    return halve(send, keep, "seq", size, bits)[0]


def shards(
    tokens, modulation, image_ids, w_qkv, w_out, w_fc1, w_fc2, w_proj1, w_proj2, w_proj3, dino, cotangent,
):
    n_seq = lax.axis_size("seq")
    n_dp = lax.axis_size("dp")
    rank = lax.axis_index("seq")
    me = lax.axis_index("dp")
    tok_dev, width = tokens.shape
    group_tok = image_ids.shape[0]
    heads = H // n_seq
    local = heads * HD
    slots = modulation.shape[0]
    dp_bits = [1 << i for i in range(n_dp.bit_length() - 1)]
    rank_arg = rank.reshape(1).astype(jnp.int32)

    my_slot = lax.dynamic_slice_in_dim(image_ids, rank * tok_dev, 1)
    mods, first = enter(my_slot, tokens, modulation)

    right, left = [first], [first]
    for s in range(1, n_seq):
        right.append(lax.ppermute(right[-1], "seq", [(i, i + 1) for i in range(s - 1, n_seq - 1)]))
        left.append(lax.ppermute(left[-1], "seq", [(i, i - 1) for i in range(1, n_seq - s + 1)]))
    pieces = [first]
    for d in range(1, n_seq):
        pieces += [left[d], right[n_seq - d]]

    columns = [lax.dynamic_slice_in_dim(w_qkv, i * width + rank * local, local, 1) for i in range(3)]
    w_rows = jnp.transpose(jnp.concatenate(columns, axis=1))
    w_pad = jnp.pad(w_rows.reshape(3 * heads, HD, width), ((0, 0), (0, HP - HD), (0, 0))).reshape(3 * heads * HP, width)
    ids_rel = lax.dynamic_slice_in_dim(jnp.concatenate([image_ids, image_ids]), rank * tok_dev, group_tok)
    idk, idq = ids_rel[:, None], ids_rel[None, :]
    one = (image_ids[0] == image_ids[group_tok - 1]).astype(jnp.int32).reshape(1)
    tile = group_tok // 4
    diagonal = tok_dev % tile == 0

    first_all, heads_out, qkv, lse = attend_forward(one, pieces, w_pad, idk, idq, heads, tile, diagonal)

    attended = [heads_out[0]]
    for d in range(1, n_seq):
        attended.append(lax.ppermute(heads_out[d], "seq", [(i, (i + d) % n_seq) for i in range(n_seq)]))
    (rounded, second, active, rounded_t, proj_a1, proj_a2, gelu_slope, dlatent, dr2, dr1,
     dmlp, dy, normed2, inv2, attn, sum_gate2) = middle(
        rank_arg, attended, tokens, mods, dino, cotangent, w_out, w_fc1, w_fc2, w_proj1, w_proj2, w_proj3
    )

    fast = all(k % (16 * n_dp) == 0 for k in (width, w_fc2.shape[0], w_proj2.shape[0])) and n_dp > 2
    xy, yx = dp_bits[1:], dp_bits[:0:-1]

    def partial(lefts, rights, bits, starts, step):
        rows = lefts.shape[0] // n_dp
        pair = [flip(lefts, "dp", n_dp, 1), flip(rights, "dp", n_dp, 1)]
        return weight_grad([lefts, pair[0]], [rights, pair[1]], starts, rows, step)

    def starts_of(deep, bits):
        return (me ^ jnp.array(masks_of(bits), jnp.int32)) * (deep // n_dp)

    def finish(send, keep, bits):
        share = halve(send, keep, "dp", n_dp, bits)[0]
        return scatter_columns(share, rank, n_seq).astype(F32)

    if fast:
        deep = w_proj2.shape[0]
        p3 = partial(proj_a2, dlatent, xy, starts_of(deep, xy), 384)
        p2 = partial(proj_a1, dr2, yx, starts_of(deep, yx), 512)
        p1 = partial(rounded_t, dr1, xy, starts_of(width, xy), 512)
        dmlp = after(dmlp, p3[0], p2[0], p1[0])

    dupper, dhidden1, dattn, dheads, sums2 = descend(
        rank_arg, n_seq, dmlp, gelu_slope, dy, normed2, inv2, attn, mods, w_fc2, w_fc1, w_out
    )
    dheads_in = [dheads[0]]
    for d in range(1, n_seq):
        dheads_in.append(lax.ppermute(dheads[d], "seq", [(i, (i - d) % n_seq) for i in range(n_seq)]))
    attn_t = jnp.concatenate(attended, axis=0)
    if fast:
        f2 = partial(active, dmlp, yx, starts_of(w_fc2.shape[0], yx), 384)
        f1 = partial(second, dupper, xy, starts_of(width, xy), 1152)
        rows = width // n_dp
        starts = starts_of(width, yx)
        owner = starts // local
        fo = partial(attn_t, dattn, yx, ((rank - owner) % n_seq) * local + starts % local, 384)
        dheads_in[0] = after(dheads_in[0], f2[0])
    dqkv, dfirst_part = attend_backward(one, dheads_in, qkv, heads_out, lse, w_rows, idk, idq, heads, tile, diagonal)

    from_left, from_right = None, None
    for s in range(1, n_seq):
        up = dfirst_part[n_seq - s] if from_left is None else add(dfirst_part[n_seq - s], from_left)
        down = dfirst_part[s] if from_right is None else add(dfirst_part[s], from_right)
        from_left = lax.ppermute(up, "seq", [(i, i + 1) for i in range(s)])
        from_right = lax.ppermute(down, "seq", [(i, i - 1) for i in range(n_seq - s, n_seq)])
    grad_inputs, sums1 = leave(dfirst_part[0], from_left, from_right, tokens, dhidden1, mods)

    dmods = jnp.concatenate(
        [sums1[0:2], sums2[0:3], sum_gate2], axis=0
    ).reshape(n_seq, 1, 6 * width // n_seq)
    grad_mods = jnp.zeros((slots, 6 * width // n_seq), F32)
    slot = jnp.arange(slots, dtype=jnp.int32)[:, None]
    for d in range(n_seq):
        mine = lax.dynamic_index_in_dim(dmods, (rank + d) % n_seq, keepdims=False)
        got = lax.ppermute(mine, "seq", [(i, (i + d) % n_seq) for i in range(n_seq)]) if d else mine
        whose = lax.dynamic_slice_in_dim(image_ids, ((rank - d) % n_seq) * tok_dev, 1)
        grad_mods = grad_mods + jnp.where(slot == whose, got, 0.0)

    if fast:
        rows = width // n_dp
        fq = weight_grad([first_all], [dqkv], starts_of(width, dp_bits), rows, 3 * local, flat=True)
        g_proj3 = finish(*p3, xy)
        g_proj2 = finish(*p2, yx)
        g_proj1 = finish(*p1, xy)
        g_fc2 = finish(*f2, yx)
        g_fc1 = finish(*f1, xy)
        g_out = finish(*fo, yx)
        g_heads = halve(*fq, "dp", n_dp, dp_bits)[0]
    else:

        def reduced(a, b):
            share = lax.psum_scatter(matmul(a, b).astype(BF), "dp", scatter_dimension=0, tiled=True)
            return lax.psum_scatter(share, "seq", scatter_dimension=1, tiled=True).astype(F32)

        g_proj3 = reduced(proj_a2, dlatent)
        g_proj2 = reduced(proj_a1, dr2)
        g_proj1 = reduced(rounded_t, dr1)
        g_fc2 = reduced(active, dmlp)
        g_fc1 = reduced(second, dupper)
        ordered = jnp.concatenate(
            [lax.dynamic_slice_in_dim(attn_t, ((rank - j) % n_seq) * local, local, 0) for j in range(n_seq)], axis=0
        )
        g_out = reduced(ordered, dattn)
        g_heads = lax.psum_scatter(
            times_trans(first_all, dqkv).astype(BF), "dp", scatter_dimension=0, tiled=True
        )

    units = [g_heads[:, i * local : (i + 1) * local] for i in range(3)]
    columns = [jnp.zeros(units[0].shape, F32) for _ in range(3)]
    for d in range(n_seq):
        target, source = (rank + d) % n_seq, (rank - d) % n_seq
        mine = jnp.zeros_like(units[0])
        for i in range(3):
            mine = jnp.where((n_seq * i + rank) // 3 == target, units[i], mine)
        got = lax.ppermute(mine, "seq", [(i, (i + d) % n_seq) for i in range(n_seq)]) if d else mine
        for i in range(3):
            unit = n_seq * i + source
            for at in range(3):
                here = (unit // 3 == rank) & (unit % 3 == at)
                columns[at] = jnp.where(here, got.astype(F32), columns[at])
    g_qkv = jnp.concatenate(columns, axis=1)

    return (rounded, grad_inputs, grad_mods, g_qkv, g_out, g_fc1, g_fc2, g_proj1, g_proj2, g_proj3)


def solution(mesh):
    tok = P(("dp", "seq"), None)
    in_specs = (tok, P("dp", None), P("dp")) + (P(),) * 7 + (tok, tok)
    out_specs = (tok, tok) + (P("dp", "seq"),) * 8
    return jax.shard_map(shards, mesh=mesh, in_specs=in_specs, out_specs=out_specs, check_vma=False)
```

```python
import functools

import jax
import jax.numpy as jnp
from jax import lax
from jax.experimental import pallas as pl
from jax.experimental.pallas import tpu as pltpu
from jax.sharding import PartitionSpec as P

H = 16
HD = 72
HP = 80
LEN = 1024
EPS_NORM = 1e-06
SCALE = HD ** (-0.5)
EXP2_SCALE = SCALE * 1.4426950408889634
GELU_A = 0.7978845608028654
GELU_B = 0.044715
BF = jnp.bfloat16
F32 = jnp.float32
ANY = pl.BlockSpec(memory_space=pl.ANY)
VMEM = pl.BlockSpec(memory_space=pltpu.VMEM)
SMEM = pl.BlockSpec(memory_space=pltpu.SMEM)
ROOM = 60 << 20


def matmul(left, right):
    return jnp.dot(left, right, preferred_element_type=F32)


def times_trans(left, right):
    return lax.dot_general(left, right, (((1,), (1,)), ((), ())), preferred_element_type=F32)


def trans_times(left, right):
    return lax.dot_general(left, right, (((0,), (0,)), ((), ())), preferred_element_type=F32)


def row_mean(v):
    return jnp.mean(v, axis=-1, keepdims=True)


def normalize(v):
    centre = v - row_mean(v)
    inv = lax.rsqrt(row_mean(centre * centre) + EPS_NORM)
    return centre * inv, inv


def norm_back(e, normed, inv):
    return (e - row_mean(e) - normed * row_mean(e * normed)) * inv


def col_sum(v):
    return jnp.sum(v, axis=0, keepdims=True)


def sigmoid(v):
    return 1.0 / (1.0 + jnp.exp(-v))


def shape(dims, kind=BF):
    return jax.ShapeDtypeStruct(dims, kind)


def price(us):
    return pl.CostEstimate(flops=0, transcendentals=0, bytes_accessed=int(us * 3.0e6))


def params(**more):
    return pltpu.CompilerParams(vmem_limit_bytes=ROOM, **more)


def enter_kernel(slot_ref, tokens_ref, mod_ref, mods_ref, out_ref):
    width = tokens_ref.shape[1]
    table = mod_ref[...].astype(F32)
    mine = lax.broadcasted_iota(jnp.int32, table.shape, 0) == slot_ref[0]
    mods = col_sum(jnp.where(mine, table, 0.0))
    mods_ref[...] = jnp.zeros_like(mods_ref)
    for i in range(6):
        mods_ref[i : i + 1, :] = mods[:, i * width : (i + 1) * width]
    normed, _ = normalize(tokens_ref[...].astype(F32))
    first = normed * (1.0 + mods[:, width : 2 * width]) + mods[:, 0:width]
    out_ref[...] = jnp.transpose(first.astype(BF))


def enter(slot, tokens, modulation):
    tok, width = tokens.shape
    return pl.pallas_call(
        enter_kernel,
        out_shape=(shape((8, width), F32), shape((width, tok))),
        in_specs=[SMEM, VMEM, VMEM],
        out_specs=(VMEM, VMEM),
        compiler_params=params(),
        cost_estimate=price(3),
        name="enter",
    )(slot, tokens, modulation)


def attend_forward_kernel(size, heads, tile, diagonal, one_ref, rank_ref, *refs):
    pieces = refs[: 2 * size - 1]
    w_ref, idk_ref, idq_ref, x_ref, o_ref, qkv_ref, lse_ref, k_ref, o_all_ref = refs[2 * size - 1 :]
    tok = pieces[0].shape[1]
    total = x_ref.shape[1]
    x_ref[:, 0:tok] = pieces[0][...]
    for d in range(1, size):
        x_ref[:, d * tok : (d + 1) * tok] = pieces[2 * d - 1][...] + pieces[2 * d][...]

    def project(i, carry):
        at = pl.ds(pl.multiple_of(i * tile, tile), tile)
        qkv_ref[:, at] = matmul(w_ref[...], x_ref[:, at]).astype(BF)
        return carry

    lax.fori_loop(0, total // tile, project, 0)

    def head_step(head, carry):
        q_at = pl.ds(pl.multiple_of(head * HP, HP), HP)
        k_at = pl.ds(pl.multiple_of((heads + head) * HP, HP), HP)
        v_at = pl.ds(pl.multiple_of((2 * heads + head) * HP, HP), HP)
        o_at = pl.ds(pl.multiple_of(head * HD, 8), HD)
        k_ref[...] = jnp.transpose(qkv_ref[k_at, :])

        def block(at, keys, masked):
            s = matmul(k_ref[keys, :], qkv_ref[q_at, at]) * EXP2_SCALE
            if masked:
                s = jnp.where(idk_ref[...] == idq_ref[:, at], s, -1e30)
            top = jnp.max(s, axis=0, keepdims=True)
            e = jnp.exp2(s - top)
            tot = col_sum(e)
            o = matmul(qkv_ref[v_at, keys], e.astype(BF)) * (1.0 / tot)
            o_all_ref[o_at, at] = o[0:HD, :]
            lse_ref[pl.ds(head, 1), at] = top + jnp.log2(tot)

        def full(masked):
            def step(i, inner):
                block(pl.ds(pl.multiple_of(i * tile, tile), tile), pl.ds(0, total), masked)
                return inner

            lax.fori_loop(0, total // tile, step, 0)

        @pl.when(one_ref[0] == 1)
        def _():
            full(False)

        @pl.when(one_ref[0] == 0)
        def _():
            if diagonal:

                def step(i, inner):
                    at = pl.ds(pl.multiple_of(i * tile, tile), tile)
                    block(at, at, False)
                    return inner

                lax.fori_loop(0, total // tile, step, 0)
            else:
                full(True)

        return carry

    lax.fori_loop(0, heads, head_step, 0)
    for d in range(size):
        o_ref[lax.rem(rank_ref[0] + d, size)] = o_all_ref[:, d * tok : (d + 1) * tok].astype(BF)


def attend_forward(one, rank, pieces, w, idk, idq, heads, tile, diagonal):
    width, tok = pieces[0].shape
    size = (len(pieces) + 1) // 2
    total = size * tok
    return pl.pallas_call(
        functools.partial(attend_forward_kernel, size, heads, tile, diagonal),
        out_shape=(
            shape((width, total)),
            shape((size, heads * HD, tok)),
            shape((3 * heads * HP, total)),
            shape((heads, total), F32),
        ),
        in_specs=[SMEM, SMEM] + [VMEM] * (len(pieces) + 3),
        out_specs=(VMEM,) * 4,
        scratch_shapes=[pltpu.VMEM((total, HP), BF), pltpu.VMEM((heads * HD, total), F32)],
        compiler_params=params(),
        cost_estimate=price(23),
        name="attend_forward",
    )(one, rank, *pieces, w, idk, idq)


def attend_backward_kernel(size, heads, tile, diagonal, one_ref, rank_ref, *refs):
    dos_ref, qkv_ref, o_ref, lse_ref, w_ref, idk_ref, idq_ref = refs[:7]
    dqkv_ref, dx_ref, k_ref, v_ref, do_ref, dk_ref, dv_ref, acc_ref, delta_ref = refs[7:]
    tok = dos_ref.shape[2]
    total = qkv_ref.shape[1]
    local = heads * HD
    for d in range(size):
        at = slice(d * tok, (d + 1) * tok)
        owner = lax.rem(rank_ref[0] + d, size)
        do = dos_ref[owner].astype(F32)
        do_ref[0:local, at] = do
        do_ref[local : local + HP - HD, at] = jnp.zeros((HP - HD, tok), F32)
        prod = do * o_ref[owner].astype(F32)
        for head in range(heads):
            delta_ref[head : head + 1, at] = col_sum(prod[head * HD : (head + 1) * HD, :])

    def head_step(head, carry):
        q_at = pl.ds(pl.multiple_of(head * HP, HP), HP)
        k_at = pl.ds(pl.multiple_of((heads + head) * HP, HP), HP)
        v_at = pl.ds(pl.multiple_of((2 * heads + head) * HP, HP), HP)
        o_at = pl.ds(pl.multiple_of(head * HD, 8), HP)
        k_ref[...] = jnp.transpose(qkv_ref[k_at, :])
        v_ref[...] = jnp.transpose(qkv_ref[v_at, :])

        def out_at(part):
            return pl.ds(pl.multiple_of(part * local + head * HD, 8), HD)

        def block(at, keys, masked, fresh):
            q = qkv_ref[q_at, at]
            do = do_ref[o_at, at].astype(BF)
            p = jnp.exp2(matmul(k_ref[keys, :], q) * EXP2_SCALE - lse_ref[pl.ds(head, 1), at])
            if masked:
                p = jnp.where(idk_ref[...] == idq_ref[:, at], p, 0.0)
            ds = (p * (matmul(v_ref[keys, :], do) - delta_ref[pl.ds(head, 1), at])).astype(BF)
            dv = times_trans(do, p.astype(BF))
            dk = times_trans(q, ds)
            if fresh:
                dv_ref[:, keys] = dv
                dk_ref[:, keys] = dk
            else:
                dv_ref[:, keys] += dv
                dk_ref[:, keys] += dk
            dq = matmul(qkv_ref[k_at, keys], ds) * SCALE
            acc_ref[out_at(0), at] = dq[0:HD, :]

        def full(masked):
            dk_ref[...] = jnp.zeros_like(dk_ref)
            dv_ref[...] = jnp.zeros_like(dv_ref)

            def step(i, inner):
                block(pl.ds(pl.multiple_of(i * tile, tile), tile), pl.ds(0, total), masked, False)
                return inner

            lax.fori_loop(0, total // tile, step, 0)

        @pl.when(one_ref[0] == 1)
        def _():
            full(False)

        @pl.when(one_ref[0] == 0)
        def _():
            if diagonal:

                def step(i, inner):
                    at = pl.ds(pl.multiple_of(i * tile, tile), tile)
                    block(at, at, False, True)
                    return inner

                lax.fori_loop(0, total // tile, step, 0)
            else:
                full(True)

        acc_ref[out_at(1), :] = dk_ref[0:HD, :] * SCALE
        acc_ref[out_at(2), :] = dv_ref[0:HD, :]
        return carry

    lax.fori_loop(0, heads, head_step, 0)
    dqkv_ref[...] = acc_ref[...].astype(BF)
    for d in range(size):
        dx_ref[lax.rem(rank_ref[0] + d, size)] = trans_times(dqkv_ref[:, d * tok : (d + 1) * tok], w_ref[...]).astype(BF)


def attend_backward(one, rank, dos, qkv, o, lse, w, idk, idq, heads, tile, diagonal):
    size, local, tok = dos.shape
    total = size * tok
    width = w.shape[1]
    return pl.pallas_call(
        functools.partial(attend_backward_kernel, size, heads, tile, diagonal),
        out_shape=(shape((3 * local, total)), shape((size, tok, width))),
        in_specs=[SMEM, SMEM] + [VMEM] * 7,
        out_specs=(VMEM, VMEM),
        scratch_shapes=[
            pltpu.VMEM((total, HP), BF),
            pltpu.VMEM((total, HP), BF),
            pltpu.VMEM((local + HP - HD, total), F32),
            pltpu.VMEM((HP, total), F32),
            pltpu.VMEM((HP, total), F32),
            pltpu.VMEM((3 * local, total), F32),
            pltpu.VMEM((heads, total), F32),
        ],
        compiler_params=params(),
        cost_estimate=price(23),
        name="attend_backward",
    )(one, rank, dos, qkv, o, lse, w, idk, idq)


STEP = 512


def middle_kernel(*refs):
    (o_refs, tokens_ref, mods_ref, dino_ref, cot_ref, wo_any, w1_any, w2_any, p1_any, p2_any, p3_any) = refs[:11]
    (out_ref, left1_ref, left2_ref, right1_ref, gp_ref, dmlp_ref, dy_ref, normed_ref, inv_ref, attn_ref,
     gate_ref) = refs[11:22]
    (wo_ref, w1_ref, w2_ref, p1_ref, p2_ref, p3_ref, act_ref, w1_sem, sems) = refs[22:]
    size, local, tok = o_refs.shape
    width = size * local
    hidden = w1_any.shape[1]
    wide, narrow = p3_ref.shape
    steps = hidden // STEP
    slots = w1_ref.shape[0]
    a2_ref, a1_ref = left1_ref.at[0:wide, :], left1_ref.at[wide : 2 * wide, :]
    y_ref = left1_ref.at[2 * wide :, :]
    g_ref, b_ref = left2_ref.at[0:hidden, :], left2_ref.at[hidden : hidden + width, :]
    o_ref = left2_ref.at[hidden + width :, :]
    dr2_ref, dr1_ref = right1_ref.at[:, 0:wide], right1_ref.at[:, wide : 2 * wide]
    dz_ref = right1_ref.at[:, 2 * wide :]
    wo_copy = pltpu.make_async_copy(wo_any, wo_ref, sems.at[4])
    wo_copy.start()

    def w1_copy(i):
        at = pl.ds(pl.multiple_of(i * STEP, STEP), STEP)
        slot = lax.rem(i, slots)
        return pltpu.make_async_copy(w1_any.at[:, at], w1_ref.at[slot], w1_sem.at[slot])

    for i in range(slots):
        w1_copy(i).start()
    w2_copy = pltpu.make_async_copy(w2_any, w2_ref, sems.at[0])
    p1_copy = pltpu.make_async_copy(p1_any, p1_ref, sems.at[1])
    p2_copy = pltpu.make_async_copy(p2_any, p2_ref, sems.at[2])
    p3_copy = pltpu.make_async_copy(p3_any, p3_ref, sems.at[3])
    for copy in (w2_copy, p1_copy, p2_copy, p3_copy):
        copy.start()

    gate1, shift2, scale2, gate2 = [mods_ref[i : i + 1, :] for i in (2, 3, 4, 5)]
    for d in range(size):
        o_ref[d * local : (d + 1) * local, :] = o_refs[d]
    wo_copy.wait()
    attn = trans_times(o_ref[...], wo_ref[...])
    attn_ref[...] = attn
    h1 = tokens_ref[...].astype(F32) + gate1 * attn
    normed, inv = normalize(h1)
    normed_ref[...] = normed
    inv_ref[...] = inv
    b = (normed * (1.0 + scale2) + shift2).astype(BF)
    b_ref[...] = jnp.transpose(b)

    def up(i, carry):
        at = pl.ds(pl.multiple_of(i * STEP, STEP), STEP)
        w1_copy(i).wait()
        u = matmul(b, w1_ref[lax.rem(i, slots)])

        @pl.when(i + slots < steps)
        def _():
            w1_copy(i + slots).start()

        sq = u * u
        t = jnp.tanh(u * (GELU_A + (GELU_A * GELU_B) * sq))
        half = 0.5 * (1.0 + t)
        g = (u * half).astype(BF)
        gp_ref[:, at] = (half + u * (1.0 - t * t) * (0.5 * GELU_A + (1.5 * GELU_A * GELU_B) * sq)).astype(BF)
        act_ref[:, at] = g
        g_ref[at, :] = jnp.transpose(g)
        return carry

    lax.fori_loop(0, steps, up, 0)
    w2_copy.wait()
    mlp = matmul(act_ref[...], w2_ref[...])
    y = (h1 + gate2 * mlp).astype(BF)
    out_ref[...] = y
    y_ref[...] = jnp.transpose(y)
    def project(source, w_ref, held, out_t_ref, slope_ref):
        def step(i, carry):
            at = pl.ds(pl.multiple_of(i * STEP, STEP), STEP)
            r = matmul(source, w_ref[:, at])
            sig = sigmoid(r)
            act = (r * sig).astype(BF)
            act_ref[:, pl.ds(pl.multiple_of(held + i * STEP, STEP), STEP)] = act
            out_t_ref[at, :] = jnp.transpose(act)
            slope_ref[:, at] = (sig * (1.0 + r * (1.0 - sig))).astype(BF)
            return carry

        lax.fori_loop(0, wide // STEP, step, 0)
        return act_ref[:, held : held + wide]

    def project_back(source, w_ref, slope_ref):
        def step(i, carry):
            at = pl.ds(pl.multiple_of(i * STEP, STEP), STEP)
            slope_ref[:, at] = (times_trans(source, w_ref[at, :]) * slope_ref[:, at].astype(F32)).astype(BF)
            return carry

        lax.fori_loop(0, wide // STEP, step, 0)
        return slope_ref[...]

    p1_copy.wait()
    a1 = project(y, p1_ref, 0, a1_ref, dr1_ref)
    p2_copy.wait()
    a2 = project(a1, p2_ref, wide, a2_ref, dr2_ref)
    p3_copy.wait()
    z = matmul(a2, p3_ref[...])
    t = dino_ref[...].astype(F32)
    nz = lax.rsqrt(jnp.sum(z * z, axis=-1, keepdims=True) + EPS_NORM)
    nt = lax.rsqrt(jnp.sum(t * t, axis=-1, keepdims=True) + EPS_NORM)
    cosine = jnp.sum(z * t, axis=-1, keepdims=True) * nz * nt
    dz = (-0.5 * (t * (nz * nt) - (cosine * nz * nz) * z)).astype(BF)
    dz_ref[...] = dz
    dr2 = project_back(dz, p3_ref, dr2_ref)
    dr1 = project_back(dr2, p2_ref, dr1_ref)
    dy = cot_ref[...].astype(F32) + times_trans(dr1, p1_ref[...])
    dy_ref[...] = dy
    dmlp_ref[...] = (gate2 * dy).astype(BF)
    gate_ref[...] = col_sum(dy * mlp)


def middle(os, tokens, mods, dino, cot, wo, w1, w2, p1, p2, p3):
    tok, width = tokens.shape
    hidden, wide, narrow = w1.shape[1], p1.shape[1], p3.shape[1]
    return pl.pallas_call(
        middle_kernel,
        out_shape=(
            shape((tok, width)), shape((2 * wide + width, tok)), shape((hidden + 2 * width, tok)),
            shape((tok, 2 * wide + narrow)), shape((tok, hidden)), shape((tok, width)), shape((tok, width), F32),
            shape((tok, width), F32), shape((tok, 1), F32), shape((tok, width), F32), shape((1, width), F32),
        ),
        in_specs=[VMEM] * 5 + [ANY] * 6,
        out_specs=(VMEM,) * 11,
        scratch_shapes=[
            pltpu.VMEM(dims, BF)
            for dims in (wo.shape, (4, width, STEP), w2.shape, p1.shape, p2.shape, p3.shape, (tok, hidden))
        ]
        + [pltpu.SemaphoreType.DMA((4,)), pltpu.SemaphoreType.DMA((5,))],
        compiler_params=params(),
        cost_estimate=price(41),
        name="middle",
    )(os, tokens, mods, dino, cot, wo, w1, w2, p1, p2, p3)


def descend_kernel(size, *refs):
    (dmlp_ref, gp_ref, dy_ref, normed_ref, inv_ref, attn_ref, mods_ref, w2_any, w1_any, wo_any) = refs[:10]
    (right2_ref, dh1_ref, do_ref, sums_ref) = refs[10:14]
    (w2_ref, w1_ref, wo_ref, w2_sem, w1_sem, wo_sem) = refs[14:]
    hidden = w1_ref.shape[1]
    du_ref, dattn_ref = right2_ref.at[:, 0:hidden], right2_ref.at[:, hidden:]
    local = do_ref.shape[1]
    steps = hidden // STEP

    def w2_copy(i):
        at = pl.ds(pl.multiple_of(i * STEP, STEP), STEP)
        return pltpu.make_async_copy(w2_any.at[at, :], w2_ref.at[at, :], w2_sem.at[i])

    for i in range(steps):
        w2_copy(i).start()
    w1_copy = pltpu.make_async_copy(w1_any, w1_ref, w1_sem.at[0])
    w1_copy.start()
    wo_copy = pltpu.make_async_copy(wo_any, wo_ref, wo_sem.at[0])
    wo_copy.start()
    dmlp = dmlp_ref[...]

    def down(i, carry):
        at = pl.ds(pl.multiple_of(i * STEP, STEP), STEP)
        w2_copy(i).wait()
        du_ref[:, at] = (times_trans(dmlp, w2_ref[at, :]) * gp_ref[:, at].astype(F32)).astype(BF)
        return carry

    lax.fori_loop(0, steps, down, 0)
    w1_copy.wait()
    db = times_trans(du_ref[...], w1_ref[...])
    gate1, scale2 = mods_ref[2:3, :], mods_ref[4:5, :]
    normed = normed_ref[...]
    dh1 = dy_ref[...] + norm_back(db * (1.0 + scale2), normed, inv_ref[...])
    dh1_ref[...] = dh1
    dattn = (gate1 * dh1).astype(BF)
    dattn_ref[...] = dattn
    sums_ref[...] = jnp.zeros_like(sums_ref)
    sums_ref[0:1, :] = col_sum(dh1 * attn_ref[...])
    sums_ref[1:2, :] = col_sum(db)
    sums_ref[2:3, :] = col_sum(db * normed)
    wo_copy.wait()
    for d in range(size):
        do_ref[d] = times_trans(wo_ref[d * local : (d + 1) * local, :], dattn).astype(BF)


def descend(size, dmlp, gp, dy, normed, inv, attn, mods, w2, w1, wo):
    tok, width = dmlp.shape
    hidden = w1.shape[1]
    return pl.pallas_call(
        functools.partial(descend_kernel, size),
        out_shape=(
            shape((tok, hidden + width)), shape((tok, width), F32),
            shape((size, width // size, tok)), shape((8, width), F32),
        ),
        in_specs=[VMEM] * 7 + [ANY] * 3,
        out_specs=(VMEM,) * 4,
        scratch_shapes=[pltpu.VMEM(w.shape, BF) for w in (w2, w1, wo)]
        + [
            pltpu.SemaphoreType.DMA((hidden // STEP,)),
            pltpu.SemaphoreType.DMA((1,)),
            pltpu.SemaphoreType.DMA((1,)),
        ],
        compiler_params=params(),
        cost_estimate=price(20),
        name="descend",
    )(dmlp, gp, dy, normed, inv, attn, mods, w2, w1, wo)


def leave_kernel(parts_ref, tokens_ref, dh1_ref, mods_ref, out_ref, sums_ref):
    da = parts_ref[0].astype(F32)
    for i in range(1, parts_ref.shape[0]):
        da = da + parts_ref[i].astype(F32)
    normed, inv = normalize(tokens_ref[...].astype(F32))
    out_ref[...] = (dh1_ref[...] + norm_back(da * (1.0 + mods_ref[1:2, :]), normed, inv)).astype(BF)
    sums_ref[...] = jnp.zeros_like(sums_ref)
    sums_ref[0:1, :] = col_sum(da)
    sums_ref[1:2, :] = col_sum(da * normed)


def leave(parts, tokens, dh1, mods):
    return pl.pallas_call(
        leave_kernel,
        out_shape=(shape(tokens.shape), shape((8, tokens.shape[1]), F32)),
        in_specs=[VMEM] * 4,
        out_specs=(VMEM, VMEM),
        compiler_params=params(),
        cost_estimate=price(4.5),
        name="leave",
    )(parts, tokens, dh1, mods)


def weight_grad_kernel(count, flat, rows, rows_ref, *refs):
    lefts = refs[:count]
    rights = refs[count : count * (1 + len(rows))]
    send_ref, keep_ref, held_ref, sem = refs[count * (1 + len(rows)) :]
    half, height, wide = send_ref.shape
    part = lefts[0].shape[1]
    copies, held_at, held = [], [], 0
    for job, deep in enumerate(rows):
        held_at.append(held)
        for i in range(2 * half):
            at = pl.ds(pl.multiple_of(rows_ref[job * 2 * half + i], 16), deep)
            for j in range(count):
                copies.append(
                    pltpu.make_async_copy(
                        lefts[j].at[at, :],
                        held_ref.at[held : held + deep, j * part : (j + 1) * part],
                        sem.at[len(copies)],
                    )
                )
            held += deep

    @pl.when(pl.program_id(0) == 0)
    def _():
        for copy in copies:
            copy.start()
        for copy in copies:
            copy.wait()

    dot = times_trans if flat else matmul
    for job, deep in enumerate(rows):
        top = sum(rows[:job])
        for out_ref, base in ((send_ref, held_at[job]), (keep_ref, held_at[job] + half * deep)):
            total = None
            for j in range(count):
                term = dot(
                    held_ref[base : base + half * deep, j * part : (j + 1) * part], rights[job * count + j][...]
                )
                total = term if total is None else total + term
            out_ref[:, top : top + deep, :] = total.reshape(half, deep, wide).astype(BF)


def weight_grad(lefts, rights, jobs, wide, step, flat=False):
    count = len(lefts)
    half = jobs[0][0].shape[0] // 2
    part = lefts[0].shape[1]
    rows = tuple(job[1] for job in jobs)
    height = sum(rows)

    def right_spec(base):
        if flat:
            return pl.BlockSpec((step, part), lambda i, b: (i + base, 0))
        return pl.BlockSpec((part, step), lambda i, b: (0, i + base))

    out_spec = pl.BlockSpec((half, height, step), lambda i, b: (0, 0, i))
    return pl.pallas_call(
        functools.partial(weight_grad_kernel, count, flat, rows),
        out_shape=(shape((half, height, wide)), shape((half, height, wide))),
        grid_spec=pltpu.PrefetchScalarGridSpec(
            num_scalar_prefetch=1,
            grid=(wide // step,),
            in_specs=[ANY] * count + [right_spec(job[2]) for job in jobs for _ in range(count)],
            out_specs=(out_spec, out_spec),
            scratch_shapes=[
                pltpu.VMEM((2 * half * height, part * count), BF),
                pltpu.SemaphoreType.DMA((2 * half * count * len(rows),)),
            ],
        ),
        compiler_params=params(dimension_semantics=("arbitrary",)),
        cost_estimate=price(3.0 + 1.2e-6 * count * half * height * wide),
        name="weight_grad",
    )(jnp.concatenate([job[0] for job in jobs]), *lefts, *(list(rights) * len(jobs)))


def flip(x, axis, size, bit):
    return lax.ppermute(x, axis, [(i, i ^ bit) for i in range(size)])


def add(a, b):
    return (a.astype(F32) + b.astype(F32)).astype(BF)


def after(x, *others):
    return lax.optimization_barrier((x,) + others)[0]


def masks_of(bits):
    out = []
    for i in range(2 ** len(bits)):
        mask = 0
        for spot, bit in enumerate(bits):
            if not (i >> (len(bits) - 1 - spot)) & 1:
                mask |= bit
        out.append(mask)
    return out


def halve(send, keep, size, bits, swap):
    for bit in bits[:-1]:
        got = swap(send, bit)
        half = keep.shape[0] // 2
        send = add(keep[:half], got[:half])
        keep = add(keep[half:], got[half:])
    got = swap(send, bits[-1])
    return add(keep, got)[0]


def exchange(blocks):
    return lax.all_to_all(blocks, "seq", split_axis=0, concat_axis=0, tiled=True)


def scatter_columns(share, size):
    rows, cols = share.shape
    blocks = jnp.transpose(share.reshape(rows, size, cols // size), (1, 0, 2))
    return jnp.sum(exchange(blocks).astype(F32), axis=0)


def shards(
    tokens, modulation, image_ids, w_qkv, w_out, w_fc1, w_fc2, w_proj1, w_proj2, w_proj3, dino, cotangent,
):
    n_seq = lax.axis_size("seq")
    n_dp = lax.axis_size("dp")
    rank = lax.axis_index("seq")
    me = lax.axis_index("dp")
    tok_dev, width = tokens.shape
    group_tok = image_ids.shape[0]
    hidden, wide, narrow = w_fc1.shape[1], w_proj2.shape[0], w_proj3.shape[1]
    heads = H // n_seq
    local = heads * HD
    slots = modulation.shape[0]
    dp_bits = [1 << i for i in range(n_dp.bit_length() - 1)]
    rank_arg = rank.reshape(1).astype(jnp.int32)

    my_slot = lax.dynamic_slice_in_dim(image_ids, rank * tok_dev, 1)
    mods, first = enter(my_slot, tokens, modulation)

    right, left = [first], [first]
    for s in range(1, n_seq):
        right.append(lax.ppermute(right[-1], "seq", [(i, i + 1) for i in range(s - 1, n_seq - 1)]))
        left.append(lax.ppermute(left[-1], "seq", [(i, i - 1) for i in range(1, n_seq - s + 1)]))
    pieces = [first]
    for d in range(1, n_seq):
        pieces += [left[d], right[n_seq - d]]

    columns = [lax.dynamic_slice_in_dim(w_qkv, i * width + rank * local, local, 1) for i in range(3)]
    w_rows = jnp.transpose(jnp.concatenate(columns, axis=1))
    w_pad = jnp.pad(w_rows.reshape(3 * heads, HD, width), ((0, 0), (0, HP - HD), (0, 0))).reshape(3 * heads * HP, width)
    ids_rel = lax.dynamic_slice_in_dim(jnp.concatenate([image_ids, image_ids]), rank * tok_dev, group_tok)
    idk, idq = ids_rel[:, None], ids_rel[None, :]
    one = (image_ids[0] == image_ids[group_tok - 1]).astype(jnp.int32).reshape(1)
    tile = group_tok // 4
    diagonal = tok_dev % tile == 0

    first_all, heads_out, qkv, lse = attend_forward(
        one, rank_arg, pieces, w_pad, idk, idq, heads, tile, diagonal
    )
    attended = exchange(heads_out)
    (rounded, left1, left2, right1, gelu_slope, dmlp, dy, normed2, inv2, attn, sum_gate2) = middle(
        attended, tokens, mods, dino, cotangent, w_out, w_fc1, w_fc2, w_proj1, w_proj2, w_proj3
    )

    fast = all(k % (16 * n_dp) == 0 for k in (width, hidden, wide)) and n_dp > 2
    xy, yx = dp_bits[1:], dp_bits[:0:-1]
    swap = lambda x, bit: flip(x, "dp", n_dp, bit)

    def starts(base, deep, bits):
        return base + (me ^ jnp.array(masks_of(bits), jnp.int32)) * (deep // n_dp)

    def job(base, deep, bits, column):
        return (starts(base, deep, bits), deep // n_dp, column)

    if fast:
        lefts1, rights1 = [left1, swap(left1, 1)], [right1, swap(right1, 1)]
        p21 = weight_grad(
            lefts1, rights1, [job(wide, wide, xy, 0), job(2 * wide, width, xy, wide // STEP)], wide, STEP
        )
        rights1[0] = after(rights1[0], p21[0])
        p3 = weight_grad(lefts1, rights1, [job(0, wide, yx, 2 * wide // 256)], narrow, 256)
        lefts2 = [left2, swap(left2, 1)]
        f2 = weight_grad(lefts2, [after(dmlp, p3[0]), swap(dmlp, 1)], [job(0, hidden, yx, 0)], width, 384)
        dmlp = after(dmlp, f2[0])

    right2, dhidden1, dheads, sums2 = descend(
        n_seq, dmlp, gelu_slope, dy, normed2, inv2, attn, mods, w_fc2, w_fc1, w_out
    )
    dheads_in = exchange(dheads)
    if fast:
        rights2 = [right2, swap(right2, 1)]
        f1 = weight_grad(lefts2, rights2, [job(hidden, width, xy, 0)], hidden, 1152)
        rights2[0] = after(rights2[0], f1[0])
        fo = weight_grad(lefts2, rights2, [job(hidden + width, width, yx, hidden // 384)], width, 384)
        dheads_in = after(dheads_in, fo[0])
    dqkv, dfirst_parts = attend_backward(
        one, rank_arg, dheads_in, qkv, heads_out, lse, w_rows, idk, idq, heads, tile, diagonal
    )

    grad_inputs, sums1 = leave(exchange(dfirst_parts), tokens, dhidden1, mods)

    dmods = jnp.concatenate([sums1[0:2], sums2[0:3], sum_gate2], axis=0)
    dmods = exchange(dmods.reshape(n_seq, 6 * width // n_seq))
    slot = jnp.arange(slots, dtype=jnp.int32)[:, None, None]
    whose = image_ids[::tok_dev]
    grad_mods = jnp.sum(jnp.where(slot == whose[None, :, None], dmods[None], 0.0), axis=1)

    if fast:
        rows = width // n_dp
        fq = weight_grad([first_all], [dqkv], [job(0, width, dp_bits, 0)], 3 * local, 3 * local, flat=True)
        g_p21 = scatter_columns(halve(*p21, n_dp, xy, swap), n_seq)
        g_proj2, g_proj1 = g_p21[: wide // n_dp], g_p21[wide // n_dp :]
        g_proj3 = scatter_columns(halve(*p3, n_dp, yx, swap), n_seq)
        g_fc2 = scatter_columns(halve(*f2, n_dp, yx, swap), n_seq)
        g_fc1 = scatter_columns(halve(*f1, n_dp, xy, swap), n_seq)
        g_out = scatter_columns(halve(*fo, n_dp, yx, swap), n_seq)
        g_heads = halve(*fq, n_dp, dp_bits, swap)
    else:

        def reduced(a, b):
            share = lax.psum_scatter(matmul(a, b).astype(BF), "dp", scatter_dimension=0, tiled=True)
            return lax.psum_scatter(share, "seq", scatter_dimension=1, tiled=True).astype(F32)

        g_proj3 = reduced(left1[:wide], right1[:, 2 * wide :])
        g_proj2 = reduced(left1[wide : 2 * wide], right1[:, :wide])
        g_proj1 = reduced(left1[2 * wide :], right1[:, wide : 2 * wide])
        g_fc2 = reduced(left2[:hidden], dmlp)
        g_fc1 = reduced(left2[hidden : hidden + width], right2[:, :hidden])
        g_out = reduced(left2[hidden + width :], right2[:, hidden:])
        g_heads = lax.psum_scatter(
            times_trans(first_all, dqkv).astype(BF), "dp", scatter_dimension=0, tiled=True
        )

    units = [g_heads[:, i * local : (i + 1) * local] for i in range(3)]
    outgoing = []
    for target in range(n_seq):
        mine = jnp.zeros_like(units[0])
        for i in range(3):
            mine = jnp.where((n_seq * i + rank) // 3 == target, units[i], mine)
        outgoing.append(mine)
    incoming = exchange(jnp.stack(outgoing))
    columns = [jnp.zeros(units[0].shape, BF) for _ in range(3)]
    for source in range(n_seq):
        for i in range(3):
            unit = n_seq * i + source
            columns[unit % 3] = jnp.where(unit // 3 == rank, incoming[source], columns[unit % 3])
    g_qkv = jnp.concatenate(columns, axis=1).astype(F32)

    return (rounded, grad_inputs, grad_mods, g_qkv, g_out, g_fc1, g_fc2, g_proj1, g_proj2, g_proj3)


def solution(mesh):
    tok = P(("dp", "seq"), None)
    in_specs = (tok, P("dp", None), P("dp")) + (P(),) * 7 + (tok, tok)
    out_specs = (tok, tok) + (P("dp", "seq"),) * 8
    return jax.shard_map(shards, mesh=mesh, in_specs=in_specs, out_specs=out_specs, check_vma=False)
```

```python
import functools

import jax
import jax.numpy as jnp
from jax import lax
from jax.experimental import pallas as pl
from jax.experimental.pallas import tpu as pltpu
from jax.sharding import PartitionSpec as P

H = 16
HD = 72
HP = 80
LEN = 1024
EPS_NORM = 1e-06
SCALE = HD ** (-0.5)
EXP2_SCALE = SCALE * 1.4426950408889634
GELU_A = 0.7978845608028654
GELU_B = 0.044715
BF = jnp.bfloat16
F32 = jnp.float32
ANY = pl.BlockSpec(memory_space=pl.ANY)
VMEM = pl.BlockSpec(memory_space=pltpu.VMEM)
SMEM = pl.BlockSpec(memory_space=pltpu.SMEM)
ROOM = 60 << 20


def matmul(left, right):
    return jnp.dot(left, right, preferred_element_type=F32)


def times_trans(left, right):
    return lax.dot_general(left, right, (((1,), (1,)), ((), ())), preferred_element_type=F32)


def trans_times(left, right):
    return lax.dot_general(left, right, (((0,), (0,)), ((), ())), preferred_element_type=F32)


def row_mean(v):
    return jnp.mean(v, axis=-1, keepdims=True)


def normalize(v):
    centre = v - row_mean(v)
    inv = lax.rsqrt(row_mean(centre * centre) + EPS_NORM)
    return centre * inv, inv


def norm_back(e, normed, inv):
    return (e - row_mean(e) - normed * row_mean(e * normed)) * inv


def col_sum(v):
    return jnp.sum(v, axis=0, keepdims=True)


def sigmoid(v):
    return 1.0 / (1.0 + jnp.exp(-v))


def shape(dims, kind=BF):
    return jax.ShapeDtypeStruct(dims, kind)


def params(**more):
    return pltpu.CompilerParams(vmem_limit_bytes=ROOM, **more)


def enter_kernel(slot_ref, tokens_ref, mod_ref, mods_ref, out_ref):
    width = tokens_ref.shape[1]
    table = mod_ref[...].astype(F32)
    mine = lax.broadcasted_iota(jnp.int32, table.shape, 0) == slot_ref[0]
    mods = col_sum(jnp.where(mine, table, 0.0))
    mods_ref[...] = jnp.zeros_like(mods_ref)
    for i in range(6):
        mods_ref[i : i + 1, :] = mods[:, i * width : (i + 1) * width]
    normed, _ = normalize(tokens_ref[...].astype(F32))
    first = normed * (1.0 + mods[:, width : 2 * width]) + mods[:, 0:width]
    out_ref[...] = jnp.transpose(first.astype(BF))


def enter(slot, tokens, modulation):
    tok, width = tokens.shape
    return pl.pallas_call(
        enter_kernel,
        out_shape=(shape((8, width), F32), shape((width, tok))),
        in_specs=[SMEM, VMEM, VMEM],
        out_specs=(VMEM, VMEM),
        compiler_params=params(),
        name="enter",
    )(slot, tokens, modulation)


def attend_forward_kernel(size, heads, tile, diagonal, one_ref, rank_ref, *refs):
    pieces = refs[: 2 * size - 1]
    w_ref, idk_ref, idq_ref, x_ref, o_ref, qkv_ref, lse_ref, k_ref, o_all_ref = refs[2 * size - 1 :]
    tok = pieces[0].shape[1]
    total = x_ref.shape[1]
    x_ref[:, 0:tok] = pieces[0][...]
    for d in range(1, size):
        x_ref[:, d * tok : (d + 1) * tok] = pieces[2 * d - 1][...] + pieces[2 * d][...]

    def project(i, carry):
        at = pl.ds(pl.multiple_of(i * tile, tile), tile)
        qkv_ref[:, at] = matmul(w_ref[...], x_ref[:, at]).astype(BF)
        return carry

    lax.fori_loop(0, total // tile, project, 0)

    def head_step(head, carry):
        q_at = pl.ds(pl.multiple_of(head * HP, HP), HP)
        k_at = pl.ds(pl.multiple_of((heads + head) * HP, HP), HP)
        v_at = pl.ds(pl.multiple_of((2 * heads + head) * HP, HP), HP)
        o_at = pl.ds(pl.multiple_of(head * HD, 8), HD)
        k_ref[...] = jnp.transpose(qkv_ref[k_at, :])

        def block(at, keys, masked):
            s = matmul(k_ref[keys, :], qkv_ref[q_at, at]) * EXP2_SCALE
            if masked:
                s = jnp.where(idk_ref[...] == idq_ref[:, at], s, -1e30)
            top = jnp.max(s, axis=0, keepdims=True)
            e = jnp.exp2(s - top)
            tot = col_sum(e)
            o = matmul(qkv_ref[v_at, keys], e.astype(BF)) * (1.0 / tot)
            o_all_ref[o_at, at] = o[0:HD, :]
            lse_ref[pl.ds(head, 1), at] = top + jnp.log2(tot)

        def full(masked):
            def step(i, inner):
                block(pl.ds(pl.multiple_of(i * tile, tile), tile), pl.ds(0, total), masked)
                return inner

            lax.fori_loop(0, total // tile, step, 0)

        @pl.when(one_ref[0] == 1)
        def _():
            full(False)

        @pl.when(one_ref[0] == 0)
        def _():
            if diagonal:

                def step(i, inner):
                    at = pl.ds(pl.multiple_of(i * tile, tile), tile)
                    block(at, at, False)
                    return inner

                lax.fori_loop(0, total // tile, step, 0)
            else:
                full(True)

        return carry

    lax.fori_loop(0, heads, head_step, 0)
    for d in range(size):
        o_ref[lax.rem(rank_ref[0] + d, size)] = o_all_ref[:, d * tok : (d + 1) * tok].astype(BF)


def attend_forward(one, rank, pieces, w, idk, idq, heads, tile, diagonal):
    width, tok = pieces[0].shape
    size = (len(pieces) + 1) // 2
    total = size * tok
    return pl.pallas_call(
        functools.partial(attend_forward_kernel, size, heads, tile, diagonal),
        out_shape=(
            shape((width, total)),
            shape((size, heads * HD, tok)),
            shape((3 * heads * HP, total)),
            shape((heads, total), F32),
        ),
        in_specs=[SMEM, SMEM] + [VMEM] * (len(pieces) + 3),
        out_specs=(VMEM,) * 4,
        scratch_shapes=[pltpu.VMEM((total, HP), BF), pltpu.VMEM((heads * HD, total), F32)],
        compiler_params=params(),
        name="attend_forward",
    )(one, rank, *pieces, w, idk, idq)


def attend_backward_kernel(size, heads, tile, diagonal, one_ref, rank_ref, *refs):
    dos_ref, qkv_ref, o_ref, lse_ref, w_ref, idk_ref, idq_ref = refs[:7]
    dqkv_ref, dx_ref, k_ref, v_ref, do_ref, dk_ref, dv_ref, acc_ref, delta_ref = refs[7:]
    tok = dos_ref.shape[2]
    total = qkv_ref.shape[1]
    local = heads * HD
    for d in range(size):
        at = slice(d * tok, (d + 1) * tok)
        owner = lax.rem(rank_ref[0] + d, size)
        do = dos_ref[owner].astype(F32)
        do_ref[0:local, at] = do
        do_ref[local : local + HP - HD, at] = jnp.zeros((HP - HD, tok), F32)
        prod = do * o_ref[owner].astype(F32)
        for head in range(heads):
            delta_ref[head : head + 1, at] = col_sum(prod[head * HD : (head + 1) * HD, :])

    def head_step(head, carry):
        q_at = pl.ds(pl.multiple_of(head * HP, HP), HP)
        k_at = pl.ds(pl.multiple_of((heads + head) * HP, HP), HP)
        v_at = pl.ds(pl.multiple_of((2 * heads + head) * HP, HP), HP)
        o_at = pl.ds(pl.multiple_of(head * HD, 8), HP)
        k_ref[...] = jnp.transpose(qkv_ref[k_at, :])
        v_ref[...] = jnp.transpose(qkv_ref[v_at, :])

        def out_at(part):
            return pl.ds(pl.multiple_of(part * local + head * HD, 8), HD)

        def block(at, keys, masked, fresh):
            q = qkv_ref[q_at, at]
            do = do_ref[o_at, at].astype(BF)
            p = jnp.exp2(matmul(k_ref[keys, :], q) * EXP2_SCALE - lse_ref[pl.ds(head, 1), at])
            if masked:
                p = jnp.where(idk_ref[...] == idq_ref[:, at], p, 0.0)
            ds = (p * (matmul(v_ref[keys, :], do) - delta_ref[pl.ds(head, 1), at])).astype(BF)
            dv = times_trans(do, p.astype(BF))
            dk = times_trans(q, ds)
            if fresh:
                dv_ref[:, keys] = dv
                dk_ref[:, keys] = dk
            else:
                dv_ref[:, keys] += dv
                dk_ref[:, keys] += dk
            dq = matmul(qkv_ref[k_at, keys], ds) * SCALE
            acc_ref[out_at(0), at] = dq[0:HD, :]

        def full(masked):
            dk_ref[...] = jnp.zeros_like(dk_ref)
            dv_ref[...] = jnp.zeros_like(dv_ref)

            def step(i, inner):
                block(pl.ds(pl.multiple_of(i * tile, tile), tile), pl.ds(0, total), masked, False)
                return inner

            lax.fori_loop(0, total // tile, step, 0)

        @pl.when(one_ref[0] == 1)
        def _():
            full(False)

        @pl.when(one_ref[0] == 0)
        def _():
            if diagonal:

                def step(i, inner):
                    at = pl.ds(pl.multiple_of(i * tile, tile), tile)
                    block(at, at, False, True)
                    return inner

                lax.fori_loop(0, total // tile, step, 0)
            else:
                full(True)

        acc_ref[out_at(1), :] = dk_ref[0:HD, :] * SCALE
        acc_ref[out_at(2), :] = dv_ref[0:HD, :]
        return carry

    lax.fori_loop(0, heads, head_step, 0)
    dqkv_ref[...] = acc_ref[...].astype(BF)
    for d in range(size):
        dx_ref[lax.rem(rank_ref[0] + d, size)] = trans_times(dqkv_ref[:, d * tok : (d + 1) * tok], w_ref[...]).astype(BF)


def attend_backward(one, rank, dos, qkv, o, lse, w, idk, idq, heads, tile, diagonal):
    size, local, tok = dos.shape
    total = size * tok
    width = w.shape[1]
    return pl.pallas_call(
        functools.partial(attend_backward_kernel, size, heads, tile, diagonal),
        out_shape=(shape((3 * local, total)), shape((size, tok, width))),
        in_specs=[SMEM, SMEM] + [VMEM] * 7,
        out_specs=(VMEM, VMEM),
        scratch_shapes=[
            pltpu.VMEM((total, HP), BF),
            pltpu.VMEM((total, HP), BF),
            pltpu.VMEM((local + HP - HD, total), F32),
            pltpu.VMEM((HP, total), F32),
            pltpu.VMEM((HP, total), F32),
            pltpu.VMEM((3 * local, total), F32),
            pltpu.VMEM((heads, total), F32),
        ],
        compiler_params=params(),
        name="attend_backward",
    )(one, rank, dos, qkv, o, lse, w, idk, idq)


STEP = 512


def middle_kernel(*refs):
    (o_refs, tokens_ref, mods_ref, dino_ref, cot_ref, wo_any, w1_any, w2_any, p1_any, p2_any, p3_any) = refs[:11]
    (out_ref, left1_ref, left2_ref, right1_ref, gp_ref, dmlp_ref, dy_ref, normed_ref, inv_ref, attn_ref,
     gate_ref) = refs[11:22]
    (wo_ref, w1_ref, w2_ref, p1_ref, p2_ref, p3_ref, act_ref, w1_sem, sems) = refs[22:]
    size, local, tok = o_refs.shape
    width = size * local
    hidden = w1_any.shape[1]
    wide, narrow = p3_ref.shape
    steps = hidden // STEP
    slots = w1_ref.shape[0]
    a2_ref, a1_ref = left1_ref.at[0:wide, :], left1_ref.at[wide : 2 * wide, :]
    y_ref = left1_ref.at[2 * wide :, :]
    g_ref, b_ref = left2_ref.at[0:hidden, :], left2_ref.at[hidden : hidden + width, :]
    o_ref = left2_ref.at[hidden + width :, :]
    dr2_ref, dr1_ref = right1_ref.at[:, 0:wide], right1_ref.at[:, wide : 2 * wide]
    dz_ref = right1_ref.at[:, 2 * wide :]
    wo_copy = pltpu.make_async_copy(wo_any, wo_ref, sems.at[4])
    wo_copy.start()

    def w1_copy(i):
        at = pl.ds(pl.multiple_of(i * STEP, STEP), STEP)
        slot = lax.rem(i, slots)
        return pltpu.make_async_copy(w1_any.at[:, at], w1_ref.at[slot], w1_sem.at[slot])

    for i in range(slots):
        w1_copy(i).start()
    w2_copy = pltpu.make_async_copy(w2_any, w2_ref, sems.at[0])
    p1_copy = pltpu.make_async_copy(p1_any, p1_ref, sems.at[1])
    p2_copy = pltpu.make_async_copy(p2_any, p2_ref, sems.at[2])
    p3_copy = pltpu.make_async_copy(p3_any, p3_ref, sems.at[3])
    for copy in (w2_copy, p1_copy, p2_copy, p3_copy):
        copy.start()

    gate1, shift2, scale2, gate2 = [mods_ref[i : i + 1, :] for i in (2, 3, 4, 5)]
    for d in range(size):
        o_ref[d * local : (d + 1) * local, :] = o_refs[d]
    wo_copy.wait()
    attn = trans_times(o_ref[...], wo_ref[...])
    attn_ref[...] = attn
    h1 = tokens_ref[...].astype(F32) + gate1 * attn
    normed, inv = normalize(h1)
    normed_ref[...] = normed
    inv_ref[...] = inv
    b = (normed * (1.0 + scale2) + shift2).astype(BF)
    b_ref[...] = jnp.transpose(b)

    def up(i, carry):
        at = pl.ds(pl.multiple_of(i * STEP, STEP), STEP)
        w1_copy(i).wait()
        u = matmul(b, w1_ref[lax.rem(i, slots)])

        @pl.when(i + slots < steps)
        def _():
            w1_copy(i + slots).start()

        sq = u * u
        t = jnp.tanh(u * (GELU_A + (GELU_A * GELU_B) * sq))
        half = 0.5 * (1.0 + t)
        g = (u * half).astype(BF)
        gp_ref[:, at] = (half + u * (1.0 - t * t) * (0.5 * GELU_A + (1.5 * GELU_A * GELU_B) * sq)).astype(BF)
        act_ref[:, at] = g
        g_ref[at, :] = jnp.transpose(g)
        return carry

    lax.fori_loop(0, steps, up, 0)
    w2_copy.wait()
    mlp = matmul(act_ref[...], w2_ref[...])
    y = (h1 + gate2 * mlp).astype(BF)
    out_ref[...] = y
    y_ref[...] = jnp.transpose(y)
    def project(source, w_ref, held, out_t_ref, slope_ref):
        def step(i, carry):
            at = pl.ds(pl.multiple_of(i * STEP, STEP), STEP)
            r = matmul(source, w_ref[:, at])
            sig = sigmoid(r)
            act = (r * sig).astype(BF)
            act_ref[:, pl.ds(pl.multiple_of(held + i * STEP, STEP), STEP)] = act
            out_t_ref[at, :] = jnp.transpose(act)
            slope_ref[:, at] = (sig * (1.0 + r * (1.0 - sig))).astype(BF)
            return carry

        lax.fori_loop(0, wide // STEP, step, 0)
        return act_ref[:, held : held + wide]

    def project_back(source, w_ref, slope_ref):
        def step(i, carry):
            at = pl.ds(pl.multiple_of(i * STEP, STEP), STEP)
            slope_ref[:, at] = (times_trans(source, w_ref[at, :]) * slope_ref[:, at].astype(F32)).astype(BF)
            return carry

        lax.fori_loop(0, wide // STEP, step, 0)
        return slope_ref[...]

    p1_copy.wait()
    a1 = project(y, p1_ref, 0, a1_ref, dr1_ref)
    p2_copy.wait()
    a2 = project(a1, p2_ref, wide, a2_ref, dr2_ref)
    p3_copy.wait()
    z = matmul(a2, p3_ref[...])
    t = dino_ref[...].astype(F32)
    nz = lax.rsqrt(jnp.sum(z * z, axis=-1, keepdims=True) + EPS_NORM)
    nt = lax.rsqrt(jnp.sum(t * t, axis=-1, keepdims=True) + EPS_NORM)
    cosine = jnp.sum(z * t, axis=-1, keepdims=True) * nz * nt
    dz = (-0.5 * (t * (nz * nt) - (cosine * nz * nz) * z)).astype(BF)
    dz_ref[...] = dz
    dr2 = project_back(dz, p3_ref, dr2_ref)
    dr1 = project_back(dr2, p2_ref, dr1_ref)
    dy = cot_ref[...].astype(F32) + times_trans(dr1, p1_ref[...])
    dy_ref[...] = dy
    dmlp_ref[...] = (gate2 * dy).astype(BF)
    gate_ref[...] = col_sum(dy * mlp)


def middle(os, tokens, mods, dino, cot, wo, w1, w2, p1, p2, p3):
    tok, width = tokens.shape
    hidden, wide, narrow = w1.shape[1], p1.shape[1], p3.shape[1]
    return pl.pallas_call(
        middle_kernel,
        out_shape=(
            shape((tok, width)), shape((2 * wide + width, tok)), shape((hidden + 2 * width, tok)),
            shape((tok, 2 * wide + narrow)), shape((tok, hidden)), shape((tok, width)), shape((tok, width), F32),
            shape((tok, width), F32), shape((tok, 1), F32), shape((tok, width), F32), shape((1, width), F32),
        ),
        in_specs=[VMEM] * 5 + [ANY] * 6,
        out_specs=(VMEM,) * 11,
        scratch_shapes=[
            pltpu.VMEM(dims, BF)
            for dims in (wo.shape, (4, width, STEP), w2.shape, p1.shape, p2.shape, p3.shape, (tok, hidden))
        ]
        + [pltpu.SemaphoreType.DMA((4,)), pltpu.SemaphoreType.DMA((5,))],
        compiler_params=params(),
        name="middle",
    )(os, tokens, mods, dino, cot, wo, w1, w2, p1, p2, p3)


def descend_kernel(size, *refs):
    (dmlp_ref, gp_ref, dy_ref, normed_ref, inv_ref, attn_ref, mods_ref, w2_any, w1_any, wo_any) = refs[:10]
    (right2_ref, dh1_ref, do_ref, sums_ref) = refs[10:14]
    (w2_ref, w1_ref, wo_ref, w2_sem, w1_sem, wo_sem) = refs[14:]
    hidden = w1_ref.shape[1]
    du_ref, dattn_ref = right2_ref.at[:, 0:hidden], right2_ref.at[:, hidden:]
    local = do_ref.shape[1]
    steps = hidden // STEP

    def w2_copy(i):
        at = pl.ds(pl.multiple_of(i * STEP, STEP), STEP)
        return pltpu.make_async_copy(w2_any.at[at, :], w2_ref.at[at, :], w2_sem.at[i])

    for i in range(steps):
        w2_copy(i).start()
    w1_copy = pltpu.make_async_copy(w1_any, w1_ref, w1_sem.at[0])
    w1_copy.start()
    wo_copy = pltpu.make_async_copy(wo_any, wo_ref, wo_sem.at[0])
    wo_copy.start()
    dmlp = dmlp_ref[...]

    def down(i, carry):
        at = pl.ds(pl.multiple_of(i * STEP, STEP), STEP)
        w2_copy(i).wait()
        du_ref[:, at] = (times_trans(dmlp, w2_ref[at, :]) * gp_ref[:, at].astype(F32)).astype(BF)
        return carry

    lax.fori_loop(0, steps, down, 0)
    w1_copy.wait()
    db = times_trans(du_ref[...], w1_ref[...])
    gate1, scale2 = mods_ref[2:3, :], mods_ref[4:5, :]
    normed = normed_ref[...]
    dh1 = dy_ref[...] + norm_back(db * (1.0 + scale2), normed, inv_ref[...])
    dh1_ref[...] = dh1
    dattn = (gate1 * dh1).astype(BF)
    dattn_ref[...] = dattn
    sums_ref[...] = jnp.zeros_like(sums_ref)
    sums_ref[0:1, :] = col_sum(dh1 * attn_ref[...])
    sums_ref[1:2, :] = col_sum(db)
    sums_ref[2:3, :] = col_sum(db * normed)
    wo_copy.wait()
    for d in range(size):
        do_ref[d] = times_trans(wo_ref[d * local : (d + 1) * local, :], dattn).astype(BF)


def descend(size, dmlp, gp, dy, normed, inv, attn, mods, w2, w1, wo):
    tok, width = dmlp.shape
    hidden = w1.shape[1]
    return pl.pallas_call(
        functools.partial(descend_kernel, size),
        out_shape=(
            shape((tok, hidden + width)), shape((tok, width), F32),
            shape((size, width // size, tok)), shape((8, width), F32),
        ),
        in_specs=[VMEM] * 7 + [ANY] * 3,
        out_specs=(VMEM,) * 4,
        scratch_shapes=[pltpu.VMEM(w.shape, BF) for w in (w2, w1, wo)]
        + [
            pltpu.SemaphoreType.DMA((hidden // STEP,)),
            pltpu.SemaphoreType.DMA((1,)),
            pltpu.SemaphoreType.DMA((1,)),
        ],
        compiler_params=params(),
        name="descend",
    )(dmlp, gp, dy, normed, inv, attn, mods, w2, w1, wo)


def leave_kernel(parts_ref, tokens_ref, dh1_ref, mods_ref, out_ref, sums_ref):
    da = parts_ref[0].astype(F32)
    for i in range(1, parts_ref.shape[0]):
        da = da + parts_ref[i].astype(F32)
    normed, inv = normalize(tokens_ref[...].astype(F32))
    out_ref[...] = (dh1_ref[...] + norm_back(da * (1.0 + mods_ref[1:2, :]), normed, inv)).astype(BF)
    sums_ref[...] = jnp.zeros_like(sums_ref)
    sums_ref[0:1, :] = col_sum(da)
    sums_ref[1:2, :] = col_sum(da * normed)


def leave(parts, tokens, dh1, mods):
    return pl.pallas_call(
        leave_kernel,
        out_shape=(shape(tokens.shape), shape((8, tokens.shape[1]), F32)),
        in_specs=[VMEM] * 4,
        out_specs=(VMEM, VMEM),
        compiler_params=params(),
        name="leave",
    )(parts, tokens, dh1, mods)


def weight_grad_kernel(count, flat, rows, packs, rows_ref, *refs):
    lefts = refs[:count]
    rights = refs[count : count * (1 + len(rows))]
    outs = refs[count * (1 + len(rows)) : -2]
    held_ref, sem = refs[-2:]
    blocks = sum(packs)
    part = lefts[0].shape[1]
    copies, held_at, held = [], [], 0
    for job, deep in enumerate(rows):
        held_at.append(held)
        for i in range(blocks):
            at = pl.ds(pl.multiple_of(rows_ref[job * blocks + i], 16), deep)
            for j in range(count):
                copies.append(
                    pltpu.make_async_copy(
                        lefts[j].at[at, :],
                        held_ref.at[held : held + deep, j * part : (j + 1) * part],
                        sem.at[len(copies)],
                    )
                )
            held += deep

    @pl.when(pl.program_id(0) == 0)
    def _():
        for copy in copies:
            copy.start()
        for copy in copies:
            copy.wait()

    dot = times_trans if flat else matmul
    for job, deep in enumerate(rows):
        base = held_at[job]
        for spot, pack in enumerate(packs):
            out_ref = outs[job * len(packs) + spot]
            total = None
            for j in range(count):
                term = dot(
                    held_ref[base : base + pack * deep, j * part : (j + 1) * part], rights[job * count + j][...]
                )
                total = term if total is None else total + term
            out_ref[...] = total.reshape(out_ref.shape).astype(BF)
            base += pack * deep


def weight_grad(lefts, rights, jobs, packs, wide, step, flat=False):
    count = len(lefts)
    part = lefts[0].shape[1]
    rows = tuple(job[1] for job in jobs)

    def right_spec(base):
        if flat:
            return pl.BlockSpec((step, part), lambda i, b: (i + base, 0))
        return pl.BlockSpec((part, step), lambda i, b: (0, i + base))

    outs = pl.pallas_call(
        functools.partial(weight_grad_kernel, count, flat, rows, packs),
        out_shape=tuple(shape((pack, deep, wide)) for deep in rows for pack in packs),
        grid_spec=pltpu.PrefetchScalarGridSpec(
            num_scalar_prefetch=1,
            grid=(wide // step,),
            in_specs=[ANY] * count + [right_spec(job[2]) for job in jobs for _ in range(count)],
            out_specs=tuple(
                pl.BlockSpec((pack, deep, step), lambda i, b: (0, 0, i)) for deep in rows for pack in packs
            ),
            scratch_shapes=[
                pltpu.VMEM((sum(packs) * sum(rows), part * count), BF),
                pltpu.SemaphoreType.DMA((sum(packs) * count * len(rows),)),
            ],
        ),
        compiler_params=params(dimension_semantics=("arbitrary",)),
        name="weight_grad",
    )(jnp.concatenate([job[0] for job in jobs]), *lefts, *(list(rights) * len(jobs)))
    return [outs[i * len(packs) : (i + 1) * len(packs)] for i in range(len(jobs))]


def split_kernel(rank_ref, keep_ref, got_ref, near_ref, far_ref, own_ref):
    rows, cols = keep_ref.shape
    size = near_ref.shape[0] * 2
    block = cols // size
    total = (keep_ref[...].astype(F32) + got_ref[...].astype(F32)).astype(BF)
    for j in range(size):
        piece = total[:, j * block : (j + 1) * block]
        mask = j ^ rank_ref[0]

        @pl.when(mask == 3)
        def _():
            near_ref[0] = piece

        @pl.when(mask == 1)
        def _():
            near_ref[1] = piece

        @pl.when(mask == 2)
        def _():
            far_ref[...] = piece

        @pl.when(mask == 0)
        def _():
            own_ref[...] = piece


def split(rank, keep, got):
    rows, cols = keep.shape
    return pl.pallas_call(
        split_kernel,
        out_shape=(shape((2, rows, cols // 4)), shape((rows, cols // 4)), shape((rows, cols // 4))),
        in_specs=[SMEM, VMEM, VMEM],
        out_specs=(VMEM,) * 3,
        compiler_params=params(),
        name="split",
    )(rank, keep, got)


def flip(x, axis, size, bit):
    return lax.ppermute(x, axis, [(i, i ^ bit) for i in range(size)])


def add(a, b):
    return (a.astype(F32) + b.astype(F32)).astype(BF)


def after(x, *others):
    return lax.optimization_barrier((x,) + others)[0]


def masks_of(bits):
    out = []
    for i in range(2 ** len(bits)):
        mask = 0
        for spot, bit in enumerate(bits):
            if not (i >> (len(bits) - 1 - spot)) & 1:
                mask |= bit
        out.append(mask)
    return out


def together(*values):
    leaves, tree = jax.tree.flatten(values)
    return jax.tree.unflatten(tree, lax.optimization_barrier(tuple(leaves)))


def exchange(blocks):
    return lax.all_to_all(blocks, "seq", split_axis=0, concat_axis=0, tiled=True)


def shards(
    tokens, modulation, image_ids, w_qkv, w_out, w_fc1, w_fc2, w_proj1, w_proj2, w_proj3, dino, cotangent,
):
    n_seq = lax.axis_size("seq")
    n_dp = lax.axis_size("dp")
    rank = lax.axis_index("seq")
    me = lax.axis_index("dp")
    tok_dev, width = tokens.shape
    group_tok = image_ids.shape[0]
    hidden, wide, narrow = w_fc1.shape[1], w_proj2.shape[0], w_proj3.shape[1]
    heads = H // n_seq
    local = heads * HD
    slots = modulation.shape[0]
    dp_bits = [1 << i for i in range(n_dp.bit_length() - 1)]
    rank_arg = rank.reshape(1).astype(jnp.int32)

    my_slot = lax.dynamic_slice_in_dim(image_ids, rank * tok_dev, 1)
    mods, first = enter(my_slot, tokens, modulation)

    right, left = [first], [first]
    for s in range(1, n_seq):
        right.append(lax.ppermute(right[-1], "seq", [(i, i + 1) for i in range(s - 1, n_seq - 1)]))
        left.append(lax.ppermute(left[-1], "seq", [(i, i - 1) for i in range(1, n_seq - s + 1)]))
    pieces = [first]
    for d in range(1, n_seq):
        pieces += [left[d], right[n_seq - d]]

    columns = [lax.dynamic_slice_in_dim(w_qkv, i * width + rank * local, local, 1) for i in range(3)]
    w_rows = jnp.transpose(jnp.concatenate(columns, axis=1))
    w_pad = jnp.pad(w_rows.reshape(3 * heads, HD, width), ((0, 0), (0, HP - HD), (0, 0))).reshape(3 * heads * HP, width)
    ids_rel = lax.dynamic_slice_in_dim(jnp.concatenate([image_ids, image_ids]), rank * tok_dev, group_tok)
    idk, idq = ids_rel[:, None], ids_rel[None, :]
    one = (image_ids[0] == image_ids[group_tok - 1]).astype(jnp.int32).reshape(1)
    tile = group_tok // 4
    diagonal = tok_dev % tile == 0

    first_all, heads_out, qkv, lse = attend_forward(
        one, rank_arg, pieces, w_pad, idk, idq, heads, tile, diagonal
    )
    attended = exchange(heads_out)
    (rounded, left1, left2, right1, gelu_slope, dmlp, dy, normed2, inv2, attn, sum_gate2) = middle(
        attended, tokens, mods, dino, cotangent, w_out, w_fc1, w_fc2, w_proj1, w_proj2, w_proj3
    )

    fast = all(k % (16 * n_dp) == 0 for k in (width, hidden, wide)) and n_dp == 8 and n_seq == 4

    def down(dmlp):
        return descend(n_seq, dmlp, gelu_slope, dy, normed2, inv2, attn, mods, w_fc2, w_fc1, w_out)

    def back(dos):
        return attend_backward(
            one, rank_arg, dos, qkv, heads_out, lse, w_rows, idk, idq, heads, tile, diagonal
        )

    if fast:
        swap = lambda x, bit: flip(x, "dp", n_dp, bit)
        core, x, y = dp_bits
        near = lambda v: flip(v, "seq", n_seq, 1)
        far = lambda v: flip(v, "seq", n_seq, 2)

        def job(base, deep, bits, column):
            starts = base + (me ^ jnp.array(masks_of(bits), jnp.int32)) * (deep // n_dp)
            return (starts, deep // n_dp, column)

        quarter = (1, 1, 1, 1)
        lefts1, rights1 = [left1, swap(left1, core)], [right1, swap(right1, core)]
        (p2, p1) = weight_grad(
            lefts1, rights1, [job(wide, wide, (x, y), 0), job(2 * wide, width, (y, x), wide // STEP)],
            quarter, wide, STEP,
        )
        left2_other, dmlp_other = swap(left2, core), swap(dmlp, core)
        lefts1, rights1, p2, p1, left2_other, dmlp_other = together(
            lefts1, rights1, p2, p1, left2_other, dmlp_other
        )

        p2a, p1a, p1b = swap(p2[0], x), swap(p1[0], y), swap(p1[1], y)
        lefts2 = [left2, left2_other]
        (f2,) = weight_grad(lefts2, [dmlp, dmlp_other], [job(0, hidden, (y, x), 0)], quarter, width, 384)
        rights1 = together(rights1, f2)[0]
        (p3,) = weight_grad(lefts1, rights1, [job(0, wide, (x, y), 2 * wide // 256)], quarter, narrow, 256)
        p2a, p1a, p1b, f2, p3, p2, p1, dmlp = together(p2a, p1a, p1b, f2, p3, p2, p1, dmlp)

        p2b, f2a = swap(p2[1], x), swap(f2[0], y)
        right2, dhidden1, dheads, sums2 = down(dmlp)
        p1s = add(p1[2], p1a)
        p2b, f2a, right2, dhidden1, dheads, sums2, p1s, f2, p3, p2a = together(
            p2b, f2a, right2, dhidden1, dheads, sums2, p1s, f2, p3, p2a
        )

        dheads_in = exchange(dheads)
        rights2 = [right2, swap(right2, core)]
        p1c, p3a, p3b, f2b = swap(p1s, x), swap(p3[0], x), swap(p3[1], x), swap(f2[1], y)
        p2s, f2s = add(p2[2], p2a), add(f2[2], f2a)
        (f1,) = weight_grad(lefts2, rights2, [job(hidden, width, (x, y), 0)], quarter, hidden, 1152)
        rights2 = together(rights2, f1)[0]
        (fo,) = weight_grad(
            lefts2, rights2, [job(hidden + width, width, (y, x), hidden // 384)], quarter, width, 384
        )
        dheads_in, p1c, p3a, p3b, f2b, p2s, f2s, f1, fo, p3 = together(
            dheads_in, p1c, p3a, p3b, f2b, p2s, f2s, f1, fo, p3
        )

        f2c, p2c = swap(f2s, x), swap(p2s, y)
        dqkv, dfirst_parts = back(dheads_in)
        p1n, p1f, p1o = split(rank_arg, add(p1[3], p1b)[0], p1c[0])
        p3s = add(p3[2], p3a)
        f2c, p2c, dqkv, dfirst_parts, p1n, p1f, p1o, p3s, f1, fo, p3b = together(
            f2c, p2c, dqkv, dfirst_parts, p1n, p1f, p1o, p3s, f1, fo, p3b
        )

        dfirst_in = exchange(dfirst_parts)
        f1a, foa, fob, p3c, p1z = swap(f1[0], x), swap(fo[0], y), swap(fo[1], y), swap(p3s, y), near(p1n)
        (fq,) = weight_grad(
            [first_all], [dqkv], [job(0, width, (core, y, x), 0)], (4, 2, 2), 3 * local, 3 * local, flat=True
        )
        fqa = swap(fq[0], core)
        f2n, f2f, f2o = split(rank_arg, add(f2[3], f2b)[0], f2c[0])
        p2n, p2f, p2o = split(rank_arg, add(p2[3], p2b)[0], p2c[0])
        f1a, foa, fob, p3c, p1z, fq, fqa, f2n, p2n, f1, fo = together(
            f1a, foa, fob, p3c, p1z, fq, fqa, f2n, p2n, f1, fo
        )

        fqs, fqk = add(fq[1], fqa[:2]), add(fq[2], fqa[2:])
        f1b, f1s, p2z = swap(f1[1], x), add(f1[2], f1a), near(p2n)
        fqb = swap(fqs, y)
        fos = add(fo[2], foa)
        p1y = far(add(p1f, p1z[0]))
        p1o = add(p1o, p1z[1])
        p3n, p3f, p3o = split(rank_arg, add(p3[3], p3b)[0], p3c[0])
        f1b, f1s, p2z, fqb, fos, p1y, p1o, p3n, f2n, fqk, f1 = together(
            f1b, f1s, p2z, fqb, fos, p1y, p1o, p3n, f2n, fqk, f1
        )

        f1c, foc, f2z = swap(f1s, y), swap(fos, x), near(f2n)
        fqs, fqk = add(fqk[0], fqb[0]), add(fqk[1], fqb[1])
        fqc = swap(fqs, x)
        p2y = far(add(p2f, p2z[0]))
        p2o = add(p2o, p2z[1])
        g_proj1 = p1o.astype(F32) + p1y.astype(F32)
        grad_inputs, sums1 = leave(dfirst_in, tokens, dhidden1, mods)
        f1c, foc, f2z, fqk, fqc, p2y, p2o, p3n, sums1 = together(f1c, foc, f2z, fqk, fqc, p2y, p2o, p3n, sums1)

        f1n, f1f, f1o = split(rank_arg, add(f1[3], f1b)[0], f1c[0])
        fon, fof, foo = split(rank_arg, add(fo[3], fob)[0], foc[0])
        f1z, f2y, p3z, foz = near(f1n), far(add(f2f, f2z[0])), near(p3n), near(fon)
        f2o = add(f2o, f2z[1])
        g_heads = add(fqk, fqc)
        g_proj2 = p2o.astype(F32) + p2y.astype(F32)
        f1z, f2y, p3z, foz, f1f, fof, f2o, f1o, foo = together(f1z, f2y, p3z, foz, f1f, fof, f2o, f1o, foo)

        f1y, p3y, foy = far(add(f1f, f1z[0])), far(add(p3f, p3z[0])), far(add(fof, foz[0]))
        g_fc2 = f2o.astype(F32) + f2y.astype(F32)
        last = lambda own, z, far_got: own.astype(F32) + z[1].astype(F32) + far_got.astype(F32)
        g_fc1, g_proj3, g_out = last(f1o, f1z, f1y), last(p3o, p3z, p3y), last(foo, foz, foy)
    else:
        right2, dhidden1, dheads, sums2 = down(dmlp)
        dqkv, dfirst_parts = back(exchange(dheads))
        grad_inputs, sums1 = leave(exchange(dfirst_parts), tokens, dhidden1, mods)

        def reduced(a, b):
            share = lax.psum_scatter(matmul(a, b).astype(BF), "dp", scatter_dimension=0, tiled=True)
            return lax.psum_scatter(share, "seq", scatter_dimension=1, tiled=True).astype(F32)

        g_proj3 = reduced(left1[:wide], right1[:, 2 * wide :])
        g_proj2 = reduced(left1[wide : 2 * wide], right1[:, :wide])
        g_proj1 = reduced(left1[2 * wide :], right1[:, wide : 2 * wide])
        g_fc2 = reduced(left2[:hidden], dmlp)
        g_fc1 = reduced(left2[hidden : hidden + width], right2[:, :hidden])
        g_out = reduced(left2[hidden + width :], right2[:, hidden:])
        g_heads = lax.psum_scatter(
            times_trans(first_all, dqkv).astype(BF), "dp", scatter_dimension=0, tiled=True
        )

    dmods = jnp.concatenate([sums1[0:2], sums2[0:3], sum_gate2], axis=0)
    dmods = exchange(dmods.reshape(n_seq, 6 * width // n_seq))
    slot = jnp.arange(slots, dtype=jnp.int32)[:, None, None]
    whose = image_ids[::tok_dev]
    grad_mods = jnp.sum(jnp.where(slot == whose[None, :, None], dmods[None], 0.0), axis=1)

    units = [g_heads[:, i * local : (i + 1) * local] for i in range(3)]
    outgoing = []
    for target in range(n_seq):
        mine = jnp.zeros_like(units[0])
        for i in range(3):
            mine = jnp.where((n_seq * i + rank) // 3 == target, units[i], mine)
        outgoing.append(mine)
    incoming = exchange(jnp.stack(outgoing))
    columns = [jnp.zeros(units[0].shape, BF) for _ in range(3)]
    for source in range(n_seq):
        for i in range(3):
            unit = n_seq * i + source
            columns[unit % 3] = jnp.where(unit // 3 == rank, incoming[source], columns[unit % 3])
    g_qkv = jnp.concatenate(columns, axis=1).astype(F32)

    return (rounded, grad_inputs, grad_mods, g_qkv, g_out, g_fc1, g_fc2, g_proj1, g_proj2, g_proj3)


def solution(mesh):
    tok = P(("dp", "seq"), None)
    in_specs = (tok, P("dp", None), P("dp")) + (P(),) * 7 + (tok, tok)
    out_specs = (tok, tok) + (P("dp", "seq"),) * 8
    return jax.shard_map(shards, mesh=mesh, in_specs=in_specs, out_specs=out_specs, check_vma=False)
```

```python
import functools

import jax
import jax.numpy as jnp
from jax import lax
from jax.experimental import pallas as pl
from jax.experimental.pallas import tpu as pltpu
from jax.sharding import PartitionSpec as P

H = 16
HD = 72
HP = 80
LEN = 1024
EPS_NORM = 1e-06
SCALE = HD ** (-0.5)
EXP2_SCALE = SCALE * 1.4426950408889634
GELU_A = 0.7978845608028654
GELU_B = 0.044715
BF = jnp.bfloat16
F32 = jnp.float32
ANY = pl.BlockSpec(memory_space=pl.ANY)
VMEM = pl.BlockSpec(memory_space=pltpu.VMEM)
SMEM = pl.BlockSpec(memory_space=pltpu.SMEM)
ROOM = 60 << 20


def matmul(left, right):
    return jnp.dot(left, right, preferred_element_type=F32)


def times_trans(left, right):
    return lax.dot_general(left, right, (((1,), (1,)), ((), ())), preferred_element_type=F32)


def trans_times(left, right):
    return lax.dot_general(left, right, (((0,), (0,)), ((), ())), preferred_element_type=F32)


def row_mean(v):
    return jnp.mean(v, axis=-1, keepdims=True)


def normalize(v):
    centre = v - row_mean(v)
    inv = lax.rsqrt(row_mean(centre * centre) + EPS_NORM)
    return centre * inv, inv


def norm_back(e, normed, inv):
    return (e - row_mean(e) - normed * row_mean(e * normed)) * inv


def col_sum(v):
    return jnp.sum(v, axis=0, keepdims=True)


def sigmoid(v):
    return 1.0 / (1.0 + jnp.exp(-v))


def shape(dims, kind=BF):
    return jax.ShapeDtypeStruct(dims, kind)


def params(**more):
    return pltpu.CompilerParams(vmem_limit_bytes=ROOM, **more)


def enter_kernel(slot_ref, tokens_ref, mod_ref, mods_ref, out_ref):
    width = tokens_ref.shape[1]
    table = mod_ref[...].astype(F32)
    mine = lax.broadcasted_iota(jnp.int32, table.shape, 0) == slot_ref[0]
    mods = col_sum(jnp.where(mine, table, 0.0))
    mods_ref[...] = jnp.zeros_like(mods_ref)
    for i in range(6):
        mods_ref[i : i + 1, :] = mods[:, i * width : (i + 1) * width]
    normed, _ = normalize(tokens_ref[...].astype(F32))
    first = normed * (1.0 + mods[:, width : 2 * width]) + mods[:, 0:width]
    out_ref[...] = jnp.transpose(first.astype(BF))


def enter(slot, tokens, modulation):
    tok, width = tokens.shape
    return pl.pallas_call(
        enter_kernel,
        out_shape=(shape((8, width), F32), shape((width, tok))),
        in_specs=[SMEM, VMEM, VMEM],
        out_specs=(VMEM, VMEM),
        compiler_params=params(),
        name="enter",
    )(slot, tokens, modulation)


def attend_forward_kernel(size, heads, tile, diagonal, one_ref, rank_ref, *refs):
    pieces = refs[: 2 * size - 1]
    w_ref, idk_ref, idq_ref, x_ref, o_ref, qkv_ref, lse_ref, k_ref, o_all_ref = refs[2 * size - 1 :]
    tok = pieces[0].shape[1]
    total = x_ref.shape[1]
    x_ref[:, 0:tok] = pieces[0][...]
    for d in range(1, size):
        x_ref[:, d * tok : (d + 1) * tok] = pieces[2 * d - 1][...] + pieces[2 * d][...]

    def project(i, carry):
        at = pl.ds(pl.multiple_of(i * tile, tile), tile)
        qkv_ref[:, at] = matmul(w_ref[...], x_ref[:, at]).astype(BF)
        return carry

    lax.fori_loop(0, total // tile, project, 0)

    def head_step(head, carry):
        q_at = pl.ds(pl.multiple_of(head * HP, HP), HP)
        k_at = pl.ds(pl.multiple_of((heads + head) * HP, HP), HP)
        v_at = pl.ds(pl.multiple_of((2 * heads + head) * HP, HP), HP)
        o_at = pl.ds(pl.multiple_of(head * HD, 8), HD)
        k_ref[...] = jnp.transpose(qkv_ref[k_at, :])

        def block(at, keys, masked):
            s = matmul(k_ref[keys, :], qkv_ref[q_at, at]) * EXP2_SCALE
            if masked:
                s = jnp.where(idk_ref[...] == idq_ref[:, at], s, -1e30)
            top = jnp.max(s, axis=0, keepdims=True)
            e = jnp.exp2(s - top)
            tot = col_sum(e)
            o = matmul(qkv_ref[v_at, keys], e.astype(BF)) * (1.0 / tot)
            o_all_ref[o_at, at] = o[0:HD, :]
            lse_ref[pl.ds(head, 1), at] = top + jnp.log2(tot)

        def full(masked):
            def step(i, inner):
                block(pl.ds(pl.multiple_of(i * tile, tile), tile), pl.ds(0, total), masked)
                return inner

            lax.fori_loop(0, total // tile, step, 0)

        @pl.when(one_ref[0] == 1)
        def _():
            full(False)

        @pl.when(one_ref[0] == 0)
        def _():
            if diagonal:

                def step(i, inner):
                    at = pl.ds(pl.multiple_of(i * tile, tile), tile)
                    block(at, at, False)
                    return inner

                lax.fori_loop(0, total // tile, step, 0)
            else:
                full(True)

        return carry

    lax.fori_loop(0, heads, head_step, 0)
    for d in range(size):
        o_ref[lax.rem(rank_ref[0] + d, size)] = o_all_ref[:, d * tok : (d + 1) * tok].astype(BF)


def attend_forward(one, rank, pieces, w, idk, idq, heads, tile, diagonal):
    width, tok = pieces[0].shape
    size = (len(pieces) + 1) // 2
    total = size * tok
    return pl.pallas_call(
        functools.partial(attend_forward_kernel, size, heads, tile, diagonal),
        out_shape=(
            shape((width, total)),
            shape((size, heads * HD, tok)),
            shape((3 * heads * HP, total)),
            shape((heads, total), F32),
        ),
        in_specs=[SMEM, SMEM] + [VMEM] * (len(pieces) + 3),
        out_specs=(VMEM,) * 4,
        scratch_shapes=[pltpu.VMEM((total, HP), BF), pltpu.VMEM((heads * HD, total), F32)],
        compiler_params=params(),
        name="attend_forward",
    )(one, rank, *pieces, w, idk, idq)


def attend_backward_kernel(size, heads, tile, diagonal, one_ref, rank_ref, *refs):
    dos_ref, qkv_ref, o_ref, lse_ref, w_ref, idk_ref, idq_ref = refs[:7]
    dqkv_ref, dx_ref, k_ref, v_ref, do_ref, dk_ref, dv_ref, acc_ref, delta_ref = refs[7:]
    tok = dos_ref.shape[2]
    total = qkv_ref.shape[1]
    local = heads * HD
    for d in range(size):
        at = slice(d * tok, (d + 1) * tok)
        owner = lax.rem(rank_ref[0] + d, size)
        do = dos_ref[owner].astype(F32)
        do_ref[0:local, at] = do
        do_ref[local : local + HP - HD, at] = jnp.zeros((HP - HD, tok), F32)
        prod = do * o_ref[owner].astype(F32)
        for head in range(heads):
            delta_ref[head : head + 1, at] = col_sum(prod[head * HD : (head + 1) * HD, :])

    def head_step(head, carry):
        q_at = pl.ds(pl.multiple_of(head * HP, HP), HP)
        k_at = pl.ds(pl.multiple_of((heads + head) * HP, HP), HP)
        v_at = pl.ds(pl.multiple_of((2 * heads + head) * HP, HP), HP)
        o_at = pl.ds(pl.multiple_of(head * HD, 8), HP)
        k_ref[...] = jnp.transpose(qkv_ref[k_at, :])
        v_ref[...] = jnp.transpose(qkv_ref[v_at, :])

        def out_at(part):
            return pl.ds(pl.multiple_of(part * local + head * HD, 8), HD)

        def block(at, keys, masked, fresh):
            q = qkv_ref[q_at, at]
            do = do_ref[o_at, at].astype(BF)
            p = jnp.exp2(matmul(k_ref[keys, :], q) * EXP2_SCALE - lse_ref[pl.ds(head, 1), at])
            if masked:
                p = jnp.where(idk_ref[...] == idq_ref[:, at], p, 0.0)
            ds = (p * (matmul(v_ref[keys, :], do) - delta_ref[pl.ds(head, 1), at])).astype(BF)
            dv = times_trans(do, p.astype(BF))
            dk = times_trans(q, ds)
            if fresh:
                dv_ref[:, keys] = dv
                dk_ref[:, keys] = dk
            else:
                dv_ref[:, keys] += dv
                dk_ref[:, keys] += dk
            dq = matmul(qkv_ref[k_at, keys], ds) * SCALE
            acc_ref[out_at(0), at] = dq[0:HD, :]

        def full(masked):
            dk_ref[...] = jnp.zeros_like(dk_ref)
            dv_ref[...] = jnp.zeros_like(dv_ref)

            def step(i, inner):
                block(pl.ds(pl.multiple_of(i * tile, tile), tile), pl.ds(0, total), masked, False)
                return inner

            lax.fori_loop(0, total // tile, step, 0)

        @pl.when(one_ref[0] == 1)
        def _():
            full(False)

        @pl.when(one_ref[0] == 0)
        def _():
            if diagonal:

                def step(i, inner):
                    at = pl.ds(pl.multiple_of(i * tile, tile), tile)
                    block(at, at, False, True)
                    return inner

                lax.fori_loop(0, total // tile, step, 0)
            else:
                full(True)

        acc_ref[out_at(1), :] = dk_ref[0:HD, :] * SCALE
        acc_ref[out_at(2), :] = dv_ref[0:HD, :]
        return carry

    lax.fori_loop(0, heads, head_step, 0)
    dqkv_ref[...] = acc_ref[...].astype(BF)
    for d in range(size):
        dx_ref[d] = trans_times(dqkv_ref[:, d * tok : (d + 1) * tok], w_ref[...]).astype(BF)


def attend_backward(one, rank, dos, qkv, o, lse, w, idk, idq, heads, tile, diagonal):
    size, local, tok = dos.shape
    total = size * tok
    width = w.shape[1]
    return pl.pallas_call(
        functools.partial(attend_backward_kernel, size, heads, tile, diagonal),
        out_shape=(shape((3 * local, total)), shape((size, tok, width))),
        in_specs=[SMEM, SMEM] + [VMEM] * 7,
        out_specs=(VMEM, VMEM),
        scratch_shapes=[
            pltpu.VMEM((total, HP), BF),
            pltpu.VMEM((total, HP), BF),
            pltpu.VMEM((local + HP - HD, total), F32),
            pltpu.VMEM((HP, total), F32),
            pltpu.VMEM((HP, total), F32),
            pltpu.VMEM((3 * local, total), F32),
            pltpu.VMEM((heads, total), F32),
        ],
        compiler_params=params(),
        name="attend_backward",
    )(one, rank, dos, qkv, o, lse, w, idk, idq)


STEP = 512


def middle_kernel(*refs):
    (o_refs, tokens_ref, mods_ref, dino_ref, cot_ref, wo_any, w1_any, w2_any, p1_any, p2_any, p3_any) = refs[:11]
    (out_ref, a1_ref, dr2_ref, left1_ref, right1_ref, left2_ref, gp_ref, dmlp_ref, dy_ref, normed_ref, inv_ref, attn_ref,
     gate_ref) = refs[11:24]
    (wo_ref, w1_ref, w2_ref, p1_ref, p2_ref, p3_ref, act_ref, w1_sem, sems) = refs[24:]
    size, local, tok = o_refs.shape
    width = size * local
    hidden = w1_any.shape[1]
    wide, narrow = p3_ref.shape
    steps = hidden // STEP
    slots = w1_ref.shape[0]
    a2_ref, y_ref = left1_ref.at[0:wide, :], left1_ref.at[wide:, :]
    g_ref, b_ref = left2_ref.at[0:hidden, :], left2_ref.at[hidden : hidden + width, :]
    o_ref = left2_ref.at[hidden + width :, :]
    dr1_ref, dz_ref = right1_ref.at[:, 0:wide], right1_ref.at[:, wide:]
    wo_copy = pltpu.make_async_copy(wo_any, wo_ref, sems.at[4])
    wo_copy.start()

    def w1_copy(i):
        at = pl.ds(pl.multiple_of(i * STEP, STEP), STEP)
        slot = lax.rem(i, slots)
        return pltpu.make_async_copy(w1_any.at[:, at], w1_ref.at[slot], w1_sem.at[slot])

    for i in range(slots):
        w1_copy(i).start()
    w2_copy = pltpu.make_async_copy(w2_any, w2_ref, sems.at[0])
    p1_copy = pltpu.make_async_copy(p1_any, p1_ref, sems.at[1])
    p2_copy = pltpu.make_async_copy(p2_any, p2_ref, sems.at[2])
    p3_copy = pltpu.make_async_copy(p3_any, p3_ref, sems.at[3])
    for copy in (w2_copy, p1_copy, p2_copy, p3_copy):
        copy.start()

    gate1, shift2, scale2, gate2 = [mods_ref[i : i + 1, :] for i in (2, 3, 4, 5)]
    for d in range(size):
        o_ref[d * local : (d + 1) * local, :] = o_refs[d]
    wo_copy.wait()
    attn = trans_times(o_ref[...], wo_ref[...])
    attn_ref[...] = attn
    h1 = tokens_ref[...].astype(F32) + gate1 * attn
    normed, inv = normalize(h1)
    normed_ref[...] = normed
    inv_ref[...] = inv
    b = (normed * (1.0 + scale2) + shift2).astype(BF)
    b_ref[...] = jnp.transpose(b)

    def up(i, carry):
        at = pl.ds(pl.multiple_of(i * STEP, STEP), STEP)
        w1_copy(i).wait()
        u = matmul(b, w1_ref[lax.rem(i, slots)])

        @pl.when(i + slots < steps)
        def _():
            w1_copy(i + slots).start()

        sq = u * u
        t = jnp.tanh(u * (GELU_A + (GELU_A * GELU_B) * sq))
        half = 0.5 * (1.0 + t)
        g = (u * half).astype(BF)
        gp_ref[:, at] = (half + u * (1.0 - t * t) * (0.5 * GELU_A + (1.5 * GELU_A * GELU_B) * sq)).astype(BF)
        act_ref[:, at] = g
        g_ref[at, :] = jnp.transpose(g)
        return carry

    lax.fori_loop(0, steps, up, 0)
    w2_copy.wait()
    mlp = matmul(act_ref[...], w2_ref[...])
    y = (h1 + gate2 * mlp).astype(BF)
    out_ref[...] = y
    y_ref[...] = jnp.transpose(y)
    def project(source, w_ref, held, out_t_ref, slope_ref):
        def step(i, carry):
            at = pl.ds(pl.multiple_of(i * STEP, STEP), STEP)
            r = matmul(source, w_ref[:, at])
            sig = sigmoid(r)
            act = (r * sig).astype(BF)
            act_ref[:, pl.ds(pl.multiple_of(held + i * STEP, STEP), STEP)] = act
            out_t_ref[at, :] = jnp.transpose(act)
            slope_ref[:, at] = (sig * (1.0 + r * (1.0 - sig))).astype(BF)
            return carry

        lax.fori_loop(0, wide // STEP, step, 0)
        return act_ref[:, held : held + wide]

    def project_back(source, w_ref, slope_ref):
        def step(i, carry):
            at = pl.ds(pl.multiple_of(i * STEP, STEP), STEP)
            slope_ref[:, at] = (times_trans(source, w_ref[at, :]) * slope_ref[:, at].astype(F32)).astype(BF)
            return carry

        lax.fori_loop(0, wide // STEP, step, 0)
        return slope_ref[...]

    p1_copy.wait()
    a1 = project(y, p1_ref, 0, a1_ref, dr1_ref)
    p2_copy.wait()
    a2 = project(a1, p2_ref, wide, a2_ref, dr2_ref)
    p3_copy.wait()
    z = matmul(a2, p3_ref[...])
    t = dino_ref[...].astype(F32)
    nz = lax.rsqrt(jnp.sum(z * z, axis=-1, keepdims=True) + EPS_NORM)
    nt = lax.rsqrt(jnp.sum(t * t, axis=-1, keepdims=True) + EPS_NORM)
    cosine = jnp.sum(z * t, axis=-1, keepdims=True) * nz * nt
    dz = (-0.5 * (t * (nz * nt) - (cosine * nz * nz) * z)).astype(BF)
    dz_ref[...] = dz
    dr2 = project_back(dz, p3_ref, dr2_ref)
    dr1 = project_back(dr2, p2_ref, dr1_ref)
    dy = cot_ref[...].astype(F32) + times_trans(dr1, p1_ref[...])
    dy_ref[...] = dy
    dmlp_ref[...] = (gate2 * dy).astype(BF)
    gate_ref[...] = col_sum(dy * mlp)


def middle(os, tokens, mods, dino, cot, wo, w1, w2, p1, p2, p3):
    tok, width = tokens.shape
    hidden, wide, narrow = w1.shape[1], p1.shape[1], p3.shape[1]
    return pl.pallas_call(
        middle_kernel,
        out_shape=(
            shape((tok, width)), shape((wide, tok)), shape((tok, wide)), shape((wide + width, tok)),
            shape((tok, wide + narrow)), shape((hidden + 2 * width, tok)), shape((tok, hidden)), shape((tok, width)), shape((tok, width), F32),
            shape((tok, width), F32), shape((tok, 1), F32), shape((tok, width), F32), shape((1, width), F32),
        ),
        in_specs=[VMEM] * 5 + [ANY] * 6,
        out_specs=(VMEM,) * 13,
        scratch_shapes=[
            pltpu.VMEM(dims, BF)
            for dims in (wo.shape, (4, width, STEP), w2.shape, p1.shape, p2.shape, p3.shape, (tok, hidden))
        ]
        + [pltpu.SemaphoreType.DMA((4,)), pltpu.SemaphoreType.DMA((5,))],
        compiler_params=params(),
        name="middle",
    )(os, tokens, mods, dino, cot, wo, w1, w2, p1, p2, p3)


def descend_kernel(size, *refs):
    (dmlp_ref, gp_ref, dy_ref, normed_ref, inv_ref, attn_ref, mods_ref, w2_any, w1_any, wo_any) = refs[:10]
    (right2_ref, dh1_ref, do_ref, sums_ref) = refs[10:14]
    (w2_ref, w1_ref, wo_ref, w2_sem, w1_sem, wo_sem) = refs[14:]
    hidden = w1_ref.shape[1]
    du_ref, dattn_ref = right2_ref.at[:, 0:hidden], right2_ref.at[:, hidden:]
    local = do_ref.shape[1]
    steps = hidden // STEP

    def w2_copy(i):
        at = pl.ds(pl.multiple_of(i * STEP, STEP), STEP)
        return pltpu.make_async_copy(w2_any.at[at, :], w2_ref.at[at, :], w2_sem.at[i])

    for i in range(steps):
        w2_copy(i).start()
    w1_copy = pltpu.make_async_copy(w1_any, w1_ref, w1_sem.at[0])
    w1_copy.start()
    wo_copy = pltpu.make_async_copy(wo_any, wo_ref, wo_sem.at[0])
    wo_copy.start()
    dmlp = dmlp_ref[...]

    def down(i, carry):
        at = pl.ds(pl.multiple_of(i * STEP, STEP), STEP)
        w2_copy(i).wait()
        du_ref[:, at] = (times_trans(dmlp, w2_ref[at, :]) * gp_ref[:, at].astype(F32)).astype(BF)
        return carry

    lax.fori_loop(0, steps, down, 0)
    w1_copy.wait()
    db = times_trans(du_ref[...], w1_ref[...])
    gate1, scale2 = mods_ref[2:3, :], mods_ref[4:5, :]
    normed = normed_ref[...]
    dh1 = dy_ref[...] + norm_back(db * (1.0 + scale2), normed, inv_ref[...])
    dh1_ref[...] = dh1
    dattn = (gate1 * dh1).astype(BF)
    dattn_ref[...] = dattn
    sums_ref[...] = jnp.zeros_like(sums_ref)
    sums_ref[0:1, :] = col_sum(dh1 * attn_ref[...])
    sums_ref[1:2, :] = col_sum(db)
    sums_ref[2:3, :] = col_sum(db * normed)
    wo_copy.wait()
    for d in range(size):
        do_ref[d] = times_trans(wo_ref[d * local : (d + 1) * local, :], dattn).astype(BF)


def descend(size, dmlp, gp, dy, normed, inv, attn, mods, w2, w1, wo):
    tok, width = dmlp.shape
    hidden = w1.shape[1]
    return pl.pallas_call(
        functools.partial(descend_kernel, size),
        out_shape=(
            shape((tok, hidden + width)), shape((tok, width), F32),
            shape((size, width // size, tok)), shape((8, width), F32),
        ),
        in_specs=[VMEM] * 7 + [ANY] * 3,
        out_specs=(VMEM,) * 4,
        scratch_shapes=[pltpu.VMEM(w.shape, BF) for w in (w2, w1, wo)]
        + [
            pltpu.SemaphoreType.DMA((hidden // STEP,)),
            pltpu.SemaphoreType.DMA((1,)),
            pltpu.SemaphoreType.DMA((1,)),
        ],
        compiler_params=params(),
        name="descend",
    )(dmlp, gp, dy, normed, inv, attn, mods, w2, w1, wo)


def leave_kernel(part_ref, left_ref, right_ref, tokens_ref, dh1_ref, mods_ref, out_ref, sums_ref):
    da = part_ref[...].astype(F32) + left_ref[...].astype(F32) + right_ref[...].astype(F32)
    normed, inv = normalize(tokens_ref[...].astype(F32))
    out_ref[...] = (dh1_ref[...] + norm_back(da * (1.0 + mods_ref[1:2, :]), normed, inv)).astype(BF)
    sums_ref[...] = jnp.zeros_like(sums_ref)
    sums_ref[0:1, :] = col_sum(da)
    sums_ref[1:2, :] = col_sum(da * normed)


def leave(part, from_left, from_right, tokens, dh1, mods):
    return pl.pallas_call(
        leave_kernel,
        out_shape=(shape(tokens.shape), shape((8, tokens.shape[1]), F32)),
        in_specs=[VMEM] * 6,
        out_specs=(VMEM, VMEM),
        compiler_params=params(),
        name="leave",
    )(part, from_left, from_right, tokens, dh1, mods)


def weight_grad_kernel(count, flat, rows, packs, rows_ref, *refs):
    lefts = refs[:count]
    rights = refs[count : count * (1 + len(rows))]
    outs = refs[count * (1 + len(rows)) : -2]
    held_ref, sem = refs[-2:]
    blocks = sum(packs)
    part = lefts[0].shape[1]
    copies, held_at, held = [], [], 0
    for job, deep in enumerate(rows):
        held_at.append(held)
        for i in range(blocks):
            at = pl.ds(pl.multiple_of(rows_ref[job * blocks + i], 16), deep)
            for j in range(count):
                copies.append(
                    pltpu.make_async_copy(
                        lefts[j].at[at, :],
                        held_ref.at[held : held + deep, j * part : (j + 1) * part],
                        sem.at[len(copies)],
                    )
                )
            held += deep

    @pl.when(pl.program_id(0) == 0)
    def _():
        for copy in copies:
            copy.start()
        for copy in copies:
            copy.wait()

    dot = times_trans if flat else matmul
    for job, deep in enumerate(rows):
        base = held_at[job]
        for spot, pack in enumerate(packs):
            out_ref = outs[job * len(packs) + spot]
            total = None
            for j in range(count):
                term = dot(
                    held_ref[base : base + pack * deep, j * part : (j + 1) * part], rights[job * count + j][...]
                )
                total = term if total is None else total + term
            out_ref[...] = total.reshape(out_ref.shape).astype(BF)
            base += pack * deep


def weight_grad(lefts, rights, jobs, packs, wide, step, flat=False):
    count = len(lefts)
    part = lefts[0].shape[1]
    rows = tuple(job[1] for job in jobs)

    def right_spec(base):
        if flat:
            return pl.BlockSpec((step, part), lambda i, b: (i + base, 0))
        return pl.BlockSpec((part, step), lambda i, b: (0, i + base))

    outs = pl.pallas_call(
        functools.partial(weight_grad_kernel, count, flat, rows, packs),
        out_shape=tuple(shape((pack, deep, wide)) for deep in rows for pack in packs),
        grid_spec=pltpu.PrefetchScalarGridSpec(
            num_scalar_prefetch=1,
            grid=(wide // step,),
            in_specs=[ANY] * count + [right_spec(job[2]) for job in jobs for _ in range(count)],
            out_specs=tuple(
                pl.BlockSpec((pack, deep, step), lambda i, b: (0, 0, i)) for deep in rows for pack in packs
            ),
            scratch_shapes=[
                pltpu.VMEM((sum(packs) * sum(rows), part * count), BF),
                pltpu.SemaphoreType.DMA((sum(packs) * count * len(rows),)),
            ],
        ),
        compiler_params=params(dimension_semantics=("arbitrary",)),
        name="weight_grad",
    )(jnp.concatenate([job[0] for job in jobs]), *lefts, *(list(rights) * len(jobs)))
    return [outs[i * len(packs) : (i + 1) * len(packs)] for i in range(len(jobs))]


def weight_grad_seq_kernel(count, rows, order_ref, *refs):
    lefts, rights = refs[:count], refs[count : 2 * count]
    near_ref, far_ref, own_ref, held_ref, sem = refs[2 * count :]
    blocks = held_ref.shape[0] // rows
    part = lefts[0].shape[1]
    step = pl.program_id(0)
    copies = [
        pltpu.make_async_copy(
            lefts[j].at[pl.ds(pl.multiple_of(order_ref[4 + i], 16), rows), :],
            held_ref.at[i * rows : (i + 1) * rows, j * part : (j + 1) * part],
            sem.at[i * count + j],
        )
        for i in range(blocks)
        for j in range(count)
    ]

    @pl.when(step == 0)
    def _():
        for copy in copies:
            copy.start()
        for copy in copies:
            copy.wait()

    total = None
    for j in range(count):
        term = matmul(held_ref[:, j * part : (j + 1) * part], rights[j][...])
        total = term if total is None else total + term
    total = total.astype(BF)

    @pl.when(step < 2)
    def _():
        near_ref[0] = total

    @pl.when(step == 2)
    def _():
        far_ref[...] = total

    @pl.when(step == 3)
    def _():
        own_ref[...] = total


def weight_grad_seq(lefts, rights, row_starts, rows, columns, step):
    count = len(lefts)
    part = lefts[0].shape[1]
    blocks = row_starts.shape[0]
    return pl.pallas_call(
        functools.partial(weight_grad_seq_kernel, count, rows),
        out_shape=(shape((2, blocks * rows, step)), shape((blocks * rows, step)), shape((blocks * rows, step))),
        grid_spec=pltpu.PrefetchScalarGridSpec(
            num_scalar_prefetch=1,
            grid=(4,),
            in_specs=[ANY] * count + [pl.BlockSpec((part, step), lambda i, b: (0, b[i]))] * count,
            out_specs=(
                pl.BlockSpec((1, blocks * rows, step), lambda i, b: (jnp.minimum(i, 1), 0, 0)),
                pl.BlockSpec((blocks * rows, step), lambda i, b: (0, 0)),
                pl.BlockSpec((blocks * rows, step), lambda i, b: (0, 0)),
            ),
            scratch_shapes=[
                pltpu.VMEM((blocks * rows, part * count), BF),
                pltpu.SemaphoreType.DMA((blocks * count,)),
            ],
        ),
        compiler_params=params(dimension_semantics=("arbitrary",)),
        name="weight_grad_seq",
    )(jnp.concatenate([columns, row_starts]), *lefts, *rights)


def split_kernel(turned, rank_ref, keep_ref, got1_ref, got2_ref, near_ref, far_ref, own_ref):
    total = keep_ref[0].astype(F32) + got1_ref[got1_ref.shape[0] - 1].astype(F32) + got2_ref[0].astype(F32)
    total = total.astype(BF)
    if turned:
        total = jnp.transpose(total)
    size = 4
    block = total.shape[0 if turned else 1] // size
    for j in range(size):
        at = slice(j * block, (j + 1) * block)
        piece = total[at, :] if turned else total[:, at]
        mask = j ^ rank_ref[0]

        @pl.when(mask == 3)
        def _():
            near_ref[0] = piece

        @pl.when(mask == 1)
        def _():
            near_ref[1] = piece

        @pl.when(mask == 2)
        def _():
            far_ref[...] = piece

        @pl.when(mask == 0)
        def _():
            own_ref[...] = piece


def split(rank, keep, got1, got2, turned=False):
    rows, cols = keep.shape[1:]
    dims = (cols // 4, rows) if turned else (rows, cols // 4)
    return pl.pallas_call(
        functools.partial(split_kernel, turned),
        out_shape=(shape((2,) + dims), shape(dims), shape(dims)),
        in_specs=[SMEM, VMEM, VMEM, VMEM],
        out_specs=(VMEM,) * 3,
        compiler_params=params(),
        name="split",
    )(rank, keep, got1, got2)


def flip(x, axis, size, bit):
    return lax.ppermute(x, axis, [(i, i ^ bit) for i in range(size)])


def add(a, b):
    return (a.astype(F32) + b.astype(F32)).astype(BF)


def masks_of(bits):
    out = []
    for i in range(2 ** len(bits)):
        mask = 0
        for spot, bit in enumerate(bits):
            if not (i >> (len(bits) - 1 - spot)) & 1:
                mask |= bit
        out.append(mask)
    return out


def after(x, *others):
    return together(x, *others)[0]


def together(*values):
    leaves, tree = jax.tree.flatten(values)
    return jax.tree.unflatten(tree, lax.optimization_barrier(tuple(leaves)))


def exchange(blocks):
    return lax.all_to_all(blocks, "seq", split_axis=0, concat_axis=0, tiled=True)


def shards(
    tokens, modulation, image_ids, w_qkv, w_out, w_fc1, w_fc2, w_proj1, w_proj2, w_proj3, dino, cotangent,
):
    n_seq = lax.axis_size("seq")
    n_dp = lax.axis_size("dp")
    rank = lax.axis_index("seq")
    me = lax.axis_index("dp")
    tok_dev, width = tokens.shape
    group_tok = image_ids.shape[0]
    hidden, wide, narrow = w_fc1.shape[1], w_proj2.shape[0], w_proj3.shape[1]
    heads = H // n_seq
    local = heads * HD
    slots = modulation.shape[0]
    dp_bits = [1 << i for i in range(n_dp.bit_length() - 1)]
    rank_arg = rank.reshape(1).astype(jnp.int32)

    my_slot = lax.dynamic_slice_in_dim(image_ids, rank * tok_dev, 1)
    mods, first = enter(my_slot, tokens, modulation)

    right, left = [first], [first]
    for s in range(1, n_seq):
        right.append(lax.ppermute(right[-1], "seq", [(i, i + 1) for i in range(s - 1, n_seq - 1)]))
        left.append(lax.ppermute(left[-1], "seq", [(i, i - 1) for i in range(1, n_seq - s + 1)]))
    pieces = [first]
    for d in range(1, n_seq):
        pieces += [left[d], right[n_seq - d]]

    columns = [lax.dynamic_slice_in_dim(w_qkv, i * width + rank * local, local, 1) for i in range(3)]
    w_rows = jnp.transpose(jnp.concatenate(columns, axis=1))
    w_pad = jnp.pad(w_rows.reshape(3 * heads, HD, width), ((0, 0), (0, HP - HD), (0, 0))).reshape(3 * heads * HP, width)
    ids_rel = lax.dynamic_slice_in_dim(jnp.concatenate([image_ids, image_ids]), rank * tok_dev, group_tok)
    idk, idq = ids_rel[:, None], ids_rel[None, :]
    one = (image_ids[0] == image_ids[group_tok - 1]).astype(jnp.int32).reshape(1)
    tile = group_tok // 4
    diagonal = tok_dev % tile == 0

    first_all, heads_out, qkv, lse = attend_forward(
        one, rank_arg, pieces, w_pad, idk, idq, heads, tile, diagonal
    )
    attended = exchange(heads_out)
    (rounded, act1, dr2, left1, right1, left2, gelu_slope, dmlp, dy, normed2, inv2, attn, sum_gate2) = middle(
        attended, tokens, mods, dino, cotangent, w_out, w_fc1, w_fc2, w_proj1, w_proj2, w_proj3
    )

    fast = all(k % (16 * n_dp) == 0 for k in (width, hidden, wide)) and n_dp == 8 and n_seq == 4

    def down(dmlp):
        return descend(n_seq, dmlp, gelu_slope, dy, normed2, inv2, attn, mods, w_fc2, w_fc1, w_out)

    def back(dos):
        return attend_backward(
            one, rank_arg, dos, qkv, heads_out, lse, w_rows, idk, idq, heads, tile, diagonal
        )

    if fast:
        swap = lambda x, bit: flip(x, "dp", n_dp, bit)
        core, x, y = dp_bits
        near = lambda v: flip(v, "seq", n_seq, 1)
        far = lambda v: flip(v, "seq", n_seq, 2)

        def job(base, deep, bits, column):
            starts = base + (me ^ jnp.array(masks_of(bits), jnp.int32)) * (deep // n_dp)
            return (starts, deep // n_dp, column)

        def right(v, step):
            return lax.ppermute(v, "seq", [(i, i + 1) for i in range(step)])

        def left(v, step):
            return lax.ppermute(v, "seq", [(i, i - 1) for i in range(n_seq - step, n_seq)])

        def row_starts(base, deep, bits):
            return base + (me ^ jnp.array(masks_of(bits), jnp.int32)) * (deep // n_dp)

        quarter = (1, 1, 1, 1)
        act1_other, dr2_other = swap(act1, core), swap(dr2, core)
        lefts2, dmlps = [left2, swap(left2, core)], [dmlp, swap(dmlp, core)]
        (p2,) = weight_grad([act1, act1_other], [dr2, dr2_other], [job(0, wide, (x, y), 0)], quarter, wide, STEP)
        p2, lefts2, dmlps, left1, right1 = together(p2, lefts2, dmlps, left1, right1)

        p2a = swap(p2[0], x)
        p2b = swap(after(p2[1], p2a), x)
        (f2,) = weight_grad(lefts2, dmlps, [job(0, hidden, (y, x), 0)], quarter, width, 384)
        f2a = swap(f2[0], y)
        lefts1, rights1 = [left1, swap(left1, core)], [right1, swap(right1, core)]
        p1n, p1f, p1o = weight_grad_seq(
            lefts1, after(rights1, f2), row_starts(wide, width, (y, x)), width // n_dp,
            rank ^ jnp.array(masks_of((1, 2)), jnp.int32), wide // n_seq,
        )
        p1z = near(p1n)
        (p3,) = weight_grad(
            lefts1, after(rights1, p1n), [job(0, wide, (y, x), wide // 256)], (2, 1, 1), narrow, 256
        )
        p3a = swap(p3[0], y)
        right2, dhidden1, dheads, sums2 = down(after(dmlp, p3, p2a))
        p2, f2, p2a, p2b, f2a, p1f, p1o, p1z, p3, p3a, right2, dhidden1, dheads, sums2, lefts2 = together(
            p2, f2, p2a, p2b, f2a, p1f, p1o, p1z, p3, p3a, right2, dhidden1, dheads, sums2, lefts2
        )

        f2c, f2b = swap(add(f2[2], f2a), x), swap(f2[1], y)
        dheads_in = exchange(dheads)
        rights2 = [right2, swap(right2, core)]
        (f1,) = weight_grad(lefts2, rights2, [job(hidden, width, (x, y), 0)], quarter, hidden, 1152)
        (fo,) = weight_grad(
            lefts2, after(rights2, f1), [job(hidden + width, width, (y, x), hidden // 384)], (2, 1, 1), width, 384
        )
        p2s, p1f, p1o = add(p2[2], p2a), add(p1f, p1z[0]), add(p1o, p1z[1])
        p3s = add(p3[1], p3a[:1])
        f2, f2c, f2b, dheads_in, p3s, f1, fo, p2s, p1f = together(f2, f2c, f2b, dheads_in, p3s, f1, fo, p2s, p1f)

        f1a, p3c, p2c, p1y = swap(f1[0], x), swap(p3s, x), swap(p2s, y), far(p1f)
        f2n, f2f, f2o = split(rank_arg, f2[3], f2b, f2c, turned=True)
        f2z = near(f2n)
        dqkv, dx = back(after(dheads_in, f2n))
        foa = swap(after(fo[0], dqkv), y)
        (fq,) = weight_grad(
            [first_all], [dqkv], [job(0, width, (core, y, x), 0)], (4, 2, 2), 3 * local, 3 * local, flat=True
        )
        p1d = add(p1o, p1y).reshape(4, width // n_dp, wide // n_seq)
        f1a, p3c, p2c, foa, p1d, f2z, f2f, dqkv, dx, fq, f1 = together(
            f1a, p3c, p2c, foa, p1d, f2z, f2f, dqkv, dx, fq, f1
        )

        f1b, f1c = swap(f1[1], x), swap(add(f1[2], f1a), y)
        up, low = right(dx[3], 1), left(dx[1], 1)
        fqa = swap(fq[0], core)
        f2y = far(add(f2f, f2z[0]))
        p2n, p2f, p2o = split(rank_arg, after(p2[3], fqa), p2b, p2c)
        p2z = near(p2n)
        p3n, p3f, p3o = split(rank_arg, after(p3[2], p2n), p3a, p3c, turned=True)
        fos = add(fo[1], foa[:1])
        f1b, f1c, up, low, f2y, fqa, p2z, p2f, p3n, fos, p1d = together(
            f1b, f1c, up, low, f2y, fqa, p2z, p2f, p3n, fos, p1d
        )

        foc, fqb = swap(fos, x), swap(add(fq[1], fqa[:2]), y)
        up, low = right(add(dx[2], up), 2), left(add(dx[2], low), 2)
        f1n, f1f, f1o = split(rank_arg, f1[3], f1b, f1c)
        f1z = near(f1n)
        fqk = add(fq[2], fqa[2:])
        fqs, fqk = add(fqk[0], fqb[0]), add(fqk[1], fqb[1])
        p1e = swap(after(p1d[0:2], fqb), y)
        fqc = swap(after(fqs, foc), x)
        p2y = far(after(add(p2f, p2z[0]), foc))
        p3z = near(after(p3n, fqb))
        foc, fqk, fqc, p1e, up, low, f1z, f1f, p2y, p3z = together(foc, fqk, fqc, p1e, up, low, f1z, f1f, p2y, p3z)

        up, low = right(add(dx[1], up), 3), left(add(dx[3], low), 3)
        f1y = far(add(f1f, f1z[0]))
        p1x = swap(add(p1d[2], p1e[0]), x)
        g_heads = add(fqk, fqc)
        fon, fof, foo = split(rank_arg, fo[2], foa, foc)
        foz = near(after(fon, p1x))
        p3y = far(after(add(p3f, p3z[0]), p1x))
        up, low, f1y, p1x, p3y, foz = together(up, low, f1y, p1x, p3y, foz)

        def last(*terms):
            return sum(v.astype(F32) for v in terms)

        foy = far(add(fof, foz[0]))
        grad_inputs, sums1 = leave(dx[0], up, low, tokens, dhidden1, mods)
        g_proj1 = last(p1d[3], p1e[1], p1x)
        g_proj2, g_fc1, g_fc2 = last(p2o, p2z[1], p2y), last(f1o, f1z[1], f1y), jnp.transpose(last(f2o, f2z[1], f2y))
        g_proj3, g_out = jnp.transpose(last(p3o, p3z[1], p3y)), last(foo, foz[1], foy)
    else:
        right2, dhidden1, dheads, sums2 = down(dmlp)
        dqkv, dx = back(exchange(dheads))
        up, low = None, None
        for s in range(1, n_seq):
            up = dx[n_seq - s] if up is None else add(dx[n_seq - s], up)
            low = dx[s] if low is None else add(dx[s], low)
            up = lax.ppermute(up, "seq", [(i, i + 1) for i in range(s)])
            low = lax.ppermute(low, "seq", [(i, i - 1) for i in range(n_seq - s, n_seq)])
        grad_inputs, sums1 = leave(dx[0], up, low, tokens, dhidden1, mods)

        def reduced(a, b):
            share = lax.psum_scatter(matmul(a, b).astype(BF), "dp", scatter_dimension=0, tiled=True)
            return lax.psum_scatter(share, "seq", scatter_dimension=1, tiled=True).astype(F32)

        g_proj3 = reduced(left1[:wide], right1[:, wide:])
        g_proj2 = reduced(act1, dr2)
        g_proj1 = reduced(left1[wide:], right1[:, :wide])
        g_fc2 = reduced(left2[:hidden], dmlp)
        g_fc1 = reduced(left2[hidden : hidden + width], right2[:, :hidden])
        g_out = reduced(left2[hidden + width :], right2[:, hidden:])
        g_heads = lax.psum_scatter(
            times_trans(first_all, dqkv).astype(BF), "dp", scatter_dimension=0, tiled=True
        )

    dmods = jnp.concatenate([sums1[0:2], sums2[0:3], sum_gate2], axis=0)
    dmods = exchange(dmods.reshape(n_seq, 6 * width // n_seq))
    slot = jnp.arange(slots, dtype=jnp.int32)[:, None, None]
    whose = image_ids[::tok_dev]
    grad_mods = jnp.sum(jnp.where(slot == whose[None, :, None], dmods[None], 0.0), axis=1)

    units = [g_heads[:, i * local : (i + 1) * local] for i in range(3)]
    outgoing = []
    for target in range(n_seq):
        mine = jnp.zeros_like(units[0])
        for i in range(3):
            mine = jnp.where((n_seq * i + rank) // 3 == target, units[i], mine)
        outgoing.append(mine)
    incoming = exchange(jnp.stack(outgoing))
    columns = [jnp.zeros(units[0].shape, BF) for _ in range(3)]
    for source in range(n_seq):
        for i in range(3):
            unit = n_seq * i + source
            columns[unit % 3] = jnp.where(unit // 3 == rank, incoming[source], columns[unit % 3])
    g_qkv = jnp.concatenate(columns, axis=1).astype(F32)

    return (rounded, grad_inputs, grad_mods, g_qkv, g_out, g_fc1, g_fc2, g_proj1, g_proj2, g_proj3)


def solution(mesh):
    tok = P(("dp", "seq"), None)
    in_specs = (tok, P("dp", None), P("dp")) + (P(),) * 7 + (tok, tok)
    out_specs = (tok, tok) + (P("dp", "seq"),) * 8
    return jax.shard_map(shards, mesh=mesh, in_specs=in_specs, out_specs=out_specs, check_vma=False)
```

```python
import functools

import jax
import jax.numpy as jnp
from jax import lax
from jax.experimental import pallas as pl
from jax.experimental.pallas import tpu as pltpu
from jax.sharding import PartitionSpec as P

H = 16
HD = 72
HP = 80
LEN = 1024
EPS_NORM = 1e-06
SCALE = HD ** (-0.5)
EXP2_SCALE = SCALE * 1.4426950408889634
GELU_A = 0.7978845608028654
GELU_B = 0.044715
BF = jnp.bfloat16
F32 = jnp.float32
ANY = pl.BlockSpec(memory_space=pl.ANY)
VMEM = pl.BlockSpec(memory_space=pltpu.VMEM)
SMEM = pl.BlockSpec(memory_space=pltpu.SMEM)
ROOM = 60 << 20


def matmul(left, right):
    return jnp.dot(left, right, preferred_element_type=F32)


def times_trans(left, right):
    return lax.dot_general(left, right, (((1,), (1,)), ((), ())), preferred_element_type=F32)


def trans_times(left, right):
    return lax.dot_general(left, right, (((0,), (0,)), ((), ())), preferred_element_type=F32)


def row_mean(v):
    return jnp.mean(v, axis=-1, keepdims=True)


def normalize(v):
    centre = v - row_mean(v)
    inv = lax.rsqrt(row_mean(centre * centre) + EPS_NORM)
    return centre * inv, inv


def norm_back(e, normed, inv):
    return (e - row_mean(e) - normed * row_mean(e * normed)) * inv


def col_sum(v):
    return jnp.sum(v, axis=0, keepdims=True)


def sigmoid(v):
    return 1.0 / (1.0 + jnp.exp(-v))


def shape(dims, kind=BF):
    return jax.ShapeDtypeStruct(dims, kind)


def params(**more):
    return pltpu.CompilerParams(vmem_limit_bytes=ROOM, **more)


def enter_kernel(slot_ref, tokens_ref, mod_ref, mods_ref, out_ref):
    width = tokens_ref.shape[1]
    table = mod_ref[...].astype(F32)
    mine = lax.broadcasted_iota(jnp.int32, table.shape, 0) == slot_ref[0]
    mods = col_sum(jnp.where(mine, table, 0.0))
    mods_ref[...] = jnp.zeros_like(mods_ref)
    for i in range(6):
        mods_ref[i : i + 1, :] = mods[:, i * width : (i + 1) * width]
    normed, _ = normalize(tokens_ref[...].astype(F32))
    first = normed * (1.0 + mods[:, width : 2 * width]) + mods[:, 0:width]
    out_ref[...] = jnp.transpose(first.astype(BF))


def enter(slot, tokens, modulation):
    tok, width = tokens.shape
    return pl.pallas_call(
        enter_kernel,
        out_shape=(shape((8, width), F32), shape((width, tok))),
        in_specs=[SMEM, VMEM, VMEM],
        out_specs=(VMEM, VMEM),
        compiler_params=params(),
        name="enter",
    )(slot, tokens, modulation)


def attend_forward_kernel(size, heads, tile, diagonal, one_ref, rank_ref, *refs):
    pieces = refs[: 2 * size - 1]
    w_ref, idk_ref, idq_ref, x_ref, o_ref, qkv_ref, lse_ref, k_ref, o_all_ref = refs[2 * size - 1 :]
    tok = pieces[0].shape[1]
    total = x_ref.shape[1]
    x_ref[:, 0:tok] = pieces[0][...]
    for d in range(1, size):
        x_ref[:, d * tok : (d + 1) * tok] = pieces[2 * d - 1][...] + pieces[2 * d][...]

    def project(i, carry):
        at = pl.ds(pl.multiple_of(i * tile, tile), tile)
        qkv_ref[:, at] = matmul(w_ref[...], x_ref[:, at]).astype(BF)
        return carry

    lax.fori_loop(0, total // tile, project, 0)

    def head_step(head, carry):
        q_at = pl.ds(pl.multiple_of(head * HP, HP), HP)
        k_at = pl.ds(pl.multiple_of((heads + head) * HP, HP), HP)
        v_at = pl.ds(pl.multiple_of((2 * heads + head) * HP, HP), HP)
        o_at = pl.ds(pl.multiple_of(head * HD, 8), HD)
        k_ref[...] = jnp.transpose(qkv_ref[k_at, :])

        def block(at, keys, masked):
            s = matmul(k_ref[keys, :], qkv_ref[q_at, at]) * EXP2_SCALE
            if masked:
                s = jnp.where(idk_ref[...] == idq_ref[:, at], s, -1e30)
            top = jnp.max(s, axis=0, keepdims=True)
            e = jnp.exp2(s - top)
            tot = col_sum(e)
            o = matmul(qkv_ref[v_at, keys], e.astype(BF)) * (1.0 / tot)
            o_all_ref[o_at, at] = o[0:HD, :]
            lse_ref[pl.ds(head, 1), at] = top + jnp.log2(tot)

        def full(masked):
            def step(i, inner):
                block(pl.ds(pl.multiple_of(i * tile, tile), tile), pl.ds(0, total), masked)
                return inner

            lax.fori_loop(0, total // tile, step, 0)

        @pl.when(one_ref[0] == 1)
        def _():
            full(False)

        @pl.when(one_ref[0] == 0)
        def _():
            if diagonal:

                def step(i, inner):
                    at = pl.ds(pl.multiple_of(i * tile, tile), tile)
                    block(at, at, False)
                    return inner

                lax.fori_loop(0, total // tile, step, 0)
            else:
                full(True)

        return carry

    lax.fori_loop(0, heads, head_step, 0)
    for d in range(size):
        o_ref[d] = o_all_ref[:, d * tok : (d + 1) * tok].astype(BF)


def attend_forward(one, rank, pieces, w, idk, idq, heads, tile, diagonal):
    width, tok = pieces[0].shape
    size = (len(pieces) + 1) // 2
    total = size * tok
    return pl.pallas_call(
        functools.partial(attend_forward_kernel, size, heads, tile, diagonal),
        out_shape=(
            shape((width, total)),
            shape((size, heads * HD, tok)),
            shape((3 * heads * HP, total)),
            shape((heads, total), F32),
        ),
        in_specs=[SMEM, SMEM] + [VMEM] * (len(pieces) + 3),
        out_specs=(VMEM,) * 4,
        scratch_shapes=[pltpu.VMEM((total, HP), BF), pltpu.VMEM((heads * HD, total), F32)],
        compiler_params=params(),
        name="attend_forward",
    )(one, rank, *pieces, w, idk, idq)


def attend_backward_kernel(size, heads, tile, diagonal, one_ref, rank_ref, *refs):
    dos_ref, qkv_ref, o_ref, lse_ref, w_ref, idk_ref, idq_ref = refs[:7]
    dqkv_ref, dx_ref, k_ref, v_ref, do_ref, dk_ref, dv_ref, acc_ref, delta_ref = refs[7:]
    tok = dos_ref.shape[2]
    total = qkv_ref.shape[1]
    local = heads * HD
    for d in range(size):
        at = slice(d * tok, (d + 1) * tok)
        owner = lax.rem(rank_ref[0] + d, size)
        do = dos_ref[owner].astype(F32)
        do_ref[0:local, at] = do
        do_ref[local : local + HP - HD, at] = jnp.zeros((HP - HD, tok), F32)
        prod = do * o_ref[d].astype(F32)
        for head in range(heads):
            delta_ref[head : head + 1, at] = col_sum(prod[head * HD : (head + 1) * HD, :])

    def head_step(head, carry):
        q_at = pl.ds(pl.multiple_of(head * HP, HP), HP)
        k_at = pl.ds(pl.multiple_of((heads + head) * HP, HP), HP)
        v_at = pl.ds(pl.multiple_of((2 * heads + head) * HP, HP), HP)
        o_at = pl.ds(pl.multiple_of(head * HD, 8), HP)
        k_ref[...] = jnp.transpose(qkv_ref[k_at, :])
        v_ref[...] = jnp.transpose(qkv_ref[v_at, :])

        def out_at(part):
            return pl.ds(pl.multiple_of(part * local + head * HD, 8), HD)

        def block(at, keys, masked, fresh):
            q = qkv_ref[q_at, at]
            do = do_ref[o_at, at].astype(BF)
            p = jnp.exp2(matmul(k_ref[keys, :], q) * EXP2_SCALE - lse_ref[pl.ds(head, 1), at])
            if masked:
                p = jnp.where(idk_ref[...] == idq_ref[:, at], p, 0.0)
            ds = (p * (matmul(v_ref[keys, :], do) - delta_ref[pl.ds(head, 1), at])).astype(BF)
            dv = times_trans(do, p.astype(BF))
            dk = times_trans(q, ds)
            if fresh:
                dv_ref[:, keys] = dv
                dk_ref[:, keys] = dk
            else:
                dv_ref[:, keys] += dv
                dk_ref[:, keys] += dk
            dq = matmul(qkv_ref[k_at, keys], ds) * SCALE
            acc_ref[out_at(0), at] = dq[0:HD, :]

        def full(masked):
            dk_ref[...] = jnp.zeros_like(dk_ref)
            dv_ref[...] = jnp.zeros_like(dv_ref)

            def step(i, inner):
                block(pl.ds(pl.multiple_of(i * tile, tile), tile), pl.ds(0, total), masked, False)
                return inner

            lax.fori_loop(0, total // tile, step, 0)

        @pl.when(one_ref[0] == 1)
        def _():
            full(False)

        @pl.when(one_ref[0] == 0)
        def _():
            if diagonal:

                def step(i, inner):
                    at = pl.ds(pl.multiple_of(i * tile, tile), tile)
                    block(at, at, False, True)
                    return inner

                lax.fori_loop(0, total // tile, step, 0)
            else:
                full(True)

        acc_ref[out_at(1), :] = dk_ref[0:HD, :] * SCALE
        acc_ref[out_at(2), :] = dv_ref[0:HD, :]
        return carry

    lax.fori_loop(0, heads, head_step, 0)
    dqkv_ref[...] = acc_ref[...].astype(BF)
    for d in range(size):
        dx_ref[d] = trans_times(dqkv_ref[:, d * tok : (d + 1) * tok], w_ref[...]).astype(BF)


def attend_backward(one, rank, dos, qkv, o, lse, w, idk, idq, heads, tile, diagonal):
    size, local, tok = dos.shape
    total = size * tok
    width = w.shape[1]
    return pl.pallas_call(
        functools.partial(attend_backward_kernel, size, heads, tile, diagonal),
        out_shape=(shape((3 * local, total)), shape((size, tok, width))),
        in_specs=[SMEM, SMEM] + [VMEM] * 7,
        out_specs=(VMEM, VMEM),
        scratch_shapes=[
            pltpu.VMEM((total, HP), BF),
            pltpu.VMEM((total, HP), BF),
            pltpu.VMEM((local + HP - HD, total), F32),
            pltpu.VMEM((HP, total), F32),
            pltpu.VMEM((HP, total), F32),
            pltpu.VMEM((3 * local, total), F32),
            pltpu.VMEM((heads, total), F32),
        ],
        compiler_params=params(),
        name="attend_backward",
    )(one, rank, dos, qkv, o, lse, w, idk, idq)


STEP = 512


def middle_kernel(size, rank_ref, *refs):
    o_refs, refs = refs[:size], refs[size:]
    (tokens_ref, mods_ref, dino_ref, cot_ref, wo_any, w1_any, w2_any, p1_any, p2_any, p3_any) = refs[:10]
    (out_ref, a1_ref, dr2_ref, left1_ref, right1_ref, left2_ref, gp_ref, dmlp_ref, dy_ref, normed_ref, inv_ref, attn_ref,
     gate_ref) = refs[10:23]
    (wo_ref, w1_ref, w2_ref, p1_ref, p2_ref, p3_ref, act_ref, w1_sem, sems) = refs[23:]
    local, tok = o_refs[0].shape
    width = size * local
    hidden = w1_any.shape[1]
    wide, narrow = p3_ref.shape
    steps = hidden // STEP
    slots = w1_ref.shape[0]
    a2_ref, y_ref = left1_ref.at[0:wide, :], left1_ref.at[wide:, :]
    g_ref, b_ref = left2_ref.at[0:hidden, :], left2_ref.at[hidden : hidden + width, :]
    o_ref = left2_ref.at[hidden + width :, :]
    dr1_ref, dz_ref = right1_ref.at[:, 0:wide], right1_ref.at[:, wide:]
    wo_copy = pltpu.make_async_copy(wo_any, wo_ref, sems.at[4])
    wo_copy.start()

    def w1_copy(i):
        at = pl.ds(pl.multiple_of(i * STEP, STEP), STEP)
        slot = lax.rem(i, slots)
        return pltpu.make_async_copy(w1_any.at[:, at], w1_ref.at[slot], w1_sem.at[slot])

    for i in range(slots):
        w1_copy(i).start()
    w2_copy = pltpu.make_async_copy(w2_any, w2_ref, sems.at[0])
    p1_copy = pltpu.make_async_copy(p1_any, p1_ref, sems.at[1])
    p2_copy = pltpu.make_async_copy(p2_any, p2_ref, sems.at[2])
    p3_copy = pltpu.make_async_copy(p3_any, p3_ref, sems.at[3])
    for copy in (w2_copy, p1_copy, p2_copy, p3_copy):
        copy.start()

    gate1, shift2, scale2, gate2 = [mods_ref[i : i + 1, :] for i in (2, 3, 4, 5)]
    for d in range(size):
        owner = lax.rem(rank_ref[0] + size - d, size)
        o_ref[pl.ds(pl.multiple_of(owner * local, 16), local), :] = o_refs[d][...]
    wo_copy.wait()
    attn = trans_times(o_ref[...], wo_ref[...])
    attn_ref[...] = attn
    h1 = tokens_ref[...].astype(F32) + gate1 * attn
    normed, inv = normalize(h1)
    normed_ref[...] = normed
    inv_ref[...] = inv
    b = (normed * (1.0 + scale2) + shift2).astype(BF)
    b_ref[...] = jnp.transpose(b)

    def up(i, carry):
        at = pl.ds(pl.multiple_of(i * STEP, STEP), STEP)
        w1_copy(i).wait()
        u = matmul(b, w1_ref[lax.rem(i, slots)])

        @pl.when(i + slots < steps)
        def _():
            w1_copy(i + slots).start()

        sq = u * u
        t = jnp.tanh(u * (GELU_A + (GELU_A * GELU_B) * sq))
        half = 0.5 * (1.0 + t)
        g = (u * half).astype(BF)
        gp_ref[:, at] = (half + u * (1.0 - t * t) * (0.5 * GELU_A + (1.5 * GELU_A * GELU_B) * sq)).astype(BF)
        act_ref[:, at] = g
        g_ref[at, :] = jnp.transpose(g)
        return carry

    lax.fori_loop(0, steps, up, 0)
    w2_copy.wait()
    mlp = matmul(act_ref[...], w2_ref[...])
    y = (h1 + gate2 * mlp).astype(BF)
    out_ref[...] = y
    y_ref[...] = jnp.transpose(y)
    def project(source, w_ref, held, out_t_ref, slope_ref):
        def step(i, carry):
            at = pl.ds(pl.multiple_of(i * STEP, STEP), STEP)
            r = matmul(source, w_ref[:, at])
            sig = sigmoid(r)
            act = (r * sig).astype(BF)
            act_ref[:, pl.ds(pl.multiple_of(held + i * STEP, STEP), STEP)] = act
            out_t_ref[at, :] = jnp.transpose(act)
            slope_ref[:, at] = (sig * (1.0 + r * (1.0 - sig))).astype(BF)
            return carry

        lax.fori_loop(0, wide // STEP, step, 0)
        return act_ref[:, held : held + wide]

    def project_back(source, w_ref, slope_ref):
        def step(i, carry):
            at = pl.ds(pl.multiple_of(i * STEP, STEP), STEP)
            slope_ref[:, at] = (times_trans(source, w_ref[at, :]) * slope_ref[:, at].astype(F32)).astype(BF)
            return carry

        lax.fori_loop(0, wide // STEP, step, 0)
        return slope_ref[...]

    p1_copy.wait()
    a1 = project(y, p1_ref, 0, a1_ref, dr1_ref)
    p2_copy.wait()
    a2 = project(a1, p2_ref, wide, a2_ref, dr2_ref)
    p3_copy.wait()
    z = matmul(a2, p3_ref[...])
    t = dino_ref[...].astype(F32)
    nz = lax.rsqrt(jnp.sum(z * z, axis=-1, keepdims=True) + EPS_NORM)
    nt = lax.rsqrt(jnp.sum(t * t, axis=-1, keepdims=True) + EPS_NORM)
    cosine = jnp.sum(z * t, axis=-1, keepdims=True) * nz * nt
    dz = (-0.5 * (t * (nz * nt) - (cosine * nz * nz) * z)).astype(BF)
    dz_ref[...] = dz
    dr2 = project_back(dz, p3_ref, dr2_ref)
    dr1 = project_back(dr2, p2_ref, dr1_ref)
    dy = cot_ref[...].astype(F32) + times_trans(dr1, p1_ref[...])
    dy_ref[...] = dy
    dmlp_ref[...] = (gate2 * dy).astype(BF)
    gate_ref[...] = col_sum(dy * mlp)


def middle(rank, os, tokens, mods, dino, cot, wo, w1, w2, p1, p2, p3):
    tok, width = tokens.shape
    hidden, wide, narrow = w1.shape[1], p1.shape[1], p3.shape[1]
    return pl.pallas_call(
        functools.partial(middle_kernel, len(os)),
        out_shape=(
            shape((tok, width)), shape((wide, tok)), shape((tok, wide)), shape((wide + width, tok)),
            shape((tok, wide + narrow)), shape((hidden + 2 * width, tok)), shape((tok, hidden)), shape((tok, width)), shape((tok, width), F32),
            shape((tok, width), F32), shape((tok, 1), F32), shape((tok, width), F32), shape((1, width), F32),
        ),
        in_specs=[SMEM] + [VMEM] * (len(os) + 4) + [ANY] * 6,
        out_specs=(VMEM,) * 13,
        scratch_shapes=[
            pltpu.VMEM(dims, BF)
            for dims in (wo.shape, (4, width, STEP), w2.shape, p1.shape, p2.shape, p3.shape, (tok, hidden))
        ]
        + [pltpu.SemaphoreType.DMA((4,)), pltpu.SemaphoreType.DMA((5,))],
        compiler_params=params(),
        name="middle",
    )(rank, *os, tokens, mods, dino, cot, wo, w1, w2, p1, p2, p3)


def descend_kernel(size, *refs):
    (dmlp_ref, gp_ref, dy_ref, normed_ref, inv_ref, attn_ref, mods_ref, w2_any, w1_any, wo_any) = refs[:10]
    (right2_ref, dh1_ref, do_ref, sums_ref) = refs[10:14]
    (w2_ref, w1_ref, wo_ref, w2_sem, w1_sem, wo_sem) = refs[14:]
    hidden = w1_ref.shape[1]
    du_ref, dattn_ref = right2_ref.at[:, 0:hidden], right2_ref.at[:, hidden:]
    local = do_ref.shape[1]
    steps = hidden // STEP

    def w2_copy(i):
        at = pl.ds(pl.multiple_of(i * STEP, STEP), STEP)
        return pltpu.make_async_copy(w2_any.at[at, :], w2_ref.at[at, :], w2_sem.at[i])

    for i in range(steps):
        w2_copy(i).start()
    w1_copy = pltpu.make_async_copy(w1_any, w1_ref, w1_sem.at[0])
    w1_copy.start()
    wo_copy = pltpu.make_async_copy(wo_any, wo_ref, wo_sem.at[0])
    wo_copy.start()
    dmlp = dmlp_ref[...]

    def down(i, carry):
        at = pl.ds(pl.multiple_of(i * STEP, STEP), STEP)
        w2_copy(i).wait()
        du_ref[:, at] = (times_trans(dmlp, w2_ref[at, :]) * gp_ref[:, at].astype(F32)).astype(BF)
        return carry

    lax.fori_loop(0, steps, down, 0)
    w1_copy.wait()
    db = times_trans(du_ref[...], w1_ref[...])
    gate1, scale2 = mods_ref[2:3, :], mods_ref[4:5, :]
    normed = normed_ref[...]
    dh1 = dy_ref[...] + norm_back(db * (1.0 + scale2), normed, inv_ref[...])
    dh1_ref[...] = dh1
    dattn = (gate1 * dh1).astype(BF)
    dattn_ref[...] = dattn
    sums_ref[...] = jnp.zeros_like(sums_ref)
    sums_ref[0:1, :] = col_sum(dh1 * attn_ref[...])
    sums_ref[1:2, :] = col_sum(db)
    sums_ref[2:3, :] = col_sum(db * normed)
    wo_copy.wait()
    for d in range(size):
        do_ref[d] = times_trans(wo_ref[d * local : (d + 1) * local, :], dattn).astype(BF)


def descend(size, dmlp, gp, dy, normed, inv, attn, mods, w2, w1, wo):
    tok, width = dmlp.shape
    hidden = w1.shape[1]
    return pl.pallas_call(
        functools.partial(descend_kernel, size),
        out_shape=(
            shape((tok, hidden + width)), shape((tok, width), F32),
            shape((size, width // size, tok)), shape((8, width), F32),
        ),
        in_specs=[VMEM] * 7 + [ANY] * 3,
        out_specs=(VMEM,) * 4,
        scratch_shapes=[pltpu.VMEM(w.shape, BF) for w in (w2, w1, wo)]
        + [
            pltpu.SemaphoreType.DMA((hidden // STEP,)),
            pltpu.SemaphoreType.DMA((1,)),
            pltpu.SemaphoreType.DMA((1,)),
        ],
        compiler_params=params(),
        name="descend",
    )(dmlp, gp, dy, normed, inv, attn, mods, w2, w1, wo)


def leave_kernel(part_ref, left_ref, right_ref, tokens_ref, dh1_ref, mods_ref, out_ref, sums_ref):
    da = part_ref[...].astype(F32) + left_ref[...].astype(F32) + right_ref[...].astype(F32)
    normed, inv = normalize(tokens_ref[...].astype(F32))
    out_ref[...] = (dh1_ref[...] + norm_back(da * (1.0 + mods_ref[1:2, :]), normed, inv)).astype(BF)
    sums_ref[...] = jnp.zeros_like(sums_ref)
    sums_ref[0:1, :] = col_sum(da)
    sums_ref[1:2, :] = col_sum(da * normed)


def leave(part, from_left, from_right, tokens, dh1, mods):
    return pl.pallas_call(
        leave_kernel,
        out_shape=(shape(tokens.shape), shape((8, tokens.shape[1]), F32)),
        in_specs=[VMEM] * 6,
        out_specs=(VMEM, VMEM),
        compiler_params=params(),
        name="leave",
    )(part, from_left, from_right, tokens, dh1, mods)


def weight_grad_kernel(count, flat, rows, packs, rows_ref, *refs):
    lefts = refs[:count]
    rights = refs[count : count * (1 + len(rows))]
    outs = refs[count * (1 + len(rows)) : -2]
    held_ref, sem = refs[-2:]
    blocks = sum(packs)
    part = lefts[0].shape[1]
    copies, held_at, held = [], [], 0
    for job, deep in enumerate(rows):
        held_at.append(held)
        for i in range(blocks):
            at = pl.ds(pl.multiple_of(rows_ref[job * blocks + i], 16), deep)
            for j in range(count):
                copies.append(
                    pltpu.make_async_copy(
                        lefts[j].at[at, :],
                        held_ref.at[held : held + deep, j * part : (j + 1) * part],
                        sem.at[len(copies)],
                    )
                )
            held += deep

    @pl.when(pl.program_id(0) == 0)
    def _():
        for copy in copies:
            copy.start()
        for copy in copies:
            copy.wait()

    dot = times_trans if flat else matmul
    for job, deep in enumerate(rows):
        base = held_at[job]
        for spot, pack in enumerate(packs):
            out_ref = outs[job * len(packs) + spot]
            total = None
            for j in range(count):
                term = dot(
                    held_ref[base : base + pack * deep, j * part : (j + 1) * part], rights[job * count + j][...]
                )
                total = term if total is None else total + term
            out_ref[...] = total.reshape(out_ref.shape).astype(BF)
            base += pack * deep


def weight_grad(lefts, rights, jobs, packs, wide, step, flat=False):
    count = len(lefts)
    part = lefts[0].shape[1]
    rows = tuple(job[1] for job in jobs)

    def right_spec(base):
        if flat:
            return pl.BlockSpec((step, part), lambda i, b: (i + base, 0))
        return pl.BlockSpec((part, step), lambda i, b: (0, i + base))

    outs = pl.pallas_call(
        functools.partial(weight_grad_kernel, count, flat, rows, packs),
        out_shape=tuple(shape((pack, deep, wide)) for deep in rows for pack in packs),
        grid_spec=pltpu.PrefetchScalarGridSpec(
            num_scalar_prefetch=1,
            grid=(wide // step,),
            in_specs=[ANY] * count + [right_spec(job[2]) for job in jobs for _ in range(count)],
            out_specs=tuple(
                pl.BlockSpec((pack, deep, step), lambda i, b: (0, 0, i)) for deep in rows for pack in packs
            ),
            scratch_shapes=[
                pltpu.VMEM((sum(packs) * sum(rows), part * count), BF),
                pltpu.SemaphoreType.DMA((sum(packs) * count * len(rows),)),
            ],
        ),
        compiler_params=params(dimension_semantics=("arbitrary",)),
        name="weight_grad",
    )(jnp.concatenate([job[0] for job in jobs]), *lefts, *(list(rights) * len(jobs)))
    return [outs[i * len(packs) : (i + 1) * len(packs)] for i in range(len(jobs))]


def weight_grad_seq_kernel(count, rows, order_ref, *refs):
    lefts, rights = refs[:count], refs[count : 2 * count]
    near_ref, far_ref, own_ref, held_ref, sem = refs[2 * count :]
    blocks = held_ref.shape[0] // rows
    part = lefts[0].shape[1]
    step = pl.program_id(0)
    copies = [
        pltpu.make_async_copy(
            lefts[j].at[pl.ds(pl.multiple_of(order_ref[4 + i], 16), rows), :],
            held_ref.at[i * rows : (i + 1) * rows, j * part : (j + 1) * part],
            sem.at[i * count + j],
        )
        for i in range(blocks)
        for j in range(count)
    ]

    @pl.when(step == 0)
    def _():
        for copy in copies:
            copy.start()
        for copy in copies:
            copy.wait()

    total = None
    for j in range(count):
        term = matmul(held_ref[:, j * part : (j + 1) * part], rights[j][...])
        total = term if total is None else total + term
    total = total.astype(BF)

    @pl.when(step < 2)
    def _():
        near_ref[0] = total

    @pl.when(step == 2)
    def _():
        far_ref[...] = total

    @pl.when(step == 3)
    def _():
        own_ref[...] = total


def weight_grad_seq(lefts, rights, row_starts, rows, columns, step):
    count = len(lefts)
    part = lefts[0].shape[1]
    blocks = row_starts.shape[0]
    return pl.pallas_call(
        functools.partial(weight_grad_seq_kernel, count, rows),
        out_shape=(shape((2, blocks * rows, step)), shape((blocks * rows, step)), shape((blocks * rows, step))),
        grid_spec=pltpu.PrefetchScalarGridSpec(
            num_scalar_prefetch=1,
            grid=(4,),
            in_specs=[ANY] * count + [pl.BlockSpec((part, step), lambda i, b: (0, b[i]))] * count,
            out_specs=(
                pl.BlockSpec((1, blocks * rows, step), lambda i, b: (jnp.minimum(i, 1), 0, 0)),
                pl.BlockSpec((blocks * rows, step), lambda i, b: (0, 0)),
                pl.BlockSpec((blocks * rows, step), lambda i, b: (0, 0)),
            ),
            scratch_shapes=[
                pltpu.VMEM((blocks * rows, part * count), BF),
                pltpu.SemaphoreType.DMA((blocks * count,)),
            ],
        ),
        compiler_params=params(dimension_semantics=("arbitrary",)),
        name="weight_grad_seq",
    )(jnp.concatenate([columns, row_starts]), *lefts, *rights)


def split_kernel(turned, rank_ref, keep_ref, got1_ref, got2_ref, near_ref, far_ref, own_ref):
    total = keep_ref[0].astype(F32) + got1_ref[got1_ref.shape[0] - 1].astype(F32) + got2_ref[0].astype(F32)
    total = total.astype(BF)
    if turned:
        total = jnp.transpose(total)
    size = 4
    block = total.shape[0 if turned else 1] // size
    for j in range(size):
        at = slice(j * block, (j + 1) * block)
        piece = total[at, :] if turned else total[:, at]
        mask = j ^ rank_ref[0]

        @pl.when(mask == 3)
        def _():
            near_ref[0] = piece

        @pl.when(mask == 1)
        def _():
            near_ref[1] = piece

        @pl.when(mask == 2)
        def _():
            far_ref[...] = piece

        @pl.when(mask == 0)
        def _():
            own_ref[...] = piece


def split(rank, keep, got1, got2, turned=False):
    rows, cols = keep.shape[1:]
    dims = (cols // 4, rows) if turned else (rows, cols // 4)
    return pl.pallas_call(
        functools.partial(split_kernel, turned),
        out_shape=(shape((2,) + dims), shape(dims), shape(dims)),
        in_specs=[SMEM, VMEM, VMEM, VMEM],
        out_specs=(VMEM,) * 3,
        compiler_params=params(),
        name="split",
    )(rank, keep, got1, got2)


def flip(x, axis, size, bit):
    return lax.ppermute(x, axis, [(i, i ^ bit) for i in range(size)])


def add(a, b):
    return (a.astype(F32) + b.astype(F32)).astype(BF)


def masks_of(bits):
    out = []
    for i in range(2 ** len(bits)):
        mask = 0
        for spot, bit in enumerate(bits):
            if not (i >> (len(bits) - 1 - spot)) & 1:
                mask |= bit
        out.append(mask)
    return out


def after(x, *others):
    return together(x, *others)[0]


def together(*values):
    leaves, tree = jax.tree.flatten(values)
    return jax.tree.unflatten(tree, lax.optimization_barrier(tuple(leaves)))


def exchange(blocks):
    return lax.all_to_all(blocks, "seq", split_axis=0, concat_axis=0, tiled=True)


def shards(
    tokens, modulation, image_ids, w_qkv, w_out, w_fc1, w_fc2, w_proj1, w_proj2, w_proj3, dino, cotangent,
):
    n_seq = lax.axis_size("seq")
    n_dp = lax.axis_size("dp")
    rank = lax.axis_index("seq")
    me = lax.axis_index("dp")
    tok_dev, width = tokens.shape
    group_tok = image_ids.shape[0]
    hidden, wide, narrow = w_fc1.shape[1], w_proj2.shape[0], w_proj3.shape[1]
    heads = H // n_seq
    local = heads * HD
    slots = modulation.shape[0]
    dp_bits = [1 << i for i in range(n_dp.bit_length() - 1)]
    rank_arg = rank.reshape(1).astype(jnp.int32)

    my_slot = lax.dynamic_slice_in_dim(image_ids, rank * tok_dev, 1)
    mods, first = enter(my_slot, tokens, modulation)

    right, left = [first], [first]
    for s in range(1, n_seq):
        right.append(lax.ppermute(right[-1], "seq", [(i, i + 1) for i in range(s - 1, n_seq - 1)]))
        left.append(lax.ppermute(left[-1], "seq", [(i, i - 1) for i in range(1, n_seq - s + 1)]))
    pieces = [first]
    for d in range(1, n_seq):
        pieces += [left[d], right[n_seq - d]]

    columns = [lax.dynamic_slice_in_dim(w_qkv, i * width + rank * local, local, 1) for i in range(3)]
    w_rows = jnp.transpose(jnp.concatenate(columns, axis=1))
    w_pad = jnp.pad(w_rows.reshape(3 * heads, HD, width), ((0, 0), (0, HP - HD), (0, 0))).reshape(3 * heads * HP, width)
    ids_rel = lax.dynamic_slice_in_dim(jnp.concatenate([image_ids, image_ids]), rank * tok_dev, group_tok)
    idk, idq = ids_rel[:, None], ids_rel[None, :]
    one = (image_ids[0] == image_ids[group_tok - 1]).astype(jnp.int32).reshape(1)
    tile = group_tok // 4
    diagonal = tok_dev % tile == 0

    first_all, heads_out, qkv, lse = attend_forward(
        one, rank_arg, pieces, w_pad, idk, idq, heads, tile, diagonal
    )
    attended = [heads_out[0]]
    for d in range(1, n_seq):
        attended.append(lax.ppermute(heads_out[d], "seq", [(i, (i + d) % n_seq) for i in range(n_seq)]))
    (rounded, act1, dr2, left1, right1, left2, gelu_slope, dmlp, dy, normed2, inv2, attn, sum_gate2) = middle(
        rank_arg, attended, tokens, mods, dino, cotangent, w_out, w_fc1, w_fc2, w_proj1, w_proj2, w_proj3
    )

    fast = all(k % (16 * n_dp) == 0 for k in (width, hidden, wide)) and n_dp == 8 and n_seq == 4

    def down(dmlp):
        return descend(n_seq, dmlp, gelu_slope, dy, normed2, inv2, attn, mods, w_fc2, w_fc1, w_out)

    def back(dos):
        return attend_backward(
            one, rank_arg, dos, qkv, heads_out, lse, w_rows, idk, idq, heads, tile, diagonal
        )

    def mods_out(sums1):
        rows = jnp.concatenate([sums1[0:2], sums2[0:3], sum_gate2], axis=0)
        return rows.reshape(n_seq, 6 * width // n_seq)

    def units_out(g_heads):
        units = [g_heads[:, i * local : (i + 1) * local] for i in range(3)]
        outgoing = []
        for target in range(n_seq):
            mine = jnp.zeros_like(units[0])
            for i in range(3):
                mine = jnp.where((n_seq * i + rank) // 3 == target, units[i], mine)
            outgoing.append(mine)
        return jnp.stack(outgoing)

    if fast:
        swap = lambda x, bit: flip(x, "dp", n_dp, bit)
        core, x, y = dp_bits
        near = lambda v: flip(v, "seq", n_seq, 1)
        far = lambda v: flip(v, "seq", n_seq, 2)

        def job(base, deep, bits, column):
            starts = base + (me ^ jnp.array(masks_of(bits), jnp.int32)) * (deep // n_dp)
            return (starts, deep // n_dp, column)

        def right(v, step):
            return lax.ppermute(v, "seq", [(i, i + 1) for i in range(step)])

        def left(v, step):
            return lax.ppermute(v, "seq", [(i, i - 1) for i in range(n_seq - step, n_seq)])

        def row_starts(base, deep, bits):
            return base + (me ^ jnp.array(masks_of(bits), jnp.int32)) * (deep // n_dp)

        def row_starts(base, deep, bits):
            return base + (me ^ jnp.array(masks_of(bits), jnp.int32)) * (deep // n_dp)

        def last(*terms):
            return sum(v.astype(F32) for v in terms)

        quarter = (1, 1, 1, 1)
        lefts2, dmlps = [left2, swap(left2, core)], [dmlp, swap(dmlp, core)]
        act1_other, dr2_other = swap(act1, core), swap(dr2, core)
        right2, dhidden1, dheads, sums2 = down(dmlp)
        act1_other, dr2_other, lefts2, dmlps, left1, right1, right2, dheads = together(
            act1_other, dr2_other, lefts2, dmlps, left1, right1, right2, dheads
        )

        dheads_in = exchange(dheads)
        (p2,) = weight_grad([act1, act1_other], [dr2, dr2_other], [job(0, wide, (x, y), 0)], quarter, wide, STEP)
        p2, lefts2, dmlps, left1, right1, right2 = together(p2, lefts2, dmlps, left1, right1, right2)

        p2a = swap(p2[0], x)
        (f2,) = weight_grad(lefts2, dmlps, [job(0, hidden, (y, x), 0)], quarter, width, 384)
        f2a = swap(f2[0], y)
        p2b = swap(after(p2[1], p2a), x)
        lefts1, rights1 = [left1, swap(left1, core)], [right1, swap(right1, core)]
        p1n, p1f, p1o = weight_grad_seq(
            lefts1, after(rights1, f2), row_starts(wide, width, (y, x)), width // n_dp,
            rank ^ jnp.array(masks_of((1, 2)), jnp.int32), wide // n_seq,
        )
        p1z = near(p1n)
        (p3,) = weight_grad(
            lefts1, after(rights1, p1n, dheads_in), [job(0, wide, (y, x), wide // 256)], (2, 1, 1), narrow, 256
        )
        p3a = swap(p3[0], y)
        rights2 = [right2, swap(right2, core)]
        dqkv, dx = back(after(dheads_in, p3, p2a))
        f2s = add(f2[2], after(f2a, dqkv))
        p2, f2, p2a, p2b, f2s, p1f, p1o, p1z, p3, p3a, rights2, dqkv, dx = together(
            p2, f2, p2a, p2b, f2s, p1f, p1o, p1z, p3, p3a, rights2, dqkv, dx
        )

        f2c, f2b = swap(f2s, x), swap(f2[1], y)
        up, low = right(dx[3], 1), left(dx[1], 1)
        (f1,) = weight_grad(lefts2, rights2, [job(hidden, width, (x, y), 0)], quarter, hidden, 1152)
        p1y = far(add(p1f, p1z[0]))
        (fq,) = weight_grad(
            [first_all], [after(dqkv, f1)], [job(0, width, (core, y, x), 0)], (4, 2, 2), 3 * local, 3 * local,
            flat=True,
        )
        (fo,) = weight_grad(
            lefts2, after(rights2, fq), [job(hidden + width, width, (y, x), hidden // 384)], (2, 1, 1), width, 384
        )
        p2s, p3s, p1o = add(p2[2], p2a), add(p3[1], p3a[:1]), add(p1o, p1z[1])
        f2, f2c, f2b, up, low, p1y, p3s, f1, fq, fo, p2s, p1o = together(
            f2, f2c, f2b, up, low, p1y, p3s, f1, fq, fo, p2s, p1o
        )

        f1a, p2c = swap(f1[0], x), swap(p2s, y)
        up, low = right(add(dx[2], up), 2), left(add(dx[2], low), 2)
        fqa = swap(fq[0], core)
        f2n, f2f, f2o = split(rank_arg, after(f2[3], fqa), f2b, f2c, turned=True)
        f2z = near(f2n)
        p3c = swap(after(p3s, f2n), x)
        foa = swap(after(fo[0], p2c), y)
        p1d = add(p1o, p1y).reshape(4, width // n_dp, wide // n_seq)
        p2n, p2f, p2o = split(rank_arg, p2[3], p2b, p2c)
        f1s = add(f1[2], f1a)
        f1s, p3c, p2n, p2f, foa, p1d, f2z, f2f, up, low, fqa, f1, fo = together(
            f1s, p3c, p2n, p2f, foa, p1d, f2z, f2f, up, low, fqa, f1, fo
        )

        f1b, f1c = swap(f1[1], x), swap(f1s, y)
        up, low = right(add(dx[1], up), 3), left(add(dx[3], low), 3)
        f2y = far(add(f2f, f2z[0]))
        p2z = near(p2n)
        p3n, p3f, p3o = split(rank_arg, p3[2], p3a, p3c, turned=True)
        fos, fqs, fqk = add(fo[1], foa[:1]), add(fq[1], fqa[:2]), add(fq[2], fqa[2:])
        f1b, f1c, up, low, f2y, p2z, p2f, p3n, fos, fqs, fqk, p1d = together(
            f1b, f1c, up, low, f2y, p2z, p2f, p3n, fos, fqs, fqk, p1d
        )

        foc, fqb = swap(fos, x), swap(fqs, y)
        p2y = far(add(p2f, p2z[0]))
        f1n, f1f, f1o = split(rank_arg, f1[3], f1b, f1c)
        f1z = near(f1n)
        p1e = swap(p1d[0:2], y)
        p3z = near(p3n)
        fqs, fqk = add(fqk[0], fqb[0]), add(fqk[1], fqb[1])
        fqc = swap(after(fqs, foc), x)
        grad_inputs, sums1 = leave(after(dx[0], f1n), up, low, tokens, dhidden1, mods)
        foc, fqk, fqc, p1e, f1z, f1f, p2y, p3z, sums1 = together(foc, fqk, fqc, p1e, f1z, f1f, p2y, p3z, sums1)

        f1y = far(add(f1f, f1z[0]))
        p1x = swap(add(p1d[2], p1e[0]), x)
        g_heads = add(fqk, fqc)
        fon, fof, foo = split(rank_arg, fo[2], foa, foc)
        foz = near(fon)
        p3y = far(add(p3f, p3z[0]))
        incoming = exchange(units_out(g_heads))
        dmods_in = exchange(mods_out(after(sums1, incoming)))
        f1y, p1x, p3y, foz, incoming, dmods_in = together(f1y, p1x, p3y, foz, incoming, dmods_in)

        foy = far(add(fof, foz[0]))
        g_proj1 = last(p1d[3], p1e[1], p1x)
        g_proj2, g_fc1, g_fc2 = last(p2o, p2z[1], p2y), last(f1o, f1z[1], f1y), jnp.transpose(last(f2o, f2z[1], f2y))
        g_proj3, g_out = jnp.transpose(last(p3o, p3z[1], p3y)), last(foo, foz[1], foy)
    else:
        right2, dhidden1, dheads, sums2 = down(dmlp)
        dqkv, dx = back(exchange(dheads))
        up, low = None, None
        for s in range(1, n_seq):
            up = dx[n_seq - s] if up is None else add(dx[n_seq - s], up)
            low = dx[s] if low is None else add(dx[s], low)
            up = lax.ppermute(up, "seq", [(i, i + 1) for i in range(s)])
            low = lax.ppermute(low, "seq", [(i, i - 1) for i in range(n_seq - s, n_seq)])
        grad_inputs, sums1 = leave(dx[0], up, low, tokens, dhidden1, mods)

        def reduced(a, b):
            share = lax.psum_scatter(matmul(a, b).astype(BF), "dp", scatter_dimension=0, tiled=True)
            return lax.psum_scatter(share, "seq", scatter_dimension=1, tiled=True).astype(F32)

        g_proj3 = reduced(left1[:wide], right1[:, wide:])
        g_proj2 = reduced(act1, dr2)
        g_proj1 = reduced(left1[wide:], right1[:, :wide])
        g_fc2 = reduced(left2[:hidden], dmlp)
        g_fc1 = reduced(left2[hidden : hidden + width], right2[:, :hidden])
        g_out = reduced(left2[hidden + width :], right2[:, hidden:])
        g_heads = lax.psum_scatter(
            times_trans(first_all, dqkv).astype(BF), "dp", scatter_dimension=0, tiled=True
        )

    if not fast:
        outgoing = units_out(g_heads)
        dmods_in, incoming = exchange(mods_out(sums1)), exchange(outgoing)
    slot = jnp.arange(slots, dtype=jnp.int32)[:, None, None]
    whose = image_ids[::tok_dev]
    grad_mods = jnp.sum(jnp.where(slot == whose[None, :, None], dmods_in[None], 0.0), axis=1)
    columns = [jnp.zeros(incoming.shape[1:], BF) for _ in range(3)]
    for source in range(n_seq):
        for i in range(3):
            unit = n_seq * i + source
            columns[unit % 3] = jnp.where(unit // 3 == rank, incoming[source], columns[unit % 3])
    g_qkv = jnp.concatenate(columns, axis=1).astype(F32)

    return (rounded, grad_inputs, grad_mods, g_qkv, g_out, g_fc1, g_fc2, g_proj1, g_proj2, g_proj3)


def solution(mesh):
    tok = P(("dp", "seq"), None)
    in_specs = (tok, P("dp", None), P("dp")) + (P(),) * 7 + (tok, tok)
    out_specs = (tok, tok) + (P("dp", "seq"),) * 8
    return jax.shard_map(shards, mesh=mesh, in_specs=in_specs, out_specs=out_specs, check_vma=False)
```

```python
import functools

import jax
import jax.numpy as jnp
from jax import lax
from jax.experimental import pallas as pl
from jax.experimental.pallas import tpu as pltpu
from jax.sharding import PartitionSpec as P

H = 16
HD = 72
HP = 80
LEN = 1024
EPS_NORM = 1e-06
SCALE = HD ** (-0.5)
EXP2_SCALE = SCALE * 1.4426950408889634
GELU_A = 0.7978845608028654
GELU_B = 0.044715
BF = jnp.bfloat16
F32 = jnp.float32
ANY = pl.BlockSpec(memory_space=pl.ANY)
VMEM = pl.BlockSpec(memory_space=pltpu.VMEM)
SMEM = pl.BlockSpec(memory_space=pltpu.SMEM)
ROOM = 60 << 20
PARTS = 2


def matmul(left, right):
    return jnp.dot(left, right, preferred_element_type=F32)


def times_trans(left, right):
    return lax.dot_general(left, right, (((1,), (1,)), ((), ())), preferred_element_type=F32)


def trans_times(left, right):
    return lax.dot_general(left, right, (((0,), (0,)), ((), ())), preferred_element_type=F32)


def row_mean(v):
    return jnp.mean(v, axis=-1, keepdims=True)


def normalize(v):
    centre = v - row_mean(v)
    inv = lax.rsqrt(row_mean(centre * centre) + EPS_NORM)
    return centre * inv, inv


def norm_back(e, normed, inv):
    return (e - row_mean(e) - normed * row_mean(e * normed)) * inv


def col_sum(v):
    return jnp.sum(v, axis=0, keepdims=True)


def sigmoid(v):
    return 1.0 / (1.0 + jnp.exp(-v))


def shape(dims, kind=BF):
    return jax.ShapeDtypeStruct(dims, kind)


def params(**more):
    return pltpu.CompilerParams(vmem_limit_bytes=ROOM, **more)


def enter_kernel(ids_ref, rank_ref, tokens_ref, mod_ref, mods_ref, *out_refs):
    width = tokens_ref.shape[1]
    table = mod_ref[...].astype(F32)
    mine = lax.broadcasted_iota(jnp.int32, table.shape, 0) == ids_ref[rank_ref[0] * tokens_ref.shape[0]]
    mods = col_sum(jnp.where(mine, table, 0.0))
    mods_ref[...] = jnp.zeros_like(mods_ref)
    for i in range(6):
        mods_ref[i : i + 1, :] = mods[:, i * width : (i + 1) * width]
    normed, _ = normalize(tokens_ref[...].astype(F32))
    first = normed * (1.0 + mods[:, width : 2 * width]) + mods[:, 0:width]
    first = jnp.transpose(first.astype(BF))
    rows = out_refs[0].shape[0]
    for i, out_ref in enumerate(out_refs):
        out_ref[...] = first[i * rows : (i + 1) * rows, :]


def enter(ids, rank, tokens, modulation):
    tok, width = tokens.shape
    return pl.pallas_call(
        enter_kernel,
        out_shape=(shape((8, width), F32),) + (shape((width // PARTS, tok)),) * PARTS,
        in_specs=[SMEM, SMEM, VMEM, VMEM],
        out_specs=(VMEM,) * (1 + PARTS),
        compiler_params=params(),
        name="enter",
    )(ids, rank, tokens, modulation)


def attend_forward_kernel(size, heads, tile, diagonal, one_ref, rank_ref, *refs):
    count = PARTS * (2 * size - 1)
    pieces = refs[:count]
    w_any, idk_ref, idq_ref = refs[count : count + 3]
    o_refs = refs[count + 3 : count + 3 + size]
    (x_any, qkv_any, lse_ref, x_ref, qkv_ref, w_ref, k_ref, o_all_ref, sem, w_sem, out_sem) = refs[count + 3 + size :]
    tok = pieces[0].shape[1]
    total = x_ref.shape[1]
    rows = pieces[0].shape[0]
    rank = rank_ref[0]
    w_copy = pltpu.make_async_copy(w_any, w_ref, w_sem.at[0])
    w_copy.start()

    def piece_copy(d, part, source):
        at = 0 if d == 0 else 2 * d - 2 + source
        return pltpu.make_async_copy(
            pieces[at * PARTS + part],
            x_ref.at[part * rows : (part + 1) * rows, d * tok : (d + 1) * tok],
            sem.at[d, part],
        )

    for part in range(PARTS):
        piece_copy(0, part, 0).start()
    for d in range(1, size):
        for part in range(PARTS):

            @pl.when(rank + d < size)
            def _():
                piece_copy(d, part, 1).start()

            @pl.when(rank + d >= size)
            def _():
                piece_copy(d, part, 2).start()

    w_copy.wait()
    for d in range(size):
        for part in range(PARTS):
            piece_copy(d, part, 1).wait()
        at = slice(d * tok, (d + 1) * tok)
        qkv_ref[:, at] = matmul(w_ref[...], x_ref[:, at]).astype(BF)
    out_copies = [
        pltpu.make_async_copy(x_ref, x_any, out_sem.at[0]),
        pltpu.make_async_copy(qkv_ref, qkv_any, out_sem.at[1]),
    ]
    for copy in out_copies:
        copy.start()

    def head_step(head, carry):
        q_at = pl.ds(pl.multiple_of(head * HP, HP), HP)
        k_at = pl.ds(pl.multiple_of((heads + head) * HP, HP), HP)
        v_at = pl.ds(pl.multiple_of((2 * heads + head) * HP, HP), HP)
        o_at = pl.ds(pl.multiple_of(head * HD, 8), HD)
        k_ref[...] = jnp.transpose(qkv_ref[k_at, :])

        def block(at, keys, masked):
            s = matmul(k_ref[keys, :], qkv_ref[q_at, at]) * EXP2_SCALE
            if masked:
                s = jnp.where(idk_ref[...] == idq_ref[:, at], s, -1e30)
            top = jnp.max(s, axis=0, keepdims=True)
            e = jnp.exp2(s - top)
            tot = col_sum(e)
            o = matmul(qkv_ref[v_at, keys], e.astype(BF)) * (1.0 / tot)
            o_all_ref[o_at, at] = o[0:HD, :]
            lse_ref[pl.ds(head, 1), at] = top + jnp.log2(tot)

        def full(masked):
            def step(i, inner):
                block(pl.ds(pl.multiple_of(i * tile, tile), tile), pl.ds(0, total), masked)
                return inner

            lax.fori_loop(0, total // tile, step, 0, unroll=True)

        @pl.when(one_ref[0] == 1)
        def _():
            full(False)

        @pl.when(one_ref[0] == 0)
        def _():
            if diagonal:

                def step(i, inner):
                    at = pl.ds(pl.multiple_of(i * tile, tile), tile)
                    block(at, at, False)
                    return inner

                lax.fori_loop(0, total // tile, step, 0, unroll=True)
            else:
                full(True)

        return carry

    lax.fori_loop(0, heads, head_step, 0)
    for d in range(size):
        o_refs[d][...] = o_all_ref[:, d * tok : (d + 1) * tok].astype(BF)
    for copy in out_copies:
        copy.wait()


def attend_forward(one, rank, pieces, w, idk, idq, heads, tile, diagonal):
    size = (len(pieces) // PARTS + 1) // 2
    tok = pieces[0].shape[1]
    width, total = PARTS * pieces[0].shape[0], size * tok
    return pl.pallas_call(
        functools.partial(attend_forward_kernel, size, heads, tile, diagonal),
        out_shape=(shape((heads * HD, tok)),) * size
        + (
            shape((width, total)),
            shape((3 * heads * HP, total)),
            shape((heads, total), F32),
        ),
        in_specs=[SMEM, SMEM] + [ANY] * (len(pieces) + 1) + [VMEM, VMEM],
        out_specs=(VMEM,) * size + (ANY, ANY, VMEM),
        scratch_shapes=[
            pltpu.VMEM((width, total), BF),
            pltpu.VMEM((3 * heads * HP, total), BF),
            pltpu.VMEM(w.shape, BF),
            pltpu.VMEM((total, HP), BF),
            pltpu.VMEM((heads * HD, total), F32),
            pltpu.SemaphoreType.DMA((size, PARTS)),
            pltpu.SemaphoreType.DMA((1,)),
            pltpu.SemaphoreType.DMA((2,)),
        ],
        compiler_params=params(),
        name="attend_forward",
    )(one, rank, *pieces, w, idk, idq)


def attend_backward_kernel(size, heads, tile, diagonal, one_ref, rank_ref, *refs):
    o_refs, refs = refs[:size], refs[size:]
    dos_ref, qkv_ref, lse_ref, w_ref, idk_ref, idq_ref = refs[:6]
    dqkv_ref, dx_ref, k_ref, v_ref, do_ref, dk_ref, dv_ref, acc_ref, delta_ref = refs[6:]
    tok = dos_ref.shape[2]
    total = qkv_ref.shape[1]
    local = heads * HD
    for d in range(size):
        at = slice(d * tok, (d + 1) * tok)
        owner = lax.rem(rank_ref[0] + d, size)
        do = dos_ref[owner].astype(F32)
        do_ref[0:local, at] = do
        do_ref[local : local + HP - HD, at] = jnp.zeros((HP - HD, tok), F32)
        prod = do * o_refs[d][...].astype(F32)
        for head in range(heads):
            delta_ref[head : head + 1, at] = col_sum(prod[head * HD : (head + 1) * HD, :])

    def head_step(head, carry):
        q_at = pl.ds(pl.multiple_of(head * HP, HP), HP)
        k_at = pl.ds(pl.multiple_of((heads + head) * HP, HP), HP)
        v_at = pl.ds(pl.multiple_of((2 * heads + head) * HP, HP), HP)
        o_at = pl.ds(pl.multiple_of(head * HD, 8), HP)
        k_ref[...] = jnp.transpose(qkv_ref[k_at, :])
        v_ref[...] = jnp.transpose(qkv_ref[v_at, :])

        def out_at(part):
            return pl.ds(pl.multiple_of(part * local + head * HD, 8), HD)

        def block(at, keys, masked, fresh):
            q = qkv_ref[q_at, at]
            do = do_ref[o_at, at].astype(BF)
            p = jnp.exp2(matmul(k_ref[keys, :], q) * EXP2_SCALE - lse_ref[pl.ds(head, 1), at])
            if masked:
                p = jnp.where(idk_ref[...] == idq_ref[:, at], p, 0.0)
            ds = (p * (matmul(v_ref[keys, :], do) - delta_ref[pl.ds(head, 1), at])).astype(BF)
            dv = times_trans(do, p.astype(BF))
            dk = times_trans(q, ds)
            if fresh:
                dv_ref[:, keys] = dv
                dk_ref[:, keys] = dk
            else:
                dv_ref[:, keys] += dv
                dk_ref[:, keys] += dk
            dq = matmul(qkv_ref[k_at, keys], ds) * SCALE
            acc_ref[out_at(0), at] = dq[0:HD, :]

        def full(masked):
            dk_ref[...] = jnp.zeros_like(dk_ref)
            dv_ref[...] = jnp.zeros_like(dv_ref)

            def step(i, inner):
                block(pl.ds(pl.multiple_of(i * tile, tile), tile), pl.ds(0, total), masked, False)
                return inner

            lax.fori_loop(0, total // tile, step, 0, unroll=True)

        @pl.when(one_ref[0] == 1)
        def _():
            full(False)

        @pl.when(one_ref[0] == 0)
        def _():
            if diagonal:

                def step(i, inner):
                    at = pl.ds(pl.multiple_of(i * tile, tile), tile)
                    block(at, at, False, True)
                    return inner

                lax.fori_loop(0, total // tile, step, 0, unroll=True)
            else:
                full(True)

        acc_ref[out_at(1), :] = dk_ref[0:HD, :] * SCALE
        acc_ref[out_at(2), :] = dv_ref[0:HD, :]
        return carry

    lax.fori_loop(0, heads, head_step, 0)
    dqkv_ref[...] = acc_ref[...].astype(BF)
    for d in range(size):
        dx_ref[d] = trans_times(dqkv_ref[:, d * tok : (d + 1) * tok], w_ref[...]).astype(BF)


def attend_backward(one, rank, dos, qkv, o, lse, w, idk, idq, heads, tile, diagonal):
    size, local, tok = dos.shape
    total = size * tok
    width = w.shape[1]
    return pl.pallas_call(
        functools.partial(attend_backward_kernel, size, heads, tile, diagonal),
        out_shape=(shape((3 * local, total)), shape((size, tok, width))),
        in_specs=[SMEM, SMEM] + [VMEM] * (size + 6),
        out_specs=(VMEM, VMEM),
        scratch_shapes=[
            pltpu.VMEM((total, HP), BF),
            pltpu.VMEM((total, HP), BF),
            pltpu.VMEM((local + HP - HD, total), F32),
            pltpu.VMEM((HP, total), F32),
            pltpu.VMEM((HP, total), F32),
            pltpu.VMEM((3 * local, total), F32),
            pltpu.VMEM((heads, total), F32),
        ],
        compiler_params=params(),
        name="attend_backward",
    )(one, rank, *o, dos, qkv, lse, w, idk, idq)


STEP = 512


def middle_kernel(size, rank_ref, *refs):
    o_refs, refs = refs[:size], refs[size:]
    (tokens_ref, mods_ref, dino_ref, cot_ref, wo_any, w1_any, w2_any, p1_any, p2_any, p3_any) = refs[:10]
    (out_any, a1_any, dr2_any, left1_any, right1_ref, left2_any, gp_any, dmlp_ref, dy_ref, normed_any, inv_ref, attn_any,
     gate_ref) = refs[10:23]
    (wo_ref, w1_ref, w2_ref, p1_ref, p2_ref, p3_ref, act_ref, out_ref, a1_ref, dr2_ref, left1_ref, left2_ref, gp_ref,
     normed_ref, attn_ref, w1_sem, sems, out_sems) = refs[23:]
    flushes = []

    def flush(source, target):
        copy = pltpu.make_async_copy(source, target, out_sems.at[len(flushes)])
        copy.start()
        flushes.append(copy)

    local, tok = o_refs[0].shape
    width = size * local
    hidden = w1_any.shape[1]
    wide, narrow = p3_ref.shape
    steps = hidden // STEP
    slots = w1_ref.shape[0]
    a2_ref, y_ref = left1_ref.at[0:wide, :], left1_ref.at[wide:, :]
    g_ref, b_ref = left2_ref.at[0:hidden, :], left2_ref.at[hidden : hidden + width, :]
    o_ref = left2_ref.at[hidden + width :, :]
    dr1_ref, dz_ref = right1_ref.at[:, 0:wide], right1_ref.at[:, wide:]
    wo_copy = pltpu.make_async_copy(wo_any, wo_ref, sems.at[4])
    wo_copy.start()

    def w1_copy(i):
        at = pl.ds(pl.multiple_of(i * STEP, STEP), STEP)
        slot = lax.rem(i, slots)
        return pltpu.make_async_copy(w1_any.at[:, at], w1_ref.at[slot], w1_sem.at[slot])

    for i in range(slots):
        w1_copy(i).start()
    w2_copy = pltpu.make_async_copy(w2_any, w2_ref, sems.at[0])
    p1_copy = pltpu.make_async_copy(p1_any, p1_ref, sems.at[1])
    p2_copy = pltpu.make_async_copy(p2_any, p2_ref, sems.at[2])
    p3_copy = pltpu.make_async_copy(p3_any, p3_ref, sems.at[3])
    for copy in (w2_copy, p1_copy, p2_copy, p3_copy):
        copy.start()

    gate1, shift2, scale2, gate2 = [mods_ref[i : i + 1, :] for i in (2, 3, 4, 5)]
    for d in range(size):
        owner = lax.rem(rank_ref[0] + size - d, size)
        o_ref[pl.ds(pl.multiple_of(owner * local, 16), local), :] = o_refs[d][...]
    wo_copy.wait()
    attn = trans_times(o_ref[...], wo_ref[...])
    attn_ref[...] = attn
    flush(attn_ref, attn_any)
    h1 = tokens_ref[...].astype(F32) + gate1 * attn
    normed, inv = normalize(h1)
    normed_ref[...] = normed
    flush(normed_ref, normed_any)
    inv_ref[...] = inv
    b = (normed * (1.0 + scale2) + shift2).astype(BF)
    b_ref[...] = jnp.transpose(b)

    def up(i, carry):
        at = pl.ds(pl.multiple_of(i * STEP, STEP), STEP)
        w1_copy(i).wait()
        u = matmul(b, w1_ref[lax.rem(i, slots)])

        @pl.when(i + slots < steps)
        def _():
            w1_copy(i + slots).start()

        sq = u * u
        t = jnp.tanh(u * (GELU_A + (GELU_A * GELU_B) * sq))
        half = 0.5 * (1.0 + t)
        g = (u * half).astype(BF)
        gp_ref[:, at] = (half + u * (1.0 - t * t) * (0.5 * GELU_A + (1.5 * GELU_A * GELU_B) * sq)).astype(BF)
        act_ref[:, at] = g
        g_ref[at, :] = jnp.transpose(g)
        return carry

    lax.fori_loop(0, steps, up, 0, unroll=True)
    flush(left2_ref, left2_any)
    flush(gp_ref, gp_any)
    w2_copy.wait()
    mlp = matmul(act_ref[...], w2_ref[...])
    y = (h1 + gate2 * mlp).astype(BF)
    out_ref[...] = y
    flush(out_ref, out_any)
    y_ref[...] = jnp.transpose(y)
    def project(source, w_ref, held, out_t_ref, slope_ref):
        def step(i, carry):
            at = pl.ds(pl.multiple_of(i * STEP, STEP), STEP)
            r = matmul(source, w_ref[:, at])
            sig = sigmoid(r)
            act = (r * sig).astype(BF)
            act_ref[:, pl.ds(pl.multiple_of(held + i * STEP, STEP), STEP)] = act
            out_t_ref[at, :] = jnp.transpose(act)
            slope_ref[:, at] = (sig * (1.0 + r * (1.0 - sig))).astype(BF)
            return carry

        lax.fori_loop(0, wide // STEP, step, 0, unroll=True)
        return act_ref[:, held : held + wide]

    def project_back(source, w_ref, slope_ref):
        def step(i, carry):
            at = pl.ds(pl.multiple_of(i * STEP, STEP), STEP)
            slope_ref[:, at] = (times_trans(source, w_ref[at, :]) * slope_ref[:, at].astype(F32)).astype(BF)
            return carry

        lax.fori_loop(0, wide // STEP, step, 0, unroll=True)
        return slope_ref[...]

    p1_copy.wait()
    a1 = project(y, p1_ref, 0, a1_ref, dr1_ref)
    flush(a1_ref, a1_any)
    p2_copy.wait()
    a2 = project(a1, p2_ref, wide, a2_ref, dr2_ref)
    flush(left1_ref, left1_any)
    p3_copy.wait()
    z = matmul(a2, p3_ref[...])
    t = dino_ref[...].astype(F32)
    nz = lax.rsqrt(jnp.sum(z * z, axis=-1, keepdims=True) + EPS_NORM)
    nt = lax.rsqrt(jnp.sum(t * t, axis=-1, keepdims=True) + EPS_NORM)
    cosine = jnp.sum(z * t, axis=-1, keepdims=True) * nz * nt
    dz = (-0.5 * (t * (nz * nt) - (cosine * nz * nz) * z)).astype(BF)
    dz_ref[...] = dz
    dr2 = project_back(dz, p3_ref, dr2_ref)
    flush(dr2_ref, dr2_any)
    dr1 = project_back(dr2, p2_ref, dr1_ref)
    dy = cot_ref[...].astype(F32) + times_trans(dr1, p1_ref[...])
    dy_ref[...] = dy
    dmlp_ref[...] = (gate2 * dy).astype(BF)
    gate_ref[...] = col_sum(dy * mlp)
    for copy in flushes:
        copy.wait()


def middle(rank, os, tokens, mods, dino, cot, wo, w1, w2, p1, p2, p3):
    tok, width = tokens.shape
    hidden, wide, narrow = w1.shape[1], p1.shape[1], p3.shape[1]
    return pl.pallas_call(
        functools.partial(middle_kernel, len(os)),
        out_shape=(
            shape((tok, width)), shape((wide, tok)), shape((tok, wide)), shape((wide + width, tok)),
            shape((tok, wide + narrow)), shape((hidden + 2 * width, tok)), shape((tok, hidden)), shape((tok, width)), shape((tok, width), F32),
            shape((tok, width), F32), shape((tok, 1), F32), shape((tok, width), F32), shape((1, width), F32),
        ),
        in_specs=[SMEM] + [VMEM] * (len(os) + 4) + [ANY] * 6,
        out_specs=(ANY, ANY, ANY, ANY, VMEM, ANY, ANY, VMEM, VMEM, ANY, VMEM, ANY, VMEM),
        scratch_shapes=[
            pltpu.VMEM(dims, BF)
            for dims in (wo.shape, (4, width, STEP), w2.shape, p1.shape, p2.shape, p3.shape, (tok, hidden))
        ]
        + [
            pltpu.VMEM(dims, kind)
            for dims, kind in (
                ((tok, width), BF), ((wide, tok), BF), ((tok, wide), BF), ((wide + width, tok), BF),
                ((hidden + 2 * width, tok), BF), ((tok, hidden), BF), ((tok, width), F32), ((tok, width), F32),
            )
        ]
        + [pltpu.SemaphoreType.DMA((4,)), pltpu.SemaphoreType.DMA((5,)), pltpu.SemaphoreType.DMA((8,))],
        compiler_params=params(),
        name="middle",
    )(rank, *os, tokens, mods, dino, cot, wo, w1, w2, p1, p2, p3)


def descend_kernel(size, *refs):
    (dmlp_ref, gp_any, dy_any, normed_any, inv_ref, attn_any, mods_ref, w2_any, w1_any, wo_any) = refs[:10]
    (right2_ref, dh1_ref, do_ref, sums_ref) = refs[10:14]
    (w2_ref, w1_ref, wo_ref, gp_ref, dy_ref, normed_ref, attn_ref, w2_sem, w1_sem, wo_sem, in_sem) = refs[14:]
    hidden = w1_ref.shape[1]
    du_ref, dattn_ref = right2_ref.at[:, 0:hidden], right2_ref.at[:, hidden:]
    local = do_ref.shape[1]
    steps = hidden // STEP

    def w2_copy(i):
        at = pl.ds(pl.multiple_of(i * STEP, STEP), STEP)
        return pltpu.make_async_copy(w2_any.at[at, :], w2_ref.at[at, :], w2_sem.at[i])

    in_copies = [
        pltpu.make_async_copy(source, held, in_sem.at[i])
        for i, (source, held) in enumerate(
            ((gp_any, gp_ref), (dy_any, dy_ref), (normed_any, normed_ref), (attn_any, attn_ref))
        )
    ]
    in_copies[0].start()
    for i in range(steps):
        w2_copy(i).start()
    w1_copy = pltpu.make_async_copy(w1_any, w1_ref, w1_sem.at[0])
    w1_copy.start()
    wo_copy = pltpu.make_async_copy(wo_any, wo_ref, wo_sem.at[0])
    wo_copy.start()
    for copy in in_copies[1:]:
        copy.start()
    in_copies[0].wait()
    dmlp = dmlp_ref[...]

    def down(i, carry):
        at = pl.ds(pl.multiple_of(i * STEP, STEP), STEP)
        w2_copy(i).wait()
        du_ref[:, at] = (times_trans(dmlp, w2_ref[at, :]) * gp_ref[:, at].astype(F32)).astype(BF)
        return carry

    lax.fori_loop(0, steps, down, 0, unroll=True)
    w1_copy.wait()
    for copy in in_copies[1:]:
        copy.wait()
    db = times_trans(du_ref[...], w1_ref[...])
    gate1, scale2 = mods_ref[2:3, :], mods_ref[4:5, :]
    normed = normed_ref[...]
    dh1 = dy_ref[...] + norm_back(db * (1.0 + scale2), normed, inv_ref[...])
    dh1_ref[...] = dh1
    dattn = (gate1 * dh1).astype(BF)
    dattn_ref[...] = dattn
    sums_ref[...] = jnp.zeros_like(sums_ref)
    sums_ref[0:1, :] = col_sum(dh1 * attn_ref[...])
    sums_ref[1:2, :] = col_sum(db)
    sums_ref[2:3, :] = col_sum(db * normed)
    wo_copy.wait()
    for d in range(size):
        do_ref[d] = times_trans(wo_ref[d * local : (d + 1) * local, :], dattn).astype(BF)


def descend(size, dmlp, gp, dy, normed, inv, attn, mods, w2, w1, wo):
    tok, width = dmlp.shape
    hidden = w1.shape[1]
    return pl.pallas_call(
        functools.partial(descend_kernel, size),
        out_shape=(
            shape((tok, hidden + width)), shape((tok, width), F32),
            shape((size, width // size, tok)), shape((8, width), F32),
        ),
        in_specs=[VMEM, ANY, ANY, ANY, VMEM, ANY, VMEM] + [ANY] * 3,
        out_specs=(VMEM,) * 4,
        scratch_shapes=[pltpu.VMEM(w.shape, BF) for w in (w2, w1, wo, gp)]
        + [pltpu.VMEM(v.shape, F32) for v in (dy, normed, attn)]
        + [
            pltpu.SemaphoreType.DMA((hidden // STEP,)),
            pltpu.SemaphoreType.DMA((1,)),
            pltpu.SemaphoreType.DMA((1,)),
            pltpu.SemaphoreType.DMA((4,)),
        ],
        compiler_params=params(),
        name="descend",
    )(dmlp, gp, dy, normed, inv, attn, mods, w2, w1, wo)


def leave_kernel(part_ref, left_ref, right_ref, tokens_ref, dh1_ref, mods_ref, out_ref, sums_ref):
    da = part_ref[...].astype(F32) + left_ref[...].astype(F32) + right_ref[...].astype(F32)
    normed, inv = normalize(tokens_ref[...].astype(F32))
    out_ref[...] = (dh1_ref[...] + norm_back(da * (1.0 + mods_ref[1:2, :]), normed, inv)).astype(BF)
    sums_ref[...] = jnp.zeros_like(sums_ref)
    sums_ref[0:1, :] = col_sum(da)
    sums_ref[1:2, :] = col_sum(da * normed)


def leave(part, from_left, from_right, tokens, dh1, mods):
    return pl.pallas_call(
        leave_kernel,
        out_shape=(shape(tokens.shape), shape((8, tokens.shape[1]), F32)),
        in_specs=[VMEM] * 6,
        out_specs=(VMEM, VMEM),
        compiler_params=params(),
        name="leave",
    )(part, from_left, from_right, tokens, dh1, mods)


def weight_grad_kernel(count, flat, rows, packs, rows_ref, *refs):
    lefts = refs[:count]
    rights = refs[count : count * (1 + len(rows))]
    outs = refs[count * (1 + len(rows)) : -2]
    held_ref, sem = refs[-2:]
    blocks = sum(packs)
    part = lefts[0].shape[1]
    copies, held_at, held = [], [], 0
    for job, deep in enumerate(rows):
        held_at.append(held)
        for i in range(blocks):
            at = pl.ds(pl.multiple_of(rows_ref[job * blocks + i], 16), deep)
            for j in range(count):
                copies.append(
                    pltpu.make_async_copy(
                        lefts[j].at[at, :],
                        held_ref.at[held : held + deep, j * part : (j + 1) * part],
                        sem.at[len(copies)],
                    )
                )
            held += deep

    @pl.when(pl.program_id(0) == 0)
    def _():
        for copy in copies:
            copy.start()
        for copy in copies:
            copy.wait()

    dot = times_trans if flat else matmul
    for job, deep in enumerate(rows):
        base = held_at[job]
        for spot, pack in enumerate(packs):
            out_ref = outs[job * len(packs) + spot]
            total = None
            for j in range(count):
                term = dot(
                    held_ref[base : base + pack * deep, j * part : (j + 1) * part], rights[job * count + j][...]
                )
                total = term if total is None else total + term
            out_ref[...] = total.reshape(out_ref.shape).astype(BF)
            base += pack * deep


def weight_grad(lefts, rights, jobs, packs, wide, step, flat=False):
    count = len(lefts)
    part = lefts[0].shape[1]
    rows = tuple(job[1] for job in jobs)

    def right_spec(base):
        if flat:
            return pl.BlockSpec((step, part), lambda i, b: (i + base, 0))
        return pl.BlockSpec((part, step), lambda i, b: (0, i + base))

    outs = pl.pallas_call(
        functools.partial(weight_grad_kernel, count, flat, rows, packs),
        out_shape=tuple(shape((pack, deep, wide)) for deep in rows for pack in packs),
        grid_spec=pltpu.PrefetchScalarGridSpec(
            num_scalar_prefetch=1,
            grid=(wide // step,),
            in_specs=[ANY] * count + [right_spec(job[2]) for job in jobs for _ in range(count)],
            out_specs=tuple(
                pl.BlockSpec((pack, deep, step), lambda i, b: (0, 0, i)) for deep in rows for pack in packs
            ),
            scratch_shapes=[
                pltpu.VMEM((sum(packs) * sum(rows), part * count), BF),
                pltpu.SemaphoreType.DMA((sum(packs) * count * len(rows),)),
            ],
        ),
        compiler_params=params(dimension_semantics=("arbitrary",)),
        name="weight_grad",
    )(jnp.concatenate([job[0] for job in jobs]), *lefts, *(list(rights) * len(jobs)))
    return [outs[i * len(packs) : (i + 1) * len(packs)] for i in range(len(jobs))]


def weight_grad_seq_kernel(count, rows, order_ref, *refs):
    lefts, rights = refs[:count], refs[count : 2 * count]
    near_ref, far_ref, own_ref, held_ref, sem = refs[2 * count :]
    blocks = held_ref.shape[0] // rows
    part = lefts[0].shape[1]
    step = pl.program_id(0)
    copies = [
        pltpu.make_async_copy(
            lefts[j].at[pl.ds(pl.multiple_of(order_ref[4 + i], 16), rows), :],
            held_ref.at[i * rows : (i + 1) * rows, j * part : (j + 1) * part],
            sem.at[i * count + j],
        )
        for i in range(blocks)
        for j in range(count)
    ]

    @pl.when(step == 0)
    def _():
        for copy in copies:
            copy.start()
        for copy in copies:
            copy.wait()

    total = None
    for j in range(count):
        term = matmul(held_ref[:, j * part : (j + 1) * part], rights[j][...])
        total = term if total is None else total + term
    total = total.astype(BF)

    @pl.when(step < 2)
    def _():
        near_ref[0] = total

    @pl.when(step == 2)
    def _():
        far_ref[...] = total

    @pl.when(step == 3)
    def _():
        own_ref[...] = total


def weight_grad_seq(lefts, rights, row_starts, rows, columns, step):
    count = len(lefts)
    part = lefts[0].shape[1]
    blocks = row_starts.shape[0]
    return pl.pallas_call(
        functools.partial(weight_grad_seq_kernel, count, rows),
        out_shape=(shape((2, blocks * rows, step)), shape((blocks * rows, step)), shape((blocks * rows, step))),
        grid_spec=pltpu.PrefetchScalarGridSpec(
            num_scalar_prefetch=1,
            grid=(4,),
            in_specs=[ANY] * count + [pl.BlockSpec((part, step), lambda i, b: (0, b[i]))] * count,
            out_specs=(
                pl.BlockSpec((1, blocks * rows, step), lambda i, b: (jnp.minimum(i, 1), 0, 0)),
                pl.BlockSpec((blocks * rows, step), lambda i, b: (0, 0)),
                pl.BlockSpec((blocks * rows, step), lambda i, b: (0, 0)),
            ),
            scratch_shapes=[
                pltpu.VMEM((blocks * rows, part * count), BF),
                pltpu.SemaphoreType.DMA((blocks * count,)),
            ],
        ),
        compiler_params=params(dimension_semantics=("arbitrary",)),
        name="weight_grad_seq",
    )(jnp.concatenate([columns, row_starts]), *lefts, *rights)


def split_kernel(turned, rank_ref, keep_ref, got1_ref, got2_ref, near_ref, far_ref, own_ref):
    total = keep_ref[0].astype(F32) + got1_ref[got1_ref.shape[0] - 1].astype(F32) + got2_ref[0].astype(F32)
    total = total.astype(BF)
    if turned:
        total = jnp.transpose(total)
    size = 4
    block = total.shape[0 if turned else 1] // size
    for j in range(size):
        at = slice(j * block, (j + 1) * block)
        piece = total[at, :] if turned else total[:, at]
        mask = j ^ rank_ref[0]

        @pl.when(mask == 3)
        def _():
            near_ref[0] = piece

        @pl.when(mask == 1)
        def _():
            near_ref[1] = piece

        @pl.when(mask == 2)
        def _():
            far_ref[...] = piece

        @pl.when(mask == 0)
        def _():
            own_ref[...] = piece


def split(rank, keep, got1, got2, turned=False):
    rows, cols = keep.shape[1:]
    dims = (cols // 4, rows) if turned else (rows, cols // 4)
    return pl.pallas_call(
        functools.partial(split_kernel, turned),
        out_shape=(shape((2,) + dims), shape(dims), shape(dims)),
        in_specs=[SMEM, VMEM, VMEM, VMEM],
        out_specs=(VMEM,) * 3,
        compiler_params=params(),
        name="split",
    )(rank, keep, got1, got2)


def flip(x, axis, size, bit):
    return lax.ppermute(x, axis, [(i, i ^ bit) for i in range(size)])


def add(a, b):
    return (a.astype(F32) + b.astype(F32)).astype(BF)


def masks_of(bits):
    out = []
    for i in range(2 ** len(bits)):
        mask = 0
        for spot, bit in enumerate(bits):
            if not (i >> (len(bits) - 1 - spot)) & 1:
                mask |= bit
        out.append(mask)
    return out


def after(x, *others):
    return together(x, *others)[0]


def together(*values):
    leaves, tree = jax.tree.flatten(values)
    return jax.tree.unflatten(tree, lax.optimization_barrier(tuple(leaves)))


def exchange(blocks):
    return lax.all_to_all(blocks, "seq", split_axis=0, concat_axis=0, tiled=True)


def shards(
    tokens, modulation, image_ids, w_qkv, w_out, w_fc1, w_fc2, w_proj1, w_proj2, w_proj3, dino, cotangent,
):
    n_seq = lax.axis_size("seq")
    n_dp = lax.axis_size("dp")
    rank = lax.axis_index("seq")
    me = lax.axis_index("dp")
    tok_dev, width = tokens.shape
    group_tok = image_ids.shape[0]
    hidden, wide, narrow = w_fc1.shape[1], w_proj2.shape[0], w_proj3.shape[1]
    heads = H // n_seq
    local = heads * HD
    slots = modulation.shape[0]
    dp_bits = [1 << i for i in range(n_dp.bit_length() - 1)]
    rank_arg = rank.reshape(1).astype(jnp.int32)

    mods, *firsts = enter(image_ids, rank_arg, tokens, modulation)

    rights, lefts = [firsts], [firsts]
    for s in range(1, n_seq):
        up = [(i, i + 1) for i in range(s - 1, n_seq - 1)]
        low = [(i, i - 1) for i in range(1, n_seq - s + 1)]
        rights.append([lax.ppermute(v, "seq", up) for v in rights[-1]])
        lefts.append([lax.ppermute(v, "seq", low) for v in lefts[-1]])
    pieces = list(firsts)
    for d in range(1, n_seq):
        pieces += lefts[d] + rights[n_seq - d]

    columns = [lax.dynamic_slice_in_dim(w_qkv, i * width + rank * local, local, 1) for i in range(3)]
    w_rows = jnp.transpose(jnp.concatenate(columns, axis=1))
    w_pad = jnp.pad(w_rows.reshape(3 * heads, HD, width), ((0, 0), (0, HP - HD), (0, 0))).reshape(3 * heads * HP, width)
    ids_rel = lax.dynamic_slice_in_dim(jnp.concatenate([image_ids, image_ids]), rank * tok_dev, group_tok)
    idk, idq = ids_rel[:, None], ids_rel[None, :]
    one = (image_ids[0] == image_ids[group_tok - 1]).astype(jnp.int32).reshape(1)
    tile = group_tok // 4
    diagonal = tok_dev % tile == 0

    *heads_out, first_all, qkv, lse = attend_forward(
        one, rank_arg, pieces, w_pad, idk, idq, heads, tile, diagonal
    )
    attended = [heads_out[0]]
    for d in range(1, n_seq):
        attended.append(lax.ppermute(heads_out[d], "seq", [(i, (i + d) % n_seq) for i in range(n_seq)]))
    (rounded, act1, dr2, left1, right1, left2, gelu_slope, dmlp, dy, normed2, inv2, attn, sum_gate2) = middle(
        rank_arg, attended, tokens, mods, dino, cotangent, w_out, w_fc1, w_fc2, w_proj1, w_proj2, w_proj3
    )

    fast = all(k % (16 * n_dp) == 0 for k in (width, hidden, wide)) and n_dp == 8 and n_seq == 4

    def down(dmlp):
        return descend(n_seq, dmlp, gelu_slope, dy, normed2, inv2, attn, mods, w_fc2, w_fc1, w_out)

    def back(dos):
        return attend_backward(
            one, rank_arg, dos, qkv, heads_out, lse, w_rows, idk, idq, heads, tile, diagonal
        )

    def outgoing(g_heads, sums1):
        units = [g_heads[:, i * local : (i + 1) * local] for i in range(3)]
        rows = jnp.concatenate([sums1[0:2], sums2[0:3], sum_gate2], axis=0).astype(BF)
        rows = rows.reshape(n_seq, 6 * width // (n_seq * local), local)
        blocks = []
        for target in range(n_seq):
            mine = jnp.zeros_like(units[0])
            for i in range(3):
                mine = jnp.where((n_seq * i + rank) // 3 == target, units[i], mine)
            blocks.append(jnp.concatenate([mine, rows[target]], axis=0))
        return jnp.stack(blocks)

    if fast:
        swap = lambda x, bit: flip(x, "dp", n_dp, bit)
        core, x, y = dp_bits
        near = lambda v: flip(v, "seq", n_seq, 1)
        far = lambda v: flip(v, "seq", n_seq, 2)

        def job(base, deep, bits, column):
            starts = base + (me ^ jnp.array(masks_of(bits), jnp.int32)) * (deep // n_dp)
            return (starts, deep // n_dp, column)

        def right(v, step):
            return lax.ppermute(v, "seq", [(i, i + 1) for i in range(step)])

        def left(v, step):
            return lax.ppermute(v, "seq", [(i, i - 1) for i in range(n_seq - step, n_seq)])

        def row_starts(base, deep, bits):
            return base + (me ^ jnp.array(masks_of(bits), jnp.int32)) * (deep // n_dp)

        def row_starts(base, deep, bits):
            return base + (me ^ jnp.array(masks_of(bits), jnp.int32)) * (deep // n_dp)

        def last(*terms):
            return sum(v.astype(F32) for v in terms)

        quarter = (1, 1, 1, 1)
        lefts2, dmlps = [left2, swap(left2, core)], [dmlp, swap(dmlp, core)]
        act1_other, dr2_other = swap(act1, core), swap(dr2, core)
        right2, dhidden1, dheads, sums2 = down(dmlp)
        act1_other, dr2_other, lefts2, dmlps, left1, right1, right2, dheads = together(
            act1_other, dr2_other, lefts2, dmlps, left1, right1, right2, dheads
        )

        dheads_in = exchange(dheads)
        lefts1, rights1 = [left1, swap(left1, core)], [right1, swap(right1, core)]
        rights2 = [right2, swap(right2, core)]
        (p2,) = weight_grad([act1, act1_other], [dr2, dr2_other], [job(0, wide, (x, y), 0)], quarter, wide, STEP)
        (f2,) = weight_grad(lefts2, after(dmlps, p2), [job(0, hidden, (y, x), 0)], quarter, width, 384)
        p2, f2, lefts2, lefts1, rights1, rights2 = together(p2, f2, lefts2, lefts1, rights1, rights2)

        p2a, p2b, f2a = swap(p2[0], x), swap(p2[1], x), swap(f2[0], y)
        p1n, p1f, p1o = weight_grad_seq(
            lefts1, rights1, row_starts(wide, width, (y, x)), width // n_dp,
            rank ^ jnp.array(masks_of((1, 2)), jnp.int32), wide // n_seq,
        )
        p1z = near(p1n)
        (p3,) = weight_grad(
            lefts1, after(rights1, p1n, dheads_in), [job(0, wide, (y, x), wide // 256)], (2, 1, 1), narrow, 256
        )
        p3a = swap(p3[0], y)
        dqkv, dx = back(after(dheads_in, p3, p2a))
        f2s = add(f2[2], after(f2a, dqkv))
        p2, f2, p2a, p2b, f2s, p1f, p1o, p1z, p3, p3a, rights2, dqkv, dx = together(
            p2, f2, p2a, p2b, f2s, p1f, p1o, p1z, p3, p3a, rights2, dqkv, dx
        )

        f2c, f2b = swap(f2s, x), swap(f2[1], y)
        up, low = right(dx[3], 1), left(dx[1], 1)
        (f1,) = weight_grad(lefts2, rights2, [job(hidden, width, (x, y), 0)], quarter, hidden, 1152)
        p1y = far(add(p1f, p1z[0]))
        (fq,) = weight_grad(
            [first_all], [after(dqkv, f1)], [job(0, width, (core, y, x), 0)], (4, 2, 2), 3 * local, 3 * local,
            flat=True,
        )
        (fo,) = weight_grad(
            lefts2, after(rights2, fq), [job(hidden + width, width, (y, x), hidden // 384)], (2, 1, 1), width, 384
        )
        p2s, p3s, p1o = add(p2[2], p2a), add(p3[1], p3a[:1]), add(p1o, p1z[1])
        f2, f2c, f2b, up, low, p1y, p3s, f1, fq, fo, p2s, p1o = together(
            f2, f2c, f2b, up, low, p1y, p3s, f1, fq, fo, p2s, p1o
        )

        f1a, p2c = swap(f1[0], x), swap(p2s, y)
        up, low = right(add(dx[2], up), 2), left(add(dx[2], low), 2)
        fqa = swap(fq[0], core)
        f2n, f2f, f2o = split(rank_arg, after(f2[3], fqa), f2b, f2c, turned=True)
        f2z = near(f2n)
        p3c = swap(after(p3s, f2n), x)
        foa = swap(after(fo[0], p2c), y)
        p1d = add(p1o, p1y).reshape(4, width // n_dp, wide // n_seq)
        p2n, p2f, p2o = split(rank_arg, p2[3], p2b, p2c)
        f1s = add(f1[2], f1a)
        f1s, foa, fqa, p3c, p2n, p2f, p1d, f2z, f2f, up, low, f1 = together(
            f1s, foa, fqa, p3c, p2n, p2f, p1d, f2z, f2f, up, low, f1
        )

        f1b, f1c = swap(f1[1], x), swap(f1s, y)
        up, low = right(add(dx[1], up), 3), left(add(dx[3], low), 3)
        f2y = far(add(f2f, f2z[0]))
        p3n, p3f, p3o = split(rank_arg, p3[2], p3a, p3c, turned=True)
        p2z, foc = near(after(p2n, up, low)), swap(add(fo[1], after(foa, up, low)[:1]), x)
        fqb, fqk = swap(add(fq[1], after(fqa, up, low)[:2]), y), add(fq[2], fqa[2:])
        f1b, f1c, up, low, f2y, p2z, p2f, p3n, foc, fqb, fqk, p1d = together(
            f1b, f1c, up, low, f2y, p2z, p2f, p3n, foc, fqb, fqk, p1d
        )

        fqs, fqk = add(fqk[0], fqb[0]), add(fqk[1], fqb[1])
        fqc, p1e = swap(fqs, x), swap(p1d[0:2], y)
        p2y, p3z = far(add(p2f, p2z[0])), near(p3n)
        f1n, f1f, f1o = split(rank_arg, f1[3], f1b, f1c)
        f1z = near(f1n)
        fon, fof, foo = split(rank_arg, after(fo[2], f1n), foa, foc)
        foz = near(fon)
        grad_inputs, sums1 = leave(after(dx[0], fon), up, low, tokens, dhidden1, mods)
        fqk, fqc, p1e, f1z, f1f, p2y, p3z, foz, fof, sums1 = together(
            fqk, fqc, p1e, f1z, f1f, p2y, p3z, foz, fof, sums1
        )

        g_heads = add(fqk, fqc)
        incoming = exchange(outgoing(g_heads, sums1))
        f1y, p3y, foy = far(add(f1f, f1z[0])), far(add(p3f, p3z[0])), far(add(fof, foz[0]))
        p1x = swap(add(p1d[2], p1e[0]), x)
        g_proj1 = last(p1d[3], p1e[1], p1x)
        g_proj2, g_fc1, g_fc2 = last(p2o, p2z[1], p2y), last(f1o, f1z[1], f1y), jnp.transpose(last(f2o, f2z[1], f2y))
        g_proj3, g_out = jnp.transpose(last(p3o, p3z[1], p3y)), last(foo, foz[1], foy)
    else:
        right2, dhidden1, dheads, sums2 = down(dmlp)
        dqkv, dx = back(exchange(dheads))
        up, low = None, None
        for s in range(1, n_seq):
            up = dx[n_seq - s] if up is None else add(dx[n_seq - s], up)
            low = dx[s] if low is None else add(dx[s], low)
            up = lax.ppermute(up, "seq", [(i, i + 1) for i in range(s)])
            low = lax.ppermute(low, "seq", [(i, i - 1) for i in range(n_seq - s, n_seq)])
        grad_inputs, sums1 = leave(dx[0], up, low, tokens, dhidden1, mods)

        def reduced(a, b):
            share = lax.psum_scatter(matmul(a, b).astype(BF), "dp", scatter_dimension=0, tiled=True)
            return lax.psum_scatter(share, "seq", scatter_dimension=1, tiled=True).astype(F32)

        g_proj3 = reduced(left1[:wide], right1[:, wide:])
        g_proj2 = reduced(act1, dr2)
        g_proj1 = reduced(left1[wide:], right1[:, :wide])
        g_fc2 = reduced(left2[:hidden], dmlp)
        g_fc1 = reduced(left2[hidden : hidden + width], right2[:, :hidden])
        g_out = reduced(left2[hidden + width :], right2[:, hidden:])
        g_heads = lax.psum_scatter(
            times_trans(first_all, dqkv).astype(BF), "dp", scatter_dimension=0, tiled=True
        )

    if not fast:
        incoming = exchange(outgoing(g_heads, sums1))
    held = g_heads.shape[0]
    slot = jnp.arange(slots, dtype=jnp.int32)[:, None, None]
    whose = image_ids[::tok_dev]
    dmods = incoming[:, held:].reshape(n_seq, 6 * width // n_seq).astype(F32)
    grad_mods = jnp.sum(jnp.where(slot == whose[None, :, None], dmods[None], 0.0), axis=1)
    incoming = incoming[:, :held]
    columns = [jnp.zeros(incoming.shape[1:], BF) for _ in range(3)]
    for source in range(n_seq):
        for i in range(3):
            unit = n_seq * i + source
            columns[unit % 3] = jnp.where(unit // 3 == rank, incoming[source], columns[unit % 3])
    g_qkv = jnp.concatenate(columns, axis=1).astype(F32)

    return (rounded, grad_inputs, grad_mods, g_qkv, g_out, g_fc1, g_fc2, g_proj1, g_proj2, g_proj3)


def solution(mesh):
    tok = P(("dp", "seq"), None)
    in_specs = (tok, P("dp", None), P("dp")) + (P(),) * 7 + (tok, tok)
    out_specs = (tok, tok) + (P("dp", "seq"),) * 8
    return jax.shard_map(shards, mesh=mesh, in_specs=in_specs, out_specs=out_specs, check_vma=False)
```

```python
import functools

import jax
import jax.numpy as jnp
from jax import lax
from jax.experimental import pallas as pl
from jax.experimental.pallas import tpu as pltpu
from jax.sharding import PartitionSpec as P

H = 16
HD = 72
HP = 80
LEN = 1024
EPS_NORM = 1e-06
SCALE = HD ** (-0.5)
EXP2_SCALE = SCALE * 1.4426950408889634
GELU_A = 0.7978845608028654
GELU_B = 0.044715
BF = jnp.bfloat16
F32 = jnp.float32
ANY = pl.BlockSpec(memory_space=pl.ANY)
VMEM = pl.BlockSpec(memory_space=pltpu.VMEM)
SMEM = pl.BlockSpec(memory_space=pltpu.SMEM)
ROOM = 60 << 20
PARTS = 2


def matmul(left, right):
    return jnp.dot(left, right, preferred_element_type=F32)


def times_trans(left, right):
    return lax.dot_general(left, right, (((1,), (1,)), ((), ())), preferred_element_type=F32)


def trans_times(left, right):
    return lax.dot_general(left, right, (((0,), (0,)), ((), ())), preferred_element_type=F32)


def row_mean(v):
    return jnp.mean(v, axis=-1, keepdims=True)


def normalize(v):
    centre = v - row_mean(v)
    inv = lax.rsqrt(row_mean(centre * centre) + EPS_NORM)
    return centre * inv, inv


def norm_back(e, normed, inv):
    return (e - row_mean(e) - normed * row_mean(e * normed)) * inv


def col_sum(v):
    return jnp.sum(v, axis=0, keepdims=True)


def sigmoid(v):
    return 1.0 / (1.0 + jnp.exp(-v))


def shape(dims, kind=BF):
    return jax.ShapeDtypeStruct(dims, kind)


def params(**more):
    return pltpu.CompilerParams(vmem_limit_bytes=ROOM, **more)


def enter_kernel(ids_ref, rank_ref, tokens_ref, mod_ref, mods_ref, *out_refs):
    width = tokens_ref.shape[1]
    table = mod_ref[...].astype(F32)
    mine = lax.broadcasted_iota(jnp.int32, table.shape, 0) == ids_ref[rank_ref[0] * tokens_ref.shape[0]]
    mods = col_sum(jnp.where(mine, table, 0.0))
    mods_ref[...] = jnp.zeros_like(mods_ref)
    for i in range(6):
        mods_ref[i : i + 1, :] = mods[:, i * width : (i + 1) * width]
    normed, _ = normalize(tokens_ref[...].astype(F32))
    first = normed * (1.0 + mods[:, width : 2 * width]) + mods[:, 0:width]
    first = jnp.transpose(first.astype(BF))
    rows = out_refs[0].shape[0]
    for i, out_ref in enumerate(out_refs):
        out_ref[...] = first[i * rows : (i + 1) * rows, :]


def enter(ids, rank, tokens, modulation):
    tok, width = tokens.shape
    return pl.pallas_call(
        enter_kernel,
        out_shape=(shape((8, width), F32),) + (shape((width // PARTS, tok)),) * PARTS,
        in_specs=[SMEM, SMEM, VMEM, VMEM],
        out_specs=(VMEM,) * (1 + PARTS),
        compiler_params=params(),
        name="enter",
    )(ids, rank, tokens, modulation)


def attend_forward_kernel(size, heads, tile, diagonal, one_ref, rank_ref, *refs):
    count = PARTS * (2 * size - 1)
    pieces = refs[:count]
    w_any, idk_ref, idq_ref = refs[count : count + 3]
    o_refs = refs[count + 3 : count + 3 + size]
    (x_any, qkv_any, lse_ref, x_ref, qkv_ref, w_ref, k_ref, o_all_ref, sem, w_sem, out_sem) = refs[count + 3 + size :]
    tok = pieces[0].shape[1]
    total = x_ref.shape[1]
    rows = pieces[0].shape[0]
    rank = rank_ref[0]
    w_copy = pltpu.make_async_copy(w_any, w_ref, w_sem.at[0])
    w_copy.start()

    def piece_copy(d, part, source):
        at = 0 if d == 0 else 2 * d - 2 + source
        return pltpu.make_async_copy(
            pieces[at * PARTS + part],
            x_ref.at[part * rows : (part + 1) * rows, d * tok : (d + 1) * tok],
            sem.at[d, part],
        )

    for part in range(PARTS):
        piece_copy(0, part, 0).start()
    for d in range(1, size):
        for part in range(PARTS):

            @pl.when(rank + d < size)
            def _():
                piece_copy(d, part, 1).start()

            @pl.when(rank + d >= size)
            def _():
                piece_copy(d, part, 2).start()

    w_copy.wait()
    for d in range(size):
        for part in range(PARTS):
            piece_copy(d, part, 1).wait()
        at = slice(d * tok, (d + 1) * tok)
        qkv_ref[:, at] = matmul(w_ref[...], x_ref[:, at]).astype(BF)
    out_copies = [
        pltpu.make_async_copy(x_ref, x_any, out_sem.at[0]),
        pltpu.make_async_copy(qkv_ref, qkv_any, out_sem.at[1]),
    ]
    for copy in out_copies:
        copy.start()

    def head_step(head, carry):
        q_at = pl.ds(pl.multiple_of(head * HP, HP), HP)
        k_at = pl.ds(pl.multiple_of((heads + head) * HP, HP), HP)
        v_at = pl.ds(pl.multiple_of((2 * heads + head) * HP, HP), HP)
        o_at = pl.ds(pl.multiple_of(head * HD, 8), HD)
        k_ref[...] = jnp.transpose(qkv_ref[k_at, :])

        def block(at, keys, masked):
            s = matmul(k_ref[keys, :], qkv_ref[q_at, at]) * EXP2_SCALE
            if masked:
                s = jnp.where(idk_ref[...] == idq_ref[:, at], s, -1e30)
            top = jnp.max(s, axis=0, keepdims=True)
            e = jnp.exp2(s - top)
            tot = col_sum(e)
            o = matmul(qkv_ref[v_at, keys], e.astype(BF)) * (1.0 / tot)
            o_all_ref[o_at, at] = o[0:HD, :]
            lse_ref[pl.ds(head, 1), at] = top + jnp.log2(tot)

        def full(masked):
            def step(i, inner):
                block(pl.ds(pl.multiple_of(i * tile, tile), tile), pl.ds(0, total), masked)
                return inner

            lax.fori_loop(0, total // tile, step, 0, unroll=True)

        @pl.when(one_ref[0] == 1)
        def _():
            full(False)

        @pl.when(one_ref[0] == 0)
        def _():
            if diagonal:

                def step(i, inner):
                    at = pl.ds(pl.multiple_of(i * tile, tile), tile)
                    block(at, at, False)
                    return inner

                lax.fori_loop(0, total // tile, step, 0, unroll=True)
            else:
                full(True)

        return carry

    lax.fori_loop(0, heads, head_step, 0)
    for d in range(size):
        o_refs[d][...] = o_all_ref[:, d * tok : (d + 1) * tok].astype(BF)
    for copy in out_copies:
        copy.wait()


def attend_forward(one, rank, pieces, w, idk, idq, heads, tile, diagonal):
    size = (len(pieces) // PARTS + 1) // 2
    tok = pieces[0].shape[1]
    width, total = PARTS * pieces[0].shape[0], size * tok
    return pl.pallas_call(
        functools.partial(attend_forward_kernel, size, heads, tile, diagonal),
        out_shape=(shape((heads * HD, tok)),) * size
        + (
            shape((width, total)),
            shape((3 * heads * HP, total)),
            shape((heads, total), F32),
        ),
        in_specs=[SMEM, SMEM] + [ANY] * (len(pieces) + 1) + [VMEM, VMEM],
        out_specs=(VMEM,) * size + (ANY, ANY, VMEM),
        scratch_shapes=[
            pltpu.VMEM((width, total), BF),
            pltpu.VMEM((3 * heads * HP, total), BF),
            pltpu.VMEM(w.shape, BF),
            pltpu.VMEM((total, HP), BF),
            pltpu.VMEM((heads * HD, total), F32),
            pltpu.SemaphoreType.DMA((size, PARTS)),
            pltpu.SemaphoreType.DMA((1,)),
            pltpu.SemaphoreType.DMA((2,)),
        ],
        compiler_params=params(),
        name="attend_forward",
    )(one, rank, *pieces, w, idk, idq)


def attend_backward_kernel(size, heads, tile, diagonal, one_ref, rank_ref, *refs):
    o_refs, refs = refs[:size], refs[size:]
    dos_ref, qkv_ref, lse_ref, w_ref, idk_ref, idq_ref = refs[:6]
    dqkv_ref, dx_ref, k_ref, v_ref, do_ref, dk_ref, dv_ref, acc_ref, delta_ref = refs[6:]
    tok = dos_ref.shape[2]
    total = qkv_ref.shape[1]
    local = heads * HD
    for d in range(size):
        at = slice(d * tok, (d + 1) * tok)
        owner = lax.rem(rank_ref[0] + d, size)
        do = dos_ref[owner].astype(F32)
        do_ref[0:local, at] = do
        do_ref[local : local + HP - HD, at] = jnp.zeros((HP - HD, tok), F32)
        prod = do * o_refs[d][...].astype(F32)
        for head in range(heads):
            delta_ref[head : head + 1, at] = col_sum(prod[head * HD : (head + 1) * HD, :])

    def head_step(head, carry):
        q_at = pl.ds(pl.multiple_of(head * HP, HP), HP)
        k_at = pl.ds(pl.multiple_of((heads + head) * HP, HP), HP)
        v_at = pl.ds(pl.multiple_of((2 * heads + head) * HP, HP), HP)
        o_at = pl.ds(pl.multiple_of(head * HD, 8), HP)
        k_ref[...] = jnp.transpose(qkv_ref[k_at, :])
        v_ref[...] = jnp.transpose(qkv_ref[v_at, :])

        def out_at(part):
            return pl.ds(pl.multiple_of(part * local + head * HD, 8), HD)

        def block(at, keys, masked, fresh):
            q = qkv_ref[q_at, at]
            do = do_ref[o_at, at].astype(BF)
            p = jnp.exp2(matmul(k_ref[keys, :], q) * EXP2_SCALE - lse_ref[pl.ds(head, 1), at])
            if masked:
                p = jnp.where(idk_ref[...] == idq_ref[:, at], p, 0.0)
            ds = (p * (matmul(v_ref[keys, :], do) - delta_ref[pl.ds(head, 1), at])).astype(BF)
            dv = times_trans(do, p.astype(BF))
            dk = times_trans(q, ds)
            if fresh:
                dv_ref[:, keys] = dv
                dk_ref[:, keys] = dk
            else:
                dv_ref[:, keys] += dv
                dk_ref[:, keys] += dk
            dq = matmul(qkv_ref[k_at, keys], ds) * SCALE
            acc_ref[out_at(0), at] = dq[0:HD, :]

        def full(masked):
            dk_ref[...] = jnp.zeros_like(dk_ref)
            dv_ref[...] = jnp.zeros_like(dv_ref)

            def step(i, inner):
                block(pl.ds(pl.multiple_of(i * tile, tile), tile), pl.ds(0, total), masked, False)
                return inner

            lax.fori_loop(0, total // tile, step, 0, unroll=True)

        @pl.when(one_ref[0] == 1)
        def _():
            full(False)

        @pl.when(one_ref[0] == 0)
        def _():
            if diagonal:

                def step(i, inner):
                    at = pl.ds(pl.multiple_of(i * tile, tile), tile)
                    block(at, at, False, True)
                    return inner

                lax.fori_loop(0, total // tile, step, 0, unroll=True)
            else:
                full(True)

        acc_ref[out_at(1), :] = dk_ref[0:HD, :] * SCALE
        acc_ref[out_at(2), :] = dv_ref[0:HD, :]
        return carry

    lax.fori_loop(0, heads, head_step, 0)
    dqkv_ref[...] = acc_ref[...].astype(BF)
    for d in range(size):
        dx_ref[d] = trans_times(dqkv_ref[:, d * tok : (d + 1) * tok], w_ref[...]).astype(BF)


def attend_backward(one, rank, dos, qkv, o, lse, w, idk, idq, heads, tile, diagonal):
    size, local, tok = dos.shape
    total = size * tok
    width = w.shape[1]
    return pl.pallas_call(
        functools.partial(attend_backward_kernel, size, heads, tile, diagonal),
        out_shape=(shape((3 * local, total)), shape((size, tok, width))),
        in_specs=[SMEM, SMEM] + [VMEM] * (size + 6),
        out_specs=(VMEM, VMEM),
        scratch_shapes=[
            pltpu.VMEM((total, HP), BF),
            pltpu.VMEM((total, HP), BF),
            pltpu.VMEM((local + HP - HD, total), F32),
            pltpu.VMEM((HP, total), F32),
            pltpu.VMEM((HP, total), F32),
            pltpu.VMEM((3 * local, total), F32),
            pltpu.VMEM((heads, total), F32),
        ],
        compiler_params=params(),
        name="attend_backward",
    )(one, rank, *o, dos, qkv, lse, w, idk, idq)


STEP = 512


def middle_kernel(size, rank_ref, *refs):
    o_refs, refs = refs[:size], refs[size:]
    (tokens_ref, mods_ref, dino_ref, cot_ref, wo_any, w1_any, w2_any, p1_any, p2_any, p3_any) = refs[:10]
    (out_any, a1_any, dr2_any, left1_any, right1_ref, left2_any, gp_any, dmlp_ref, dy_ref, normed_any, inv_ref, attn_any,
     gate_ref) = refs[10:23]
    (wo_ref, w1_ref, w2_ref, p1_ref, p2_ref, p3_ref, act_ref, out_ref, a1_ref, dr2_ref, left1_ref, left2_ref, gp_ref,
     normed_ref, attn_ref, w1_sem, sems, out_sems) = refs[23:]
    flushes = []

    def flush(source, target):
        copy = pltpu.make_async_copy(source, target, out_sems.at[len(flushes)])
        copy.start()
        flushes.append(copy)

    local, tok = o_refs[0].shape
    width = size * local
    hidden = w1_any.shape[1]
    wide, narrow = p3_ref.shape
    steps = hidden // STEP
    slots = w1_ref.shape[0]
    a2_ref, y_ref = left1_ref.at[0:wide, :], left1_ref.at[wide:, :]
    g_ref, b_ref = left2_ref.at[0:hidden, :], left2_ref.at[hidden : hidden + width, :]
    o_ref = left2_ref.at[hidden + width :, :]
    dr1_ref, dz_ref = right1_ref.at[:, 0:wide], right1_ref.at[:, wide:]
    wo_copy = pltpu.make_async_copy(wo_any, wo_ref, sems.at[4])
    wo_copy.start()

    def w1_copy(i):
        at = pl.ds(pl.multiple_of(i * STEP, STEP), STEP)
        slot = lax.rem(i, slots)
        return pltpu.make_async_copy(w1_any.at[:, at], w1_ref.at[slot], w1_sem.at[slot])

    for i in range(slots):
        w1_copy(i).start()
    w2_copy = pltpu.make_async_copy(w2_any, w2_ref, sems.at[0])
    p1_copy = pltpu.make_async_copy(p1_any, p1_ref, sems.at[1])
    p2_copy = pltpu.make_async_copy(p2_any, p2_ref, sems.at[2])
    p3_copy = pltpu.make_async_copy(p3_any, p3_ref, sems.at[3])
    for copy in (w2_copy, p1_copy, p2_copy, p3_copy):
        copy.start()

    gate1, shift2, scale2, gate2 = [mods_ref[i : i + 1, :] for i in (2, 3, 4, 5)]
    for d in range(size):
        owner = lax.rem(rank_ref[0] + size - d, size)
        o_ref[pl.ds(pl.multiple_of(owner * local, 16), local), :] = o_refs[d][...]
    wo_copy.wait()
    attn = trans_times(o_ref[...], wo_ref[...])
    attn_ref[...] = attn
    flush(attn_ref, attn_any)
    h1 = tokens_ref[...].astype(F32) + gate1 * attn
    normed, inv = normalize(h1)
    normed_ref[...] = normed
    flush(normed_ref, normed_any)
    inv_ref[...] = inv
    b = (normed * (1.0 + scale2) + shift2).astype(BF)
    b_ref[...] = jnp.transpose(b)

    def up(i, carry):
        at = pl.ds(pl.multiple_of(i * STEP, STEP), STEP)
        w1_copy(i).wait()
        u = matmul(b, w1_ref[lax.rem(i, slots)])

        @pl.when(i + slots < steps)
        def _():
            w1_copy(i + slots).start()

        sq = u * u
        t = jnp.tanh(u * (GELU_A + (GELU_A * GELU_B) * sq))
        half = 0.5 * (1.0 + t)
        g = (u * half).astype(BF)
        gp_ref[:, at] = (half + u * (1.0 - t * t) * (0.5 * GELU_A + (1.5 * GELU_A * GELU_B) * sq)).astype(BF)
        act_ref[:, at] = g
        g_ref[at, :] = jnp.transpose(g)
        return carry

    lax.fori_loop(0, steps, up, 0, unroll=True)
    flush(left2_ref, left2_any)
    flush(gp_ref, gp_any)
    w2_copy.wait()
    mlp = matmul(act_ref[...], w2_ref[...])
    y = (h1 + gate2 * mlp).astype(BF)
    out_ref[...] = y
    flush(out_ref, out_any)
    y_ref[...] = jnp.transpose(y)
    def project(source, w_ref, held, out_t_ref, slope_ref):
        def step(i, carry):
            at = pl.ds(pl.multiple_of(i * STEP, STEP), STEP)
            r = matmul(source, w_ref[:, at])
            sig = sigmoid(r)
            act = (r * sig).astype(BF)
            act_ref[:, pl.ds(pl.multiple_of(held + i * STEP, STEP), STEP)] = act
            out_t_ref[at, :] = jnp.transpose(act)
            slope_ref[:, at] = (sig * (1.0 + r * (1.0 - sig))).astype(BF)
            return carry

        lax.fori_loop(0, wide // STEP, step, 0, unroll=True)
        return act_ref[:, held : held + wide]

    def project_back(source, w_ref, slope_ref):
        def step(i, carry):
            at = pl.ds(pl.multiple_of(i * STEP, STEP), STEP)
            slope_ref[:, at] = (times_trans(source, w_ref[at, :]) * slope_ref[:, at].astype(F32)).astype(BF)
            return carry

        lax.fori_loop(0, wide // STEP, step, 0, unroll=True)
        return slope_ref[...]

    p1_copy.wait()
    a1 = project(y, p1_ref, 0, a1_ref, dr1_ref)
    flush(a1_ref, a1_any)
    p2_copy.wait()
    a2 = project(a1, p2_ref, wide, a2_ref, dr2_ref)
    flush(left1_ref, left1_any)
    p3_copy.wait()
    z = matmul(a2, p3_ref[...])
    t = dino_ref[...].astype(F32)
    nz = lax.rsqrt(jnp.sum(z * z, axis=-1, keepdims=True) + EPS_NORM)
    nt = lax.rsqrt(jnp.sum(t * t, axis=-1, keepdims=True) + EPS_NORM)
    cosine = jnp.sum(z * t, axis=-1, keepdims=True) * nz * nt
    dz = (-0.5 * (t * (nz * nt) - (cosine * nz * nz) * z)).astype(BF)
    dz_ref[...] = dz
    dr2 = project_back(dz, p3_ref, dr2_ref)
    flush(dr2_ref, dr2_any)
    dr1 = project_back(dr2, p2_ref, dr1_ref)
    dy = cot_ref[...].astype(F32) + times_trans(dr1, p1_ref[...])
    dy_ref[...] = dy
    dmlp_ref[...] = (gate2 * dy).astype(BF)
    gate_ref[...] = col_sum(dy * mlp)
    for copy in flushes:
        copy.wait()


def middle(rank, os, tokens, mods, dino, cot, wo, w1, w2, p1, p2, p3):
    tok, width = tokens.shape
    hidden, wide, narrow = w1.shape[1], p1.shape[1], p3.shape[1]
    return pl.pallas_call(
        functools.partial(middle_kernel, len(os)),
        out_shape=(
            shape((tok, width)), shape((wide, tok)), shape((tok, wide)), shape((wide + width, tok)),
            shape((tok, wide + narrow)), shape((hidden + 2 * width, tok)), shape((tok, hidden)), shape((tok, width)), shape((tok, width), F32),
            shape((tok, width), F32), shape((tok, 1), F32), shape((tok, width), F32), shape((1, width), F32),
        ),
        in_specs=[SMEM] + [VMEM] * (len(os) + 4) + [ANY] * 6,
        out_specs=(ANY, ANY, ANY, ANY, VMEM, ANY, ANY, VMEM, VMEM, ANY, VMEM, ANY, VMEM),
        scratch_shapes=[
            pltpu.VMEM(dims, BF)
            for dims in (wo.shape, (4, width, STEP), w2.shape, p1.shape, p2.shape, p3.shape, (tok, hidden))
        ]
        + [
            pltpu.VMEM(dims, kind)
            for dims, kind in (
                ((tok, width), BF), ((wide, tok), BF), ((tok, wide), BF), ((wide + width, tok), BF),
                ((hidden + 2 * width, tok), BF), ((tok, hidden), BF), ((tok, width), F32), ((tok, width), F32),
            )
        ]
        + [pltpu.SemaphoreType.DMA((4,)), pltpu.SemaphoreType.DMA((5,)), pltpu.SemaphoreType.DMA((8,))],
        compiler_params=params(),
        name="middle",
    )(rank, *os, tokens, mods, dino, cot, wo, w1, w2, p1, p2, p3)


def descend_kernel(size, *refs):
    (dmlp_ref, gp_any, dy_any, normed_any, inv_ref, attn_any, mods_ref, w2_any, w1_any, wo_any) = refs[:10]
    (right2_ref, dh1_ref, do_ref, sums_ref) = refs[10:14]
    (w2_ref, w1_ref, wo_ref, gp_ref, dy_ref, normed_ref, attn_ref, w2_sem, w1_sem, wo_sem, in_sem) = refs[14:]
    hidden = w1_ref.shape[1]
    du_ref, dattn_ref = right2_ref.at[:, 0:hidden], right2_ref.at[:, hidden:]
    local = do_ref.shape[1]
    steps = hidden // STEP

    def w2_copy(i):
        at = pl.ds(pl.multiple_of(i * STEP, STEP), STEP)
        return pltpu.make_async_copy(w2_any.at[at, :], w2_ref.at[at, :], w2_sem.at[i])

    in_copies = [
        pltpu.make_async_copy(source, held, in_sem.at[i])
        for i, (source, held) in enumerate(
            ((gp_any, gp_ref), (dy_any, dy_ref), (normed_any, normed_ref), (attn_any, attn_ref))
        )
    ]
    in_copies[0].start()
    for i in range(steps):
        w2_copy(i).start()
    w1_copy = pltpu.make_async_copy(w1_any, w1_ref, w1_sem.at[0])
    w1_copy.start()
    wo_copy = pltpu.make_async_copy(wo_any, wo_ref, wo_sem.at[0])
    wo_copy.start()
    for copy in in_copies[1:]:
        copy.start()
    in_copies[0].wait()
    dmlp = dmlp_ref[...]

    def down(i, carry):
        at = pl.ds(pl.multiple_of(i * STEP, STEP), STEP)
        w2_copy(i).wait()
        du_ref[:, at] = (times_trans(dmlp, w2_ref[at, :]) * gp_ref[:, at].astype(F32)).astype(BF)
        return carry

    lax.fori_loop(0, steps, down, 0, unroll=True)
    w1_copy.wait()
    for copy in in_copies[1:]:
        copy.wait()
    db = times_trans(du_ref[...], w1_ref[...])
    gate1, scale2 = mods_ref[2:3, :], mods_ref[4:5, :]
    normed = normed_ref[...]
    dh1 = dy_ref[...] + norm_back(db * (1.0 + scale2), normed, inv_ref[...])
    dh1_ref[...] = dh1
    dattn = (gate1 * dh1).astype(BF)
    dattn_ref[...] = dattn
    sums_ref[...] = jnp.zeros_like(sums_ref)
    sums_ref[0:1, :] = col_sum(dh1 * attn_ref[...])
    sums_ref[1:2, :] = col_sum(db)
    sums_ref[2:3, :] = col_sum(db * normed)
    wo_copy.wait()
    for d in range(size):
        do_ref[d] = times_trans(wo_ref[d * local : (d + 1) * local, :], dattn).astype(BF)


def descend(size, dmlp, gp, dy, normed, inv, attn, mods, w2, w1, wo):
    tok, width = dmlp.shape
    hidden = w1.shape[1]
    return pl.pallas_call(
        functools.partial(descend_kernel, size),
        out_shape=(
            shape((tok, hidden + width)), shape((tok, width), F32),
            shape((size, width // size, tok)), shape((8, width), F32),
        ),
        in_specs=[VMEM, ANY, ANY, ANY, VMEM, ANY, VMEM] + [ANY] * 3,
        out_specs=(VMEM,) * 4,
        scratch_shapes=[pltpu.VMEM(w.shape, BF) for w in (w2, w1, wo, gp)]
        + [pltpu.VMEM(v.shape, F32) for v in (dy, normed, attn)]
        + [
            pltpu.SemaphoreType.DMA((hidden // STEP,)),
            pltpu.SemaphoreType.DMA((1,)),
            pltpu.SemaphoreType.DMA((1,)),
            pltpu.SemaphoreType.DMA((4,)),
        ],
        compiler_params=params(),
        name="descend",
    )(dmlp, gp, dy, normed, inv, attn, mods, w2, w1, wo)


def leave_kernel(part_ref, left_ref, right_ref, tokens_ref, dh1_ref, mods_ref, out_ref, sums_ref):
    da = part_ref[...].astype(F32) + left_ref[...].astype(F32) + right_ref[...].astype(F32)
    normed, inv = normalize(tokens_ref[...].astype(F32))
    out_ref[...] = (dh1_ref[...] + norm_back(da * (1.0 + mods_ref[1:2, :]), normed, inv)).astype(BF)
    sums_ref[...] = jnp.zeros_like(sums_ref)
    sums_ref[0:1, :] = col_sum(da)
    sums_ref[1:2, :] = col_sum(da * normed)


def leave(part, from_left, from_right, tokens, dh1, mods):
    return pl.pallas_call(
        leave_kernel,
        out_shape=(shape(tokens.shape), shape((8, tokens.shape[1]), F32)),
        in_specs=[VMEM] * 6,
        out_specs=(VMEM, VMEM),
        compiler_params=params(),
        name="leave",
    )(part, from_left, from_right, tokens, dh1, mods)


def weight_grad_kernel(count, flat, rows, packs, rows_ref, *refs):
    lefts = refs[:count]
    rights = refs[count : count * (1 + len(rows))]
    outs = refs[count * (1 + len(rows)) : -2]
    held_ref, sem = refs[-2:]
    blocks = sum(packs)
    part = lefts[0].shape[1]
    copies, held_at, held = [], [], 0
    for job, deep in enumerate(rows):
        held_at.append(held)
        for i in range(blocks):
            at = pl.ds(pl.multiple_of(rows_ref[job * blocks + i], 16), deep)
            for j in range(count):
                copies.append(
                    pltpu.make_async_copy(
                        lefts[j].at[at, :],
                        held_ref.at[held : held + deep, j * part : (j + 1) * part],
                        sem.at[len(copies)],
                    )
                )
            held += deep

    @pl.when(pl.program_id(0) == 0)
    def _():
        for copy in copies:
            copy.start()
        for copy in copies:
            copy.wait()

    dot = times_trans if flat else matmul
    for job, deep in enumerate(rows):
        base = held_at[job]
        for spot, pack in enumerate(packs):
            out_ref = outs[job * len(packs) + spot]
            total = None
            for j in range(count):
                term = dot(
                    held_ref[base : base + pack * deep, j * part : (j + 1) * part], rights[job * count + j][...]
                )
                total = term if total is None else total + term
            out_ref[...] = total.reshape(out_ref.shape).astype(BF)
            base += pack * deep


def weight_grad(lefts, rights, jobs, packs, wide, step, flat=False):
    count = len(lefts)
    part = lefts[0].shape[1]
    rows = tuple(job[1] for job in jobs)

    def right_spec(base):
        if flat:
            return pl.BlockSpec((step, part), lambda i, b: (i + base, 0))
        return pl.BlockSpec((part, step), lambda i, b: (0, i + base))

    outs = pl.pallas_call(
        functools.partial(weight_grad_kernel, count, flat, rows, packs),
        out_shape=tuple(shape((pack, deep, wide)) for deep in rows for pack in packs),
        grid_spec=pltpu.PrefetchScalarGridSpec(
            num_scalar_prefetch=1,
            grid=(wide // step,),
            in_specs=[ANY] * count + [right_spec(job[2]) for job in jobs for _ in range(count)],
            out_specs=tuple(
                pl.BlockSpec((pack, deep, step), lambda i, b: (0, 0, i)) for deep in rows for pack in packs
            ),
            scratch_shapes=[
                pltpu.VMEM((sum(packs) * sum(rows), part * count), BF),
                pltpu.SemaphoreType.DMA((sum(packs) * count * len(rows),)),
            ],
        ),
        compiler_params=params(dimension_semantics=("arbitrary",)),
        name="weight_grad",
    )(jnp.concatenate([job[0] for job in jobs]), *lefts, *(list(rights) * len(jobs)))
    return [outs[i * len(packs) : (i + 1) * len(packs)] for i in range(len(jobs))]


def weight_grad_seq_kernel(count, rows, order_ref, *refs):
    lefts, rights = refs[:count], refs[count : 2 * count]
    near_ref, far_ref, own_ref, held_ref, sem = refs[2 * count :]
    blocks = held_ref.shape[0] // rows
    part = lefts[0].shape[1]
    step = pl.program_id(0)
    copies = [
        pltpu.make_async_copy(
            lefts[j].at[pl.ds(pl.multiple_of(order_ref[4 + i], 16), rows), :],
            held_ref.at[i * rows : (i + 1) * rows, j * part : (j + 1) * part],
            sem.at[i * count + j],
        )
        for i in range(blocks)
        for j in range(count)
    ]

    @pl.when(step == 0)
    def _():
        for copy in copies:
            copy.start()
        for copy in copies:
            copy.wait()

    total = None
    for j in range(count):
        term = matmul(held_ref[:, j * part : (j + 1) * part], rights[j][...])
        total = term if total is None else total + term
    total = total.astype(BF)

    @pl.when(step < 2)
    def _():
        near_ref[0] = total

    @pl.when(step == 2)
    def _():
        far_ref[...] = total

    @pl.when(step == 3)
    def _():
        own_ref[...] = total


def weight_grad_seq(lefts, rights, row_starts, rows, columns, step):
    count = len(lefts)
    part = lefts[0].shape[1]
    blocks = row_starts.shape[0]
    return pl.pallas_call(
        functools.partial(weight_grad_seq_kernel, count, rows),
        out_shape=(shape((2, blocks * rows, step)), shape((blocks * rows, step)), shape((blocks * rows, step))),
        grid_spec=pltpu.PrefetchScalarGridSpec(
            num_scalar_prefetch=1,
            grid=(4,),
            in_specs=[ANY] * count + [pl.BlockSpec((part, step), lambda i, b: (0, b[i]))] * count,
            out_specs=(
                pl.BlockSpec((1, blocks * rows, step), lambda i, b: (jnp.minimum(i, 1), 0, 0)),
                pl.BlockSpec((blocks * rows, step), lambda i, b: (0, 0)),
                pl.BlockSpec((blocks * rows, step), lambda i, b: (0, 0)),
            ),
            scratch_shapes=[
                pltpu.VMEM((blocks * rows, part * count), BF),
                pltpu.SemaphoreType.DMA((blocks * count,)),
            ],
        ),
        compiler_params=params(dimension_semantics=("arbitrary",)),
        name="weight_grad_seq",
    )(jnp.concatenate([columns, row_starts]), *lefts, *rights)


def split_kernel(turned, rank_ref, keep_ref, got1_ref, got2_ref, near_ref, far_ref, own_ref):
    total = keep_ref[0].astype(F32) + got1_ref[got1_ref.shape[0] - 1].astype(F32) + got2_ref[0].astype(F32)
    total = total.astype(BF)
    if turned:
        total = jnp.transpose(total)
    size = 4
    block = total.shape[0 if turned else 1] // size
    for j in range(size):
        at = slice(j * block, (j + 1) * block)
        piece = total[at, :] if turned else total[:, at]
        mask = j ^ rank_ref[0]

        @pl.when(mask == 3)
        def _():
            near_ref[0] = piece

        @pl.when(mask == 1)
        def _():
            near_ref[1] = piece

        @pl.when(mask == 2)
        def _():
            far_ref[...] = piece

        @pl.when(mask == 0)
        def _():
            own_ref[...] = piece


def split(rank, keep, got1, got2, turned=False):
    rows, cols = keep.shape[1:]
    dims = (cols // 4, rows) if turned else (rows, cols // 4)
    return pl.pallas_call(
        functools.partial(split_kernel, turned),
        out_shape=(shape((2,) + dims), shape(dims), shape(dims)),
        in_specs=[SMEM, VMEM, VMEM, VMEM],
        out_specs=(VMEM,) * 3,
        compiler_params=params(),
        name="split",
    )(rank, keep, got1, got2)


def flip(x, axis, size, bit):
    return lax.ppermute(x, axis, [(i, i ^ bit) for i in range(size)])


def add(a, b):
    return (a.astype(F32) + b.astype(F32)).astype(BF)


def masks_of(bits):
    out = []
    for i in range(2 ** len(bits)):
        mask = 0
        for spot, bit in enumerate(bits):
            if not (i >> (len(bits) - 1 - spot)) & 1:
                mask |= bit
        out.append(mask)
    return out


def after(x, *others):
    return together(x, *others)[0]


def together(*values):
    leaves, tree = jax.tree.flatten(values)
    return jax.tree.unflatten(tree, lax.optimization_barrier(tuple(leaves)))


def exchange(blocks):
    return lax.all_to_all(blocks, "seq", split_axis=0, concat_axis=0, tiled=True)


def shards(
    tokens, modulation, image_ids, w_qkv, w_out, w_fc1, w_fc2, w_proj1, w_proj2, w_proj3, dino, cotangent,
):
    n_seq = lax.axis_size("seq")
    n_dp = lax.axis_size("dp")
    rank = lax.axis_index("seq")
    me = lax.axis_index("dp")
    tok_dev, width = tokens.shape
    group_tok = image_ids.shape[0]
    hidden, wide, narrow = w_fc1.shape[1], w_proj2.shape[0], w_proj3.shape[1]
    heads = H // n_seq
    local = heads * HD
    slots = modulation.shape[0]
    dp_bits = [1 << i for i in range(n_dp.bit_length() - 1)]
    rank_arg = rank.reshape(1).astype(jnp.int32)

    mods, *firsts = enter(image_ids, rank_arg, tokens, modulation)

    rights, lefts = [firsts], [firsts]
    for s in range(1, n_seq):
        up = [(i, i + 1) for i in range(s - 1, n_seq - 1)]
        low = [(i, i - 1) for i in range(1, n_seq - s + 1)]
        rights.append([lax.ppermute(v, "seq", up) for v in rights[-1]])
        lefts.append([lax.ppermute(v, "seq", low) for v in lefts[-1]])
    pieces = list(firsts)
    for d in range(1, n_seq):
        pieces += lefts[d] + rights[n_seq - d]

    columns = [lax.dynamic_slice_in_dim(w_qkv, i * width + rank * local, local, 1) for i in range(3)]
    w_rows = jnp.transpose(jnp.concatenate(columns, axis=1))
    w_pad = jnp.pad(w_rows.reshape(3 * heads, HD, width), ((0, 0), (0, HP - HD), (0, 0))).reshape(3 * heads * HP, width)
    ids_rel = lax.dynamic_slice_in_dim(jnp.concatenate([image_ids, image_ids]), rank * tok_dev, group_tok)
    idk, idq = ids_rel[:, None], ids_rel[None, :]
    one = (image_ids[0] == image_ids[group_tok - 1]).astype(jnp.int32).reshape(1)
    tile = group_tok // 4
    diagonal = tok_dev % tile == 0

    *heads_out, first_all, qkv, lse = attend_forward(
        one, rank_arg, pieces, w_pad, idk, idq, heads, tile, diagonal
    )
    attended = [heads_out[0]]
    for d in range(1, n_seq):
        attended.append(lax.ppermute(heads_out[d], "seq", [(i, (i + d) % n_seq) for i in range(n_seq)]))
    (rounded, act1, dr2, left1, right1, left2, gelu_slope, dmlp, dy, normed2, inv2, attn, sum_gate2) = middle(
        rank_arg, attended, tokens, mods, dino, cotangent, w_out, w_fc1, w_fc2, w_proj1, w_proj2, w_proj3
    )

    fast = all(k % (16 * n_dp) == 0 for k in (width, hidden, wide)) and n_dp == 8 and n_seq == 4

    def down(dmlp):
        return descend(n_seq, dmlp, gelu_slope, dy, normed2, inv2, attn, mods, w_fc2, w_fc1, w_out)

    def back(dos):
        return attend_backward(
            one, rank_arg, dos, qkv, heads_out, lse, w_rows, idk, idq, heads, tile, diagonal
        )

    def outgoing(g_heads, sums1):
        units = [g_heads[:, i * local : (i + 1) * local] for i in range(3)]
        rows = jnp.concatenate([sums1[0:2], sums2[0:3], sum_gate2], axis=0).astype(BF)
        rows = rows.reshape(n_seq, 6 * width // (n_seq * local), local)
        blocks = []
        for target in range(n_seq):
            mine = jnp.zeros_like(units[0])
            for i in range(3):
                mine = jnp.where((n_seq * i + rank) // 3 == target, units[i], mine)
            blocks.append(jnp.concatenate([mine, rows[target]], axis=0))
        return jnp.stack(blocks)

    if fast:
        swap = lambda x, bit: flip(x, "dp", n_dp, bit)
        core, x, y = dp_bits
        near = lambda v: flip(v, "seq", n_seq, 1)
        far = lambda v: flip(v, "seq", n_seq, 2)

        def job(base, deep, bits, column):
            starts = base + (me ^ jnp.array(masks_of(bits), jnp.int32)) * (deep // n_dp)
            return (starts, deep // n_dp, column)

        def right(v, step):
            return lax.ppermute(v, "seq", [(i, i + 1) for i in range(step)])

        def left(v, step):
            return lax.ppermute(v, "seq", [(i, i - 1) for i in range(n_seq - step, n_seq)])

        def row_starts(base, deep, bits):
            return base + (me ^ jnp.array(masks_of(bits), jnp.int32)) * (deep // n_dp)

        def row_starts(base, deep, bits):
            return base + (me ^ jnp.array(masks_of(bits), jnp.int32)) * (deep // n_dp)

        def last(*terms):
            return sum(v.astype(F32) for v in terms)

        quarter = (1, 1, 1, 1)
        lefts2, dmlps = [left2, swap(left2, core)], [dmlp, swap(dmlp, core)]
        act1_other, dr2_other = swap(act1, core), swap(dr2, core)
        right2, dhidden1, dheads, sums2 = down(dmlp)
        act1_other, dr2_other, lefts2, dmlps, left1, right1, right2, dheads = together(
            act1_other, dr2_other, lefts2, dmlps, left1, right1, right2, dheads
        )

        dheads_in = exchange(dheads)
        lefts1, rights1 = [left1, swap(left1, core)], [right1, swap(right1, core)]
        rights2 = [right2, swap(right2, core)]
        (p2,) = weight_grad([act1, act1_other], [dr2, dr2_other], [job(0, wide, (x, y), 0)], quarter, wide, STEP)
        (f2,) = weight_grad(lefts2, after(dmlps, p2), [job(0, hidden, (y, x), 0)], quarter, width, 384)
        p2, f2, lefts2, lefts1, rights1, rights2 = together(p2, f2, lefts2, lefts1, rights1, rights2)

        p2a, p2b, f2a = swap(p2[0], x), swap(p2[1], x), swap(f2[0], y)
        p1n, p1f, p1o = weight_grad_seq(
            lefts1, rights1, row_starts(wide, width, (y, x)), width // n_dp,
            rank ^ jnp.array(masks_of((1, 2)), jnp.int32), wide // n_seq,
        )
        p1z = near(p1n)
        (p3,) = weight_grad(
            lefts1, after(rights1, p1n), [job(0, wide, (y, x), wide // 256)], (2, 1, 1), narrow, 256
        )
        p3a = swap(p3[0], y)
        dqkv, dx = back(after(dheads_in, p3, p2a))
        f2s = add(f2[2], after(f2a, dqkv))
        p2, f2, p2a, p2b, f2s, p1f, p1o, p1z, p3, p3a, rights2, dqkv, dx = together(
            p2, f2, p2a, p2b, f2s, p1f, p1o, p1z, p3, p3a, rights2, dqkv, dx
        )

        f2c, f2b = swap(f2s, x), swap(f2[1], y)
        up, low = right(dx[3], 1), left(dx[1], 1)
        (f1,) = weight_grad(lefts2, rights2, [job(hidden, width, (x, y), 0)], quarter, hidden, 1152)
        p1y = far(add(p1f, p1z[0]))
        (fq,) = weight_grad(
            [first_all], [after(dqkv, f1)], [job(0, width, (core, y, x), 0)], (4, 2, 2), 3 * local, 3 * local,
            flat=True,
        )
        (fo,) = weight_grad(
            lefts2, after(rights2, fq), [job(hidden + width, width, (y, x), hidden // 384)], (2, 1, 1), width, 384
        )
        p2s, p3s, p1o = add(p2[2], p2a), add(p3[1], p3a[:1]), add(p1o, p1z[1])
        f2, f2c, f2b, up, low, p1y, p3s, f1, fq, fo, p2s, p1o = together(
            f2, f2c, f2b, up, low, p1y, p3s, f1, fq, fo, p2s, p1o
        )

        f1a, p2c = swap(f1[0], x), swap(p2s, y)
        up, low = right(add(dx[2], up), 2), left(add(dx[2], low), 2)
        fqa = swap(fq[0], core)
        f2n, f2f, f2o = split(rank_arg, after(f2[3], fqa), f2b, f2c, turned=True)
        f2z = near(f2n)
        p3c = swap(after(p3s, f2n), x)
        foa = swap(after(fo[0], p2c), y)
        p1d = add(p1o, p1y).reshape(4, width // n_dp, wide // n_seq)
        p2n, p2f, p2o = split(rank_arg, p2[3], p2b, p2c)
        up, low = add(dx[1], up), add(dx[3], low)
        f1s = add(f1[2], f1a)
        f1s, foa, fqa, p3c, p2n, p2f, p1d, f2z, f2f, up, low, f1 = together(
            f1s, foa, fqa, p3c, p2n, p2f, p1d, f2z, f2f, up, low, f1
        )

        f1b, f1c = swap(f1[1], x), swap(f1s, y)
        up, low = right(up, 3), left(low, 3)
        f2y = far(add(f2f, f2z[0]))
        p3n, p3f, p3o = split(rank_arg, p3[2], p3a, p3c, turned=True)
        p2z, foc = near(after(p2n, up, low)), swap(add(fo[1], after(foa, up, low)[:1]), x)
        fqb, fqk = swap(add(fq[1], after(fqa, up, low)[:2]), y), add(fq[2], fqa[2:])
        f1b, f1c, up, low, f2y, p2z, p2f, p3n, foc, fqb, fqk, p1d = together(
            f1b, f1c, up, low, f2y, p2z, p2f, p3n, foc, fqb, fqk, p1d
        )

        fqs, fqk = add(fqk[0], fqb[0]), add(fqk[1], fqb[1])
        fqc, p1e = swap(fqs, x), swap(p1d[0:2], y)
        p2y, p3z = far(add(p2f, p2z[0])), near(p3n)
        f1n, f1f, f1o = split(rank_arg, f1[3], f1b, f1c)
        f1z = near(f1n)
        fon, fof, foo = split(rank_arg, after(fo[2], f1n), foa, foc)
        foz = near(fon)
        grad_inputs, sums1 = leave(after(dx[0], fon, fqc), up, low, tokens, dhidden1, mods)
        incoming = exchange(outgoing(add(fqk, fqc), sums1))
        p1e, f1z, f1f, p2y, p3z, foz, fof = together(p1e, f1z, f1f, p2y, p3z, foz, fof)

        f1y, p3y, foy = far(add(f1f, f1z[0])), far(add(p3f, p3z[0])), far(add(fof, foz[0]))
        p1x = swap(add(p1d[2], p1e[0]), x)
        g_proj1 = last(p1d[3], p1e[1], p1x)
        g_proj2, g_fc1, g_fc2 = last(p2o, p2z[1], p2y), last(f1o, f1z[1], f1y), jnp.transpose(last(f2o, f2z[1], f2y))
        g_proj3, g_out = jnp.transpose(last(p3o, p3z[1], p3y)), last(foo, foz[1], foy)
    else:
        right2, dhidden1, dheads, sums2 = down(dmlp)
        dqkv, dx = back(exchange(dheads))
        up, low = None, None
        for s in range(1, n_seq):
            up = dx[n_seq - s] if up is None else add(dx[n_seq - s], up)
            low = dx[s] if low is None else add(dx[s], low)
            up = lax.ppermute(up, "seq", [(i, i + 1) for i in range(s)])
            low = lax.ppermute(low, "seq", [(i, i - 1) for i in range(n_seq - s, n_seq)])
        grad_inputs, sums1 = leave(dx[0], up, low, tokens, dhidden1, mods)

        def reduced(a, b):
            share = lax.psum_scatter(matmul(a, b).astype(BF), "dp", scatter_dimension=0, tiled=True)
            return lax.psum_scatter(share, "seq", scatter_dimension=1, tiled=True).astype(F32)

        g_proj3 = reduced(left1[:wide], right1[:, wide:])
        g_proj2 = reduced(act1, dr2)
        g_proj1 = reduced(left1[wide:], right1[:, :wide])
        g_fc2 = reduced(left2[:hidden], dmlp)
        g_fc1 = reduced(left2[hidden : hidden + width], right2[:, :hidden])
        g_out = reduced(left2[hidden + width :], right2[:, hidden:])
        g_heads = lax.psum_scatter(
            times_trans(first_all, dqkv).astype(BF), "dp", scatter_dimension=0, tiled=True
        )

    if not fast:
        incoming = exchange(outgoing(g_heads, sums1))
    held = width // n_dp
    slot = jnp.arange(slots, dtype=jnp.int32)[:, None, None]
    whose = image_ids[::tok_dev]
    dmods = incoming[:, held:].reshape(n_seq, 6 * width // n_seq).astype(F32)
    grad_mods = jnp.sum(jnp.where(slot == whose[None, :, None], dmods[None], 0.0), axis=1)
    incoming = incoming[:, :held]
    columns = [jnp.zeros(incoming.shape[1:], BF) for _ in range(3)]
    for source in range(n_seq):
        for i in range(3):
            unit = n_seq * i + source
            columns[unit % 3] = jnp.where(unit // 3 == rank, incoming[source], columns[unit % 3])
    g_qkv = jnp.concatenate(columns, axis=1).astype(F32)

    return (rounded, grad_inputs, grad_mods, g_qkv, g_out, g_fc1, g_fc2, g_proj1, g_proj2, g_proj3)


def solution(mesh):
    tok = P(("dp", "seq"), None)
    in_specs = (tok, P("dp", None), P("dp")) + (P(),) * 7 + (tok, tok)
    out_specs = (tok, tok) + (P("dp", "seq"),) * 8
    return jax.shard_map(shards, mesh=mesh, in_specs=in_specs, out_specs=out_specs, check_vma=False)
```

```python
import functools

import jax
import jax.numpy as jnp
from jax import lax
from jax.experimental import pallas as pl
from jax.experimental.pallas import tpu as pltpu
from jax.sharding import PartitionSpec as P

H = 16
HD = 72
HP = 80
LEN = 1024
EPS_NORM = 1e-06
SCALE = HD ** (-0.5)
EXP2_SCALE = SCALE * 1.4426950408889634
GELU_A = 0.7978845608028654
GELU_B = 0.044715
BF = jnp.bfloat16
F32 = jnp.float32
ANY = pl.BlockSpec(memory_space=pl.ANY)
VMEM = pl.BlockSpec(memory_space=pltpu.VMEM)
SMEM = pl.BlockSpec(memory_space=pltpu.SMEM)
ROOM = 60 << 20
PARTS = 2


def matmul(left, right):
    return jnp.dot(left, right, preferred_element_type=F32)


def times_trans(left, right):
    return lax.dot_general(left, right, (((1,), (1,)), ((), ())), preferred_element_type=F32)


def trans_times(left, right):
    return lax.dot_general(left, right, (((0,), (0,)), ((), ())), preferred_element_type=F32)


def row_mean(v):
    return jnp.mean(v, axis=-1, keepdims=True)


def normalize(v):
    centre = v - row_mean(v)
    inv = lax.rsqrt(row_mean(centre * centre) + EPS_NORM)
    return centre * inv, inv


def norm_back(e, normed, inv):
    return (e - row_mean(e) - normed * row_mean(e * normed)) * inv


def col_sum(v):
    return jnp.sum(v, axis=0, keepdims=True)


def sigmoid(v):
    return 1.0 / (1.0 + jnp.exp(-v))


def shape(dims, kind=BF):
    return jax.ShapeDtypeStruct(dims, kind)


def params(**more):
    return pltpu.CompilerParams(vmem_limit_bytes=ROOM, **more)


def enter_kernel(ids_ref, rank_ref, tokens_ref, mod_ref, mods_ref, *out_refs):
    width = tokens_ref.shape[1]
    table = mod_ref[...].astype(F32)
    mine = lax.broadcasted_iota(jnp.int32, table.shape, 0) == ids_ref[rank_ref[0] * tokens_ref.shape[0]]
    mods = col_sum(jnp.where(mine, table, 0.0))
    mods_ref[...] = jnp.zeros_like(mods_ref)
    for i in range(6):
        mods_ref[i : i + 1, :] = mods[:, i * width : (i + 1) * width]
    normed, _ = normalize(tokens_ref[...].astype(F32))
    first = normed * (1.0 + mods[:, width : 2 * width]) + mods[:, 0:width]
    first = jnp.transpose(first.astype(BF))
    rows = out_refs[0].shape[0]
    for i, out_ref in enumerate(out_refs):
        out_ref[...] = first[i * rows : (i + 1) * rows, :]


def enter(ids, rank, tokens, modulation):
    tok, width = tokens.shape
    return pl.pallas_call(
        enter_kernel,
        out_shape=(shape((8, width), F32),) + (shape((width // PARTS, tok)),) * PARTS,
        in_specs=[SMEM, SMEM, VMEM, VMEM],
        out_specs=(VMEM,) * (1 + PARTS),
        compiler_params=params(),
        name="enter",
    )(ids, rank, tokens, modulation)


def attend_forward_kernel(size, heads, tile, diagonal, one_ref, rank_ref, *refs):
    count = PARTS * (2 * size - 1)
    pieces = refs[:count]
    w_any, idk_ref, idq_ref = refs[count : count + 3]
    o_refs = refs[count + 3 : count + 3 + size]
    (x_any, qkv_any, lse_ref, x_ref, qkv_ref, w_ref, k_ref, o_all_ref, sem, w_sem, out_sem) = refs[count + 3 + size :]
    tok = pieces[0].shape[1]
    total = x_ref.shape[1]
    rows = pieces[0].shape[0]
    rank = rank_ref[0]
    w_copy = pltpu.make_async_copy(w_any, w_ref, w_sem.at[0])
    w_copy.start()

    def piece_copy(d, part, source):
        at = 0 if d == 0 else 2 * d - 2 + source
        return pltpu.make_async_copy(
            pieces[at * PARTS + part],
            x_ref.at[part * rows : (part + 1) * rows, d * tok : (d + 1) * tok],
            sem.at[d, part],
        )

    for part in range(PARTS):
        piece_copy(0, part, 0).start()
    for d in range(1, size):
        for part in range(PARTS):

            @pl.when(rank + d < size)
            def _():
                piece_copy(d, part, 1).start()

            @pl.when(rank + d >= size)
            def _():
                piece_copy(d, part, 2).start()

    w_copy.wait()
    for d in range(size):
        for part in range(PARTS):
            piece_copy(d, part, 1).wait()
        at = slice(d * tok, (d + 1) * tok)
        qkv_ref[:, at] = matmul(w_ref[...], x_ref[:, at]).astype(BF)
    out_copies = [
        pltpu.make_async_copy(x_ref, x_any, out_sem.at[0]),
        pltpu.make_async_copy(qkv_ref, qkv_any, out_sem.at[1]),
    ]
    for copy in out_copies:
        copy.start()

    def head_step(head, carry):
        q_at = pl.ds(pl.multiple_of(head * HP, HP), HP)
        k_at = pl.ds(pl.multiple_of((heads + head) * HP, HP), HP)
        v_at = pl.ds(pl.multiple_of((2 * heads + head) * HP, HP), HP)
        o_at = pl.ds(pl.multiple_of(head * HD, 8), HD)
        k_ref[...] = jnp.transpose(qkv_ref[k_at, :])

        def block(at, keys, masked):
            s = matmul(k_ref[keys, :], qkv_ref[q_at, at]) * EXP2_SCALE
            if masked:
                s = jnp.where(idk_ref[...] == idq_ref[:, at], s, -1e30)
            top = jnp.max(s, axis=0, keepdims=True)
            e = jnp.exp2(s - top)
            tot = col_sum(e)
            o = matmul(qkv_ref[v_at, keys], e.astype(BF)) * (1.0 / tot)
            o_all_ref[o_at, at] = o[0:HD, :]
            lse_ref[pl.ds(head, 1), at] = top + jnp.log2(tot)

        def full(masked):
            def step(i, inner):
                block(pl.ds(pl.multiple_of(i * tile, tile), tile), pl.ds(0, total), masked)
                return inner

            lax.fori_loop(0, total // tile, step, 0, unroll=True)

        @pl.when(one_ref[0] == 1)
        def _():
            full(False)

        @pl.when(one_ref[0] == 0)
        def _():
            if diagonal:

                def step(i, inner):
                    at = pl.ds(pl.multiple_of(i * tile, tile), tile)
                    block(at, at, False)
                    return inner

                lax.fori_loop(0, total // tile, step, 0, unroll=True)
            else:
                full(True)

        return carry

    lax.fori_loop(0, heads, head_step, 0)
    for d in range(size):
        o_refs[d][...] = o_all_ref[:, d * tok : (d + 1) * tok].astype(BF)
    for copy in out_copies:
        copy.wait()


def attend_forward(one, rank, pieces, w, idk, idq, heads, tile, diagonal):
    size = (len(pieces) // PARTS + 1) // 2
    tok = pieces[0].shape[1]
    width, total = PARTS * pieces[0].shape[0], size * tok
    return pl.pallas_call(
        functools.partial(attend_forward_kernel, size, heads, tile, diagonal),
        out_shape=(shape((heads * HD, tok)),) * size
        + (
            shape((width, total)),
            shape((3 * heads * HP, total)),
            shape((heads, total), F32),
        ),
        in_specs=[SMEM, SMEM] + [ANY] * (len(pieces) + 1) + [VMEM, VMEM],
        out_specs=(VMEM,) * size + (ANY, ANY, VMEM),
        scratch_shapes=[
            pltpu.VMEM((width, total), BF),
            pltpu.VMEM((3 * heads * HP, total), BF),
            pltpu.VMEM(w.shape, BF),
            pltpu.VMEM((total, HP), BF),
            pltpu.VMEM((heads * HD, total), F32),
            pltpu.SemaphoreType.DMA((size, PARTS)),
            pltpu.SemaphoreType.DMA((1,)),
            pltpu.SemaphoreType.DMA((2,)),
        ],
        compiler_params=params(),
        name="attend_forward",
    )(one, rank, *pieces, w, idk, idq)


def attend_backward_kernel(size, heads, tile, diagonal, one_ref, rank_ref, *refs):
    o_refs, refs = refs[:size], refs[size:]
    dos_ref, qkv_ref, lse_ref, w_ref, idk_ref, idq_ref = refs[:6]
    dqkv_ref, dx_ref, k_ref, v_ref, do_ref, dk_ref, dv_ref, acc_ref, delta_ref = refs[6:]
    tok = dos_ref.shape[2]
    total = qkv_ref.shape[1]
    local = heads * HD
    for d in range(size):
        at = slice(d * tok, (d + 1) * tok)
        owner = lax.rem(rank_ref[0] + d, size)
        do = dos_ref[owner].astype(F32)
        do_ref[0:local, at] = do
        do_ref[local : local + HP - HD, at] = jnp.zeros((HP - HD, tok), F32)
        prod = do * o_refs[d][...].astype(F32)
        for head in range(heads):
            delta_ref[head : head + 1, at] = col_sum(prod[head * HD : (head + 1) * HD, :])

    def head_step(head, carry):
        q_at = pl.ds(pl.multiple_of(head * HP, HP), HP)
        k_at = pl.ds(pl.multiple_of((heads + head) * HP, HP), HP)
        v_at = pl.ds(pl.multiple_of((2 * heads + head) * HP, HP), HP)
        o_at = pl.ds(pl.multiple_of(head * HD, 8), HP)
        k_ref[...] = jnp.transpose(qkv_ref[k_at, :])
        v_ref[...] = jnp.transpose(qkv_ref[v_at, :])

        def out_at(part):
            return pl.ds(pl.multiple_of(part * local + head * HD, 8), HD)

        def block(at, keys, masked, fresh):
            q = qkv_ref[q_at, at]
            do = do_ref[o_at, at].astype(BF)
            p = jnp.exp2(matmul(k_ref[keys, :], q) * EXP2_SCALE - lse_ref[pl.ds(head, 1), at])
            if masked:
                p = jnp.where(idk_ref[...] == idq_ref[:, at], p, 0.0)
            ds = (p * (matmul(v_ref[keys, :], do) - delta_ref[pl.ds(head, 1), at])).astype(BF)
            dv = times_trans(do, p.astype(BF))
            dk = times_trans(q, ds)
            if fresh:
                dv_ref[:, keys] = dv
                dk_ref[:, keys] = dk
            else:
                dv_ref[:, keys] += dv
                dk_ref[:, keys] += dk
            dq = matmul(qkv_ref[k_at, keys], ds) * SCALE
            acc_ref[out_at(0), at] = dq[0:HD, :]

        def full(masked):
            dk_ref[...] = jnp.zeros_like(dk_ref)
            dv_ref[...] = jnp.zeros_like(dv_ref)

            def step(i, inner):
                block(pl.ds(pl.multiple_of(i * tile, tile), tile), pl.ds(0, total), masked, False)
                return inner

            lax.fori_loop(0, total // tile, step, 0, unroll=True)

        @pl.when(one_ref[0] == 1)
        def _():
            full(False)

        @pl.when(one_ref[0] == 0)
        def _():
            if diagonal:

                def step(i, inner):
                    at = pl.ds(pl.multiple_of(i * tile, tile), tile)
                    block(at, at, False, True)
                    return inner

                lax.fori_loop(0, total // tile, step, 0, unroll=True)
            else:
                full(True)

        acc_ref[out_at(1), :] = dk_ref[0:HD, :] * SCALE
        acc_ref[out_at(2), :] = dv_ref[0:HD, :]
        return carry

    lax.fori_loop(0, heads, head_step, 0)
    dqkv_ref[...] = acc_ref[...].astype(BF)
    for d in range(size):
        dx_ref[d] = trans_times(dqkv_ref[:, d * tok : (d + 1) * tok], w_ref[...]).astype(BF)


def attend_backward(one, rank, dos, qkv, o, lse, w, idk, idq, heads, tile, diagonal):
    size, local, tok = dos.shape
    total = size * tok
    width = w.shape[1]
    return pl.pallas_call(
        functools.partial(attend_backward_kernel, size, heads, tile, diagonal),
        out_shape=(shape((3 * local, total)), shape((size, tok, width))),
        in_specs=[SMEM, SMEM] + [VMEM] * (size + 6),
        out_specs=(VMEM, VMEM),
        scratch_shapes=[
            pltpu.VMEM((total, HP), BF),
            pltpu.VMEM((total, HP), BF),
            pltpu.VMEM((local + HP - HD, total), F32),
            pltpu.VMEM((HP, total), F32),
            pltpu.VMEM((HP, total), F32),
            pltpu.VMEM((3 * local, total), F32),
            pltpu.VMEM((heads, total), F32),
        ],
        compiler_params=params(),
        name="attend_backward",
    )(one, rank, *o, dos, qkv, lse, w, idk, idq)


STEP = 512


def middle_kernel(size, rank_ref, *refs):
    o_refs, refs = refs[:size], refs[size:]
    (tokens_ref, mods_ref, dino_ref, cot_ref, wo_any, w1_any, w2_any, p1_any, p2_any, p3_any) = refs[:10]
    (out_any, a1_any, dr2_any, left1_any, right1_ref, left2_any, gp_any, dmlp_ref, dy_ref, normed_any, inv_ref, attn_any,
     gate_ref) = refs[10:23]
    (wo_ref, w1_ref, w2_ref, p1_ref, p2_ref, p3_ref, act_ref, out_ref, a1_ref, dr2_ref, left1_ref, left2_ref, gp_ref,
     normed_ref, attn_ref, w1_sem, sems, out_sems) = refs[23:]
    flushes = []

    def flush(source, target):
        copy = pltpu.make_async_copy(source, target, out_sems.at[len(flushes)])
        copy.start()
        flushes.append(copy)

    local, tok = o_refs[0].shape
    width = size * local
    hidden = w1_any.shape[1]
    wide, narrow = p3_ref.shape
    steps = hidden // STEP
    slots = w1_ref.shape[0]
    a2_ref, y_ref = left1_ref.at[0:wide, :], left1_ref.at[wide:, :]
    g_ref, b_ref = left2_ref.at[0:hidden, :], left2_ref.at[hidden : hidden + width, :]
    o_ref = left2_ref.at[hidden + width :, :]
    dr1_ref, dz_ref = right1_ref.at[:, 0:wide], right1_ref.at[:, wide:]
    wo_copy = pltpu.make_async_copy(wo_any, wo_ref, sems.at[4])
    wo_copy.start()

    def w1_copy(i):
        at = pl.ds(pl.multiple_of(i * STEP, STEP), STEP)
        slot = lax.rem(i, slots)
        return pltpu.make_async_copy(w1_any.at[:, at], w1_ref.at[slot], w1_sem.at[slot])

    for i in range(slots):
        w1_copy(i).start()
    w2_copy = pltpu.make_async_copy(w2_any, w2_ref, sems.at[0])
    p1_copy = pltpu.make_async_copy(p1_any, p1_ref, sems.at[1])
    p2_copy = pltpu.make_async_copy(p2_any, p2_ref, sems.at[2])
    p3_copy = pltpu.make_async_copy(p3_any, p3_ref, sems.at[3])
    for copy in (w2_copy, p1_copy, p2_copy, p3_copy):
        copy.start()

    gate1, shift2, scale2, gate2 = [mods_ref[i : i + 1, :] for i in (2, 3, 4, 5)]
    for d in range(size):
        owner = lax.rem(rank_ref[0] + size - d, size)
        o_ref[pl.ds(pl.multiple_of(owner * local, 16), local), :] = o_refs[d][...]
    wo_copy.wait()
    attn = trans_times(o_ref[...], wo_ref[...])
    attn_ref[...] = attn
    flush(attn_ref, attn_any)
    h1 = tokens_ref[...].astype(F32) + gate1 * attn
    normed, inv = normalize(h1)
    normed_ref[...] = normed
    flush(normed_ref, normed_any)
    inv_ref[...] = inv
    b = (normed * (1.0 + scale2) + shift2).astype(BF)
    b_ref[...] = jnp.transpose(b)

    def up(i, carry):
        at = pl.ds(pl.multiple_of(i * STEP, STEP), STEP)
        w1_copy(i).wait()
        u = matmul(b, w1_ref[lax.rem(i, slots)])

        @pl.when(i + slots < steps)
        def _():
            w1_copy(i + slots).start()

        sq = u * u
        t = jnp.tanh(u * (GELU_A + (GELU_A * GELU_B) * sq))
        half = 0.5 * (1.0 + t)
        g = (u * half).astype(BF)
        gp_ref[:, at] = (half + u * (1.0 - t * t) * (0.5 * GELU_A + (1.5 * GELU_A * GELU_B) * sq)).astype(BF)
        act_ref[:, at] = g
        g_ref[at, :] = jnp.transpose(g)
        return carry

    lax.fori_loop(0, steps, up, 0, unroll=True)
    flush(left2_ref, left2_any)
    flush(gp_ref, gp_any)
    w2_copy.wait()
    mlp = matmul(act_ref[...], w2_ref[...])
    y = (h1 + gate2 * mlp).astype(BF)
    out_ref[...] = y
    flush(out_ref, out_any)
    y_ref[...] = jnp.transpose(y)
    def project(source, w_ref, held, out_t_ref, slope_ref):
        def step(i, carry):
            at = pl.ds(pl.multiple_of(i * STEP, STEP), STEP)
            r = matmul(source, w_ref[:, at])
            sig = sigmoid(r)
            act = (r * sig).astype(BF)
            act_ref[:, pl.ds(pl.multiple_of(held + i * STEP, STEP), STEP)] = act
            out_t_ref[at, :] = jnp.transpose(act)
            slope_ref[:, at] = (sig * (1.0 + r * (1.0 - sig))).astype(BF)
            return carry

        lax.fori_loop(0, wide // STEP, step, 0, unroll=True)
        return act_ref[:, held : held + wide]

    def project_back(source, w_ref, slope_ref):
        def step(i, carry):
            at = pl.ds(pl.multiple_of(i * STEP, STEP), STEP)
            slope_ref[:, at] = (times_trans(source, w_ref[at, :]) * slope_ref[:, at].astype(F32)).astype(BF)
            return carry

        lax.fori_loop(0, wide // STEP, step, 0, unroll=True)
        return slope_ref[...]

    p1_copy.wait()
    a1 = project(y, p1_ref, 0, a1_ref, dr1_ref)
    flush(a1_ref, a1_any)
    p2_copy.wait()
    a2 = project(a1, p2_ref, wide, a2_ref, dr2_ref)
    flush(left1_ref, left1_any)
    p3_copy.wait()
    z = matmul(a2, p3_ref[...])
    t = dino_ref[...].astype(F32)
    nz = lax.rsqrt(jnp.sum(z * z, axis=-1, keepdims=True) + EPS_NORM)
    nt = lax.rsqrt(jnp.sum(t * t, axis=-1, keepdims=True) + EPS_NORM)
    cosine = jnp.sum(z * t, axis=-1, keepdims=True) * nz * nt
    dz = (-0.5 * (t * (nz * nt) - (cosine * nz * nz) * z)).astype(BF)
    dz_ref[...] = dz
    dr2 = project_back(dz, p3_ref, dr2_ref)
    flush(dr2_ref, dr2_any)
    dr1 = project_back(dr2, p2_ref, dr1_ref)
    dy = cot_ref[...].astype(F32) + times_trans(dr1, p1_ref[...])
    dy_ref[...] = dy
    dmlp_ref[...] = (gate2 * dy).astype(BF)
    gate_ref[...] = col_sum(dy * mlp)
    for copy in flushes:
        copy.wait()


def middle(rank, os, tokens, mods, dino, cot, wo, w1, w2, p1, p2, p3):
    tok, width = tokens.shape
    hidden, wide, narrow = w1.shape[1], p1.shape[1], p3.shape[1]
    return pl.pallas_call(
        functools.partial(middle_kernel, len(os)),
        out_shape=(
            shape((tok, width)), shape((wide, tok)), shape((tok, wide)), shape((wide + width, tok)),
            shape((tok, wide + narrow)), shape((hidden + 2 * width, tok)), shape((tok, hidden)), shape((tok, width)), shape((tok, width), F32),
            shape((tok, width), F32), shape((tok, 1), F32), shape((tok, width), F32), shape((1, width), F32),
        ),
        in_specs=[SMEM] + [VMEM] * (len(os) + 4) + [ANY] * 6,
        out_specs=(ANY, ANY, ANY, ANY, VMEM, ANY, ANY, VMEM, VMEM, ANY, VMEM, ANY, VMEM),
        scratch_shapes=[
            pltpu.VMEM(dims, BF)
            for dims in (wo.shape, (4, width, STEP), w2.shape, p1.shape, p2.shape, p3.shape, (tok, hidden))
        ]
        + [
            pltpu.VMEM(dims, kind)
            for dims, kind in (
                ((tok, width), BF), ((wide, tok), BF), ((tok, wide), BF), ((wide + width, tok), BF),
                ((hidden + 2 * width, tok), BF), ((tok, hidden), BF), ((tok, width), F32), ((tok, width), F32),
            )
        ]
        + [pltpu.SemaphoreType.DMA((4,)), pltpu.SemaphoreType.DMA((5,)), pltpu.SemaphoreType.DMA((8,))],
        compiler_params=params(),
        name="middle",
    )(rank, *os, tokens, mods, dino, cot, wo, w1, w2, p1, p2, p3)


def descend_kernel(size, *refs):
    (dmlp_ref, gp_any, dy_any, normed_any, inv_ref, attn_any, mods_ref, w2_any, w1_any, wo_any) = refs[:10]
    (right2_ref, dh1_ref, do_ref, sums_ref) = refs[10:14]
    (w2_ref, w1_ref, wo_ref, gp_ref, dy_ref, normed_ref, attn_ref, w2_sem, w1_sem, wo_sem, in_sem) = refs[14:]
    hidden = w1_ref.shape[1]
    du_ref, dattn_ref = right2_ref.at[:, 0:hidden], right2_ref.at[:, hidden:]
    local = do_ref.shape[1]
    steps = hidden // STEP

    def w2_copy(i):
        at = pl.ds(pl.multiple_of(i * STEP, STEP), STEP)
        return pltpu.make_async_copy(w2_any.at[at, :], w2_ref.at[at, :], w2_sem.at[i])

    in_copies = [
        pltpu.make_async_copy(source, held, in_sem.at[i])
        for i, (source, held) in enumerate(
            ((gp_any, gp_ref), (dy_any, dy_ref), (normed_any, normed_ref), (attn_any, attn_ref))
        )
    ]
    in_copies[0].start()
    for i in range(steps):
        w2_copy(i).start()
    w1_copy = pltpu.make_async_copy(w1_any, w1_ref, w1_sem.at[0])
    w1_copy.start()
    wo_copy = pltpu.make_async_copy(wo_any, wo_ref, wo_sem.at[0])
    wo_copy.start()
    for copy in in_copies[1:]:
        copy.start()
    in_copies[0].wait()
    dmlp = dmlp_ref[...]

    def down(i, carry):
        at = pl.ds(pl.multiple_of(i * STEP, STEP), STEP)
        w2_copy(i).wait()
        du_ref[:, at] = (times_trans(dmlp, w2_ref[at, :]) * gp_ref[:, at].astype(F32)).astype(BF)
        return carry

    lax.fori_loop(0, steps, down, 0, unroll=True)
    w1_copy.wait()
    for copy in in_copies[1:]:
        copy.wait()
    db = times_trans(du_ref[...], w1_ref[...])
    gate1, scale2 = mods_ref[2:3, :], mods_ref[4:5, :]
    normed = normed_ref[...]
    dh1 = dy_ref[...] + norm_back(db * (1.0 + scale2), normed, inv_ref[...])
    dh1_ref[...] = dh1
    dattn = (gate1 * dh1).astype(BF)
    dattn_ref[...] = dattn
    sums_ref[...] = jnp.zeros_like(sums_ref)
    sums_ref[0:1, :] = col_sum(dh1 * attn_ref[...])
    sums_ref[1:2, :] = col_sum(db)
    sums_ref[2:3, :] = col_sum(db * normed)
    wo_copy.wait()
    for d in range(size):
        do_ref[d] = times_trans(wo_ref[d * local : (d + 1) * local, :], dattn).astype(BF)


def descend(size, dmlp, gp, dy, normed, inv, attn, mods, w2, w1, wo):
    tok, width = dmlp.shape
    hidden = w1.shape[1]
    return pl.pallas_call(
        functools.partial(descend_kernel, size),
        out_shape=(
            shape((tok, hidden + width)), shape((tok, width), F32),
            shape((size, width // size, tok)), shape((8, width), F32),
        ),
        in_specs=[VMEM, ANY, ANY, ANY, VMEM, ANY, VMEM] + [ANY] * 3,
        out_specs=(VMEM,) * 4,
        scratch_shapes=[pltpu.VMEM(w.shape, BF) for w in (w2, w1, wo, gp)]
        + [pltpu.VMEM(v.shape, F32) for v in (dy, normed, attn)]
        + [
            pltpu.SemaphoreType.DMA((hidden // STEP,)),
            pltpu.SemaphoreType.DMA((1,)),
            pltpu.SemaphoreType.DMA((1,)),
            pltpu.SemaphoreType.DMA((4,)),
        ],
        compiler_params=params(),
        name="descend",
    )(dmlp, gp, dy, normed, inv, attn, mods, w2, w1, wo)


def leave_kernel(part_ref, left_ref, right_ref, tokens_ref, dh1_ref, mods_ref, out_ref, sums_ref):
    da = part_ref[...].astype(F32) + left_ref[...].astype(F32) + right_ref[...].astype(F32)
    normed, inv = normalize(tokens_ref[...].astype(F32))
    out_ref[...] = (dh1_ref[...] + norm_back(da * (1.0 + mods_ref[1:2, :]), normed, inv)).astype(BF)
    sums_ref[...] = jnp.zeros_like(sums_ref)
    sums_ref[0:1, :] = col_sum(da)
    sums_ref[1:2, :] = col_sum(da * normed)


def leave(part, from_left, from_right, tokens, dh1, mods):
    return pl.pallas_call(
        leave_kernel,
        out_shape=(shape(tokens.shape), shape((8, tokens.shape[1]), F32)),
        in_specs=[VMEM] * 6,
        out_specs=(VMEM, VMEM),
        compiler_params=params(),
        name="leave",
    )(part, from_left, from_right, tokens, dh1, mods)


def weight_grad_kernel(count, flat, rows, packs, rows_ref, *refs):
    lefts = refs[:count]
    rights = refs[count : count * (1 + len(rows))]
    outs = refs[count * (1 + len(rows)) : -2]
    held_ref, sem = refs[-2:]
    blocks = sum(packs)
    part = lefts[0].shape[1]
    copies, held_at, held = [], [], 0
    for job, deep in enumerate(rows):
        held_at.append(held)
        for i in range(blocks):
            at = pl.ds(pl.multiple_of(rows_ref[job * blocks + i], 16), deep)
            for j in range(count):
                copies.append(
                    pltpu.make_async_copy(
                        lefts[j].at[at, :],
                        held_ref.at[held : held + deep, j * part : (j + 1) * part],
                        sem.at[len(copies)],
                    )
                )
            held += deep

    @pl.when(pl.program_id(0) == 0)
    def _():
        for copy in copies:
            copy.start()
        for copy in copies:
            copy.wait()

    dot = times_trans if flat else matmul
    for job, deep in enumerate(rows):
        base = held_at[job]
        for spot, pack in enumerate(packs):
            out_ref = outs[job * len(packs) + spot]
            total = None
            for j in range(count):
                term = dot(
                    held_ref[base : base + pack * deep, j * part : (j + 1) * part], rights[job * count + j][...]
                )
                total = term if total is None else total + term
            out_ref[...] = total.reshape(out_ref.shape).astype(BF)
            base += pack * deep


def weight_grad(lefts, rights, jobs, packs, wide, step, flat=False):
    count = len(lefts)
    part = lefts[0].shape[1]
    rows = tuple(job[1] for job in jobs)

    def right_spec(base):
        if flat:
            return pl.BlockSpec((step, part), lambda i, b: (i + base, 0))
        return pl.BlockSpec((part, step), lambda i, b: (0, i + base))

    outs = pl.pallas_call(
        functools.partial(weight_grad_kernel, count, flat, rows, packs),
        out_shape=tuple(shape((pack, deep, wide)) for deep in rows for pack in packs),
        grid_spec=pltpu.PrefetchScalarGridSpec(
            num_scalar_prefetch=1,
            grid=(wide // step,),
            in_specs=[ANY] * count + [right_spec(job[2]) for job in jobs for _ in range(count)],
            out_specs=tuple(
                pl.BlockSpec((pack, deep, step), lambda i, b: (0, 0, i)) for deep in rows for pack in packs
            ),
            scratch_shapes=[
                pltpu.VMEM((sum(packs) * sum(rows), part * count), BF),
                pltpu.SemaphoreType.DMA((sum(packs) * count * len(rows),)),
            ],
        ),
        compiler_params=params(dimension_semantics=("arbitrary",)),
        name="weight_grad",
    )(jnp.concatenate([job[0] for job in jobs]), *lefts, *(list(rights) * len(jobs)))
    return [outs[i * len(packs) : (i + 1) * len(packs)] for i in range(len(jobs))]


def weight_grad_seq_kernel(count, rows, order_ref, *refs):
    lefts, rights = refs[:count], refs[count : 2 * count]
    near_ref, far_ref, own_ref, held_ref, sem = refs[2 * count :]
    blocks = held_ref.shape[0] // rows
    part = lefts[0].shape[1]
    step = pl.program_id(0)
    copies = [
        pltpu.make_async_copy(
            lefts[j].at[pl.ds(pl.multiple_of(order_ref[4 + i], 16), rows), :],
            held_ref.at[i * rows : (i + 1) * rows, j * part : (j + 1) * part],
            sem.at[i * count + j],
        )
        for i in range(blocks)
        for j in range(count)
    ]

    @pl.when(step == 0)
    def _():
        for copy in copies:
            copy.start()
        for copy in copies:
            copy.wait()

    total = None
    for j in range(count):
        term = matmul(held_ref[:, j * part : (j + 1) * part], rights[j][...])
        total = term if total is None else total + term
    total = total.astype(BF)

    @pl.when(step < 2)
    def _():
        near_ref[0] = total

    @pl.when(step == 2)
    def _():
        far_ref[...] = total

    @pl.when(step == 3)
    def _():
        own_ref[...] = total


def weight_grad_seq(lefts, rights, row_starts, rows, columns, step):
    count = len(lefts)
    part = lefts[0].shape[1]
    blocks = row_starts.shape[0]
    return pl.pallas_call(
        functools.partial(weight_grad_seq_kernel, count, rows),
        out_shape=(shape((2, blocks * rows, step)), shape((blocks * rows, step)), shape((blocks * rows, step))),
        grid_spec=pltpu.PrefetchScalarGridSpec(
            num_scalar_prefetch=1,
            grid=(4,),
            in_specs=[ANY] * count + [pl.BlockSpec((part, step), lambda i, b: (0, b[i]))] * count,
            out_specs=(
                pl.BlockSpec((1, blocks * rows, step), lambda i, b: (jnp.minimum(i, 1), 0, 0)),
                pl.BlockSpec((blocks * rows, step), lambda i, b: (0, 0)),
                pl.BlockSpec((blocks * rows, step), lambda i, b: (0, 0)),
            ),
            scratch_shapes=[
                pltpu.VMEM((blocks * rows, part * count), BF),
                pltpu.SemaphoreType.DMA((blocks * count,)),
            ],
        ),
        compiler_params=params(dimension_semantics=("arbitrary",)),
        name="weight_grad_seq",
    )(jnp.concatenate([columns, row_starts]), *lefts, *rights)


def split_kernel(turned, rank_ref, keep_ref, got1_ref, got2_ref, near_ref, far_ref, own_ref):
    total = keep_ref[0].astype(F32) + got1_ref[got1_ref.shape[0] - 1].astype(F32) + got2_ref[0].astype(F32)
    total = total.astype(BF)
    if turned:
        total = jnp.transpose(total)
    size = 4
    block = total.shape[0 if turned else 1] // size
    for j in range(size):
        at = slice(j * block, (j + 1) * block)
        piece = total[at, :] if turned else total[:, at]
        mask = j ^ rank_ref[0]

        @pl.when(mask == 3)
        def _():
            near_ref[0] = piece

        @pl.when(mask == 1)
        def _():
            near_ref[1] = piece

        @pl.when(mask == 2)
        def _():
            far_ref[...] = piece

        @pl.when(mask == 0)
        def _():
            own_ref[...] = piece


def split(rank, keep, got1, got2, turned=False):
    rows, cols = keep.shape[1:]
    dims = (cols // 4, rows) if turned else (rows, cols // 4)
    return pl.pallas_call(
        functools.partial(split_kernel, turned),
        out_shape=(shape((2,) + dims), shape(dims), shape(dims)),
        in_specs=[SMEM, VMEM, VMEM, VMEM],
        out_specs=(VMEM,) * 3,
        compiler_params=params(),
        name="split",
    )(rank, keep, got1, got2)


def flip(x, axis, size, bit):
    return lax.ppermute(x, axis, [(i, i ^ bit) for i in range(size)])


def add(a, b):
    return (a.astype(F32) + b.astype(F32)).astype(BF)


def masks_of(bits):
    out = []
    for i in range(2 ** len(bits)):
        mask = 0
        for spot, bit in enumerate(bits):
            if not (i >> (len(bits) - 1 - spot)) & 1:
                mask |= bit
        out.append(mask)
    return out


def after(x, *others):
    return together(x, *others)[0]


def together(*values):
    leaves, tree = jax.tree.flatten(values)
    return jax.tree.unflatten(tree, lax.optimization_barrier(tuple(leaves)))


def exchange(blocks):
    return lax.all_to_all(blocks, "seq", split_axis=0, concat_axis=0, tiled=True)


def shards(
    tokens, modulation, image_ids, w_qkv, w_out, w_fc1, w_fc2, w_proj1, w_proj2, w_proj3, dino, cotangent,
):
    n_seq = lax.axis_size("seq")
    n_dp = lax.axis_size("dp")
    rank = lax.axis_index("seq")
    me = lax.axis_index("dp")
    tok_dev, width = tokens.shape
    group_tok = image_ids.shape[0]
    hidden, wide, narrow = w_fc1.shape[1], w_proj2.shape[0], w_proj3.shape[1]
    heads = H // n_seq
    local = heads * HD
    slots = modulation.shape[0]
    dp_bits = [1 << i for i in range(n_dp.bit_length() - 1)]
    rank_arg = rank.reshape(1).astype(jnp.int32)

    mods, *firsts = enter(image_ids, rank_arg, tokens, modulation)

    rights, lefts = [firsts], [firsts]
    for s in range(1, n_seq):
        up = [(i, i + 1) for i in range(s - 1, n_seq - 1)]
        low = [(i, i - 1) for i in range(1, n_seq - s + 1)]
        rights.append([lax.ppermute(v, "seq", up) for v in rights[-1]])
        lefts.append([lax.ppermute(v, "seq", low) for v in lefts[-1]])
    pieces = list(firsts)
    for d in range(1, n_seq):
        pieces += lefts[d] + rights[n_seq - d]

    columns = [lax.dynamic_slice_in_dim(w_qkv, i * width + rank * local, local, 1) for i in range(3)]
    w_rows = jnp.transpose(jnp.concatenate(columns, axis=1))
    w_pad = jnp.pad(w_rows.reshape(3 * heads, HD, width), ((0, 0), (0, HP - HD), (0, 0))).reshape(3 * heads * HP, width)
    ids_rel = lax.dynamic_slice_in_dim(jnp.concatenate([image_ids, image_ids]), rank * tok_dev, group_tok)
    idk, idq = ids_rel[:, None], ids_rel[None, :]
    one = (image_ids[0] == image_ids[group_tok - 1]).astype(jnp.int32).reshape(1)
    tile = group_tok // 4
    diagonal = tok_dev % tile == 0

    *heads_out, first_all, qkv, lse = attend_forward(
        one, rank_arg, pieces, w_pad, idk, idq, heads, tile, diagonal
    )
    attended = [heads_out[0]]
    for d in range(1, n_seq):
        attended.append(lax.ppermute(heads_out[d], "seq", [(i, (i + d) % n_seq) for i in range(n_seq)]))
    (rounded, act1, dr2, left1, right1, left2, gelu_slope, dmlp, dy, normed2, inv2, attn, sum_gate2) = middle(
        rank_arg, attended, tokens, mods, dino, cotangent, w_out, w_fc1, w_fc2, w_proj1, w_proj2, w_proj3
    )

    fast = all(k % (16 * n_dp) == 0 for k in (width, hidden, wide)) and n_dp == 8 and n_seq == 4

    def down(dmlp):
        return descend(n_seq, dmlp, gelu_slope, dy, normed2, inv2, attn, mods, w_fc2, w_fc1, w_out)

    def back(dos):
        return attend_backward(
            one, rank_arg, dos, qkv, heads_out, lse, w_rows, idk, idq, heads, tile, diagonal
        )

    def outgoing(g_heads, sums1):
        units = [g_heads[:, i * local : (i + 1) * local] for i in range(3)]
        rows = jnp.concatenate([sums1[0:2], sums2[0:3], sum_gate2], axis=0).astype(BF)
        rows = rows.reshape(n_seq, 6 * width // (n_seq * local), local)
        blocks = []
        for target in range(n_seq):
            mine = jnp.zeros_like(units[0])
            for i in range(3):
                mine = jnp.where((n_seq * i + rank) // 3 == target, units[i], mine)
            blocks.append(jnp.concatenate([mine, rows[target]], axis=0))
        return jnp.stack(blocks)

    if fast:
        swap = lambda x, bit: flip(x, "dp", n_dp, bit)
        core, x, y = dp_bits
        near = lambda v: flip(v, "seq", n_seq, 1)
        far = lambda v: flip(v, "seq", n_seq, 2)

        def job(base, deep, bits, column):
            starts = base + (me ^ jnp.array(masks_of(bits), jnp.int32)) * (deep // n_dp)
            return (starts, deep // n_dp, column)

        def right(v, step):
            return lax.ppermute(v, "seq", [(i, i + 1) for i in range(step)])

        def left(v, step):
            return lax.ppermute(v, "seq", [(i, i - 1) for i in range(n_seq - step, n_seq)])

        def row_starts(base, deep, bits):
            return base + (me ^ jnp.array(masks_of(bits), jnp.int32)) * (deep // n_dp)

        def row_starts(base, deep, bits):
            return base + (me ^ jnp.array(masks_of(bits), jnp.int32)) * (deep // n_dp)

        def last(*terms):
            return sum(v.astype(F32) for v in terms)

        quarter = (1, 1, 1, 1)
        lefts2, dmlps = [left2, swap(left2, core)], [dmlp, swap(dmlp, core)]
        act1_other, dr2_other = swap(act1, core), swap(dr2, core)
        right2, dhidden1, dheads, sums2 = down(dmlp)
        act1_other, dr2_other, lefts2, dmlps, left1, right1, right2, dheads = together(
            act1_other, dr2_other, lefts2, dmlps, left1, right1, right2, dheads
        )

        dheads_in = exchange(dheads)
        lefts1, rights1 = [left1, swap(left1, core)], [right1, swap(right1, core)]
        rights2 = [right2, swap(right2, core)]
        (p2,) = weight_grad([act1, act1_other], [dr2, dr2_other], [job(0, wide, (x, y), 0)], quarter, wide, STEP)
        (f2,) = weight_grad(lefts2, after(dmlps, p2), [job(0, hidden, (y, x), 0)], quarter, width, 384)
        p2, f2, lefts2, lefts1, rights1, rights2 = together(p2, f2, lefts2, lefts1, rights1, rights2)

        p2a, p2b, f2a = swap(p2[0], x), swap(p2[1], x), swap(f2[0], y)
        p1n, p1f, p1o = weight_grad_seq(
            lefts1, rights1, row_starts(wide, width, (y, x)), width // n_dp,
            rank ^ jnp.array(masks_of((1, 2)), jnp.int32), wide // n_seq,
        )
        p1z = near(p1n)
        (p3,) = weight_grad(
            lefts1, after(rights1, p1n), [job(0, wide, (y, x), wide // 256)], (2, 1, 1), narrow, 256
        )
        p3a = swap(p3[0], y)
        dqkv, dx = back(after(dheads_in, p3, p2a))
        f2s = add(f2[2], after(f2a, dqkv))
        p2, f2, p2a, p2b, f2s, p1f, p1o, p1z, p3, p3a, rights2, dqkv, dx = together(
            p2, f2, p2a, p2b, f2s, p1f, p1o, p1z, p3, p3a, rights2, dqkv, dx
        )

        f2c, f2b = swap(f2s, x), swap(f2[1], y)
        up, low = right(dx[3], 1), left(dx[1], 1)
        (f1,) = weight_grad(lefts2, rights2, [job(hidden, width, (x, y), 0)], quarter, hidden, 1152)
        p1y = far(add(p1f, p1z[0]))
        (fq,) = weight_grad(
            [first_all], [after(dqkv, f1)], [job(0, width, (core, y, x), 0)], (4, 2, 2), 3 * local, 3 * local,
            flat=True,
        )
        (fo,) = weight_grad(
            lefts2, after(rights2, fq), [job(hidden + width, width, (y, x), hidden // 384)], (2, 1, 1), width, 384
        )
        p2s, p3s, p1o = add(p2[2], p2a), add(p3[1], p3a[:1]), add(p1o, p1z[1])
        f2, f2c, f2b, up, low, p1y, p3s, f1, fq, fo, p2s, p1o = together(
            f2, f2c, f2b, up, low, p1y, p3s, f1, fq, fo, p2s, p1o
        )

        f1a, p2c = swap(f1[0], x), swap(p2s, y)
        up, low = right(add(dx[2], up), 2), left(add(dx[2], low), 2)
        fqa = swap(fq[0], core)
        f2n, f2f, f2o = split(rank_arg, after(f2[3], fqa), f2b, f2c, turned=True)
        f2z = near(f2n)
        p3c = swap(after(p3s, f2n), x)
        foa = swap(after(fo[0], p2c), y)
        p1d = add(p1o, p1y).reshape(4, width // n_dp, wide // n_seq)
        p2n, p2f, p2o = split(rank_arg, p2[3], p2b, p2c)
        up, low = add(dx[1], up), add(dx[3], low)
        f1s = add(f1[2], f1a)
        f1s, foa, fqa, p3c, p2n, p2f, p1d, f2z, f2f, up, low, f1 = together(
            f1s, foa, fqa, p3c, p2n, p2f, p1d, f2z, f2f, up, low, f1
        )

        f1b, f1c = swap(f1[1], x), swap(f1s, y)
        up, low = right(up, 3), left(low, 3)
        f2y = far(add(f2f, f2z[0]))
        p3n, p3f, p3o = split(rank_arg, p3[2], p3a, p3c, turned=True)
        p2z, foc = near(after(p2n, up, low)), swap(add(fo[1], after(foa, up, low)[:1]), x)
        fqb, fqk = swap(add(fq[1], after(fqa, up, low)[:2]), y), add(fq[2], fqa[2:])
        f1b, f1c, up, low, f2y, p2z, p2f, p3n, foc, fqb, fqk, p1d = together(
            f1b, f1c, up, low, f2y, p2z, p2f, p3n, foc, fqb, fqk, p1d
        )

        fqs, fqk = add(fqk[0], fqb[0]), add(fqk[1], fqb[1])
        fqc, p1e = swap(fqs, x), swap(p1d[0:2], y)
        p2y, p3z = far(add(p2f, p2z[0])), near(p3n)
        f1n, f1f, f1o = split(rank_arg, f1[3], f1b, f1c)
        f1z = near(f1n)
        fon, fof, foo = split(rank_arg, after(fo[2], f1n), foa, foc)
        foz = near(fon)
        grad_inputs, sums1 = leave(after(dx[0], fon, fqc), up, low, tokens, dhidden1, mods)
        fqk, fqc, sums1, p1e, f1z, f1f, p2y, p3z, foz, fof = together(
            fqk, fqc, sums1, p1e, f1z, f1f, p2y, p3z, foz, fof
        )

        f1s = add(f1f, f1z[0])
        f1y, p3y, foy = far(f1s), far(add(after(p3f, f1s), p3z[0])), far(add(after(fof, f1s), foz[0]))
        p1x = swap(add(after(p1d[2], f1s), p1e[0]), x)
        incoming = exchange(outgoing(add(fqk, after(fqc, f1s)), sums1))
        g_proj1 = last(p1d[3], p1e[1], p1x)
        g_proj2, g_fc1, g_fc2 = last(p2o, p2z[1], p2y), last(f1o, f1z[1], f1y), jnp.transpose(last(f2o, f2z[1], f2y))
        g_proj3, g_out = jnp.transpose(last(p3o, p3z[1], p3y)), last(foo, foz[1], foy)
    else:
        right2, dhidden1, dheads, sums2 = down(dmlp)
        dqkv, dx = back(exchange(dheads))
        up, low = None, None
        for s in range(1, n_seq):
            up = dx[n_seq - s] if up is None else add(dx[n_seq - s], up)
            low = dx[s] if low is None else add(dx[s], low)
            up = lax.ppermute(up, "seq", [(i, i + 1) for i in range(s)])
            low = lax.ppermute(low, "seq", [(i, i - 1) for i in range(n_seq - s, n_seq)])
        grad_inputs, sums1 = leave(dx[0], up, low, tokens, dhidden1, mods)

        def reduced(a, b):
            share = lax.psum_scatter(matmul(a, b).astype(BF), "dp", scatter_dimension=0, tiled=True)
            return lax.psum_scatter(share, "seq", scatter_dimension=1, tiled=True).astype(F32)

        g_proj3 = reduced(left1[:wide], right1[:, wide:])
        g_proj2 = reduced(act1, dr2)
        g_proj1 = reduced(left1[wide:], right1[:, :wide])
        g_fc2 = reduced(left2[:hidden], dmlp)
        g_fc1 = reduced(left2[hidden : hidden + width], right2[:, :hidden])
        g_out = reduced(left2[hidden + width :], right2[:, hidden:])
        g_heads = lax.psum_scatter(
            times_trans(first_all, dqkv).astype(BF), "dp", scatter_dimension=0, tiled=True
        )

    if not fast:
        incoming = exchange(outgoing(g_heads, sums1))
    held = width // n_dp
    slot = jnp.arange(slots, dtype=jnp.int32)[:, None, None]
    whose = image_ids[::tok_dev]
    dmods = incoming[:, held:].reshape(n_seq, 6 * width // n_seq).astype(F32)
    grad_mods = jnp.sum(jnp.where(slot == whose[None, :, None], dmods[None], 0.0), axis=1)
    incoming = incoming[:, :held]
    columns = [jnp.zeros(incoming.shape[1:], BF) for _ in range(3)]
    for source in range(n_seq):
        for i in range(3):
            unit = n_seq * i + source
            columns[unit % 3] = jnp.where(unit // 3 == rank, incoming[source], columns[unit % 3])
    g_qkv = jnp.concatenate(columns, axis=1).astype(F32)

    return (rounded, grad_inputs, grad_mods, g_qkv, g_out, g_fc1, g_fc2, g_proj1, g_proj2, g_proj3)


def solution(mesh):
    tok = P(("dp", "seq"), None)
    in_specs = (tok, P("dp", None), P("dp")) + (P(),) * 7 + (tok, tok)
    out_specs = (tok, tok) + (P("dp", "seq"),) * 8
    return jax.shard_map(shards, mesh=mesh, in_specs=in_specs, out_specs=out_specs, check_vma=False)
```

```python
import functools

import jax
import jax.numpy as jnp
from jax import lax
from jax.experimental import pallas as pl
from jax.experimental.pallas import tpu as pltpu
from jax.sharding import PartitionSpec as P

H = 16
HD = 72
HP = 80
LEN = 1024
EPS_NORM = 1e-06
SCALE = HD ** (-0.5)
EXP2_SCALE = SCALE * 1.4426950408889634
GELU_A = 0.7978845608028654
GELU_B = 0.044715
BF = jnp.bfloat16
F32 = jnp.float32
ANY = pl.BlockSpec(memory_space=pl.ANY)
VMEM = pl.BlockSpec(memory_space=pltpu.VMEM)
SMEM = pl.BlockSpec(memory_space=pltpu.SMEM)
ROOM = 60 << 20
PARTS = 2


def matmul(left, right):
    return jnp.dot(left, right, preferred_element_type=F32)


def times_trans(left, right):
    return lax.dot_general(left, right, (((1,), (1,)), ((), ())), preferred_element_type=F32)


def trans_times(left, right):
    return lax.dot_general(left, right, (((0,), (0,)), ((), ())), preferred_element_type=F32)


def row_mean(v):
    return jnp.mean(v, axis=-1, keepdims=True)


def normalize(v):
    centre = v - row_mean(v)
    inv = lax.rsqrt(row_mean(centre * centre) + EPS_NORM)
    return centre * inv, inv


def norm_back(e, normed, inv):
    return (e - row_mean(e) - normed * row_mean(e * normed)) * inv


def col_sum(v):
    return jnp.sum(v, axis=0, keepdims=True)


def sigmoid(v):
    return 1.0 / (1.0 + jnp.exp(-v))


def shape(dims, kind=BF):
    return jax.ShapeDtypeStruct(dims, kind)


def params(**more):
    return pltpu.CompilerParams(vmem_limit_bytes=ROOM, **more)


def enter_kernel(ids_ref, rank_ref, tokens_ref, mod_ref, mods_ref, *out_refs):
    width = tokens_ref.shape[1]
    table = mod_ref[...].astype(F32)
    mine = lax.broadcasted_iota(jnp.int32, table.shape, 0) == ids_ref[rank_ref[0] * tokens_ref.shape[0]]
    mods = col_sum(jnp.where(mine, table, 0.0))
    mods_ref[...] = jnp.zeros_like(mods_ref)
    for i in range(6):
        mods_ref[i : i + 1, :] = mods[:, i * width : (i + 1) * width]
    normed, _ = normalize(tokens_ref[...].astype(F32))
    first = normed * (1.0 + mods[:, width : 2 * width]) + mods[:, 0:width]
    first = jnp.transpose(first.astype(BF))
    rows = out_refs[0].shape[0]
    for i, out_ref in enumerate(out_refs):
        out_ref[...] = first[i * rows : (i + 1) * rows, :]


def enter(ids, rank, tokens, modulation):
    tok, width = tokens.shape
    return pl.pallas_call(
        enter_kernel,
        out_shape=(shape((8, width), F32),) + (shape((width // PARTS, tok)),) * PARTS,
        in_specs=[SMEM, SMEM, VMEM, VMEM],
        out_specs=(VMEM,) * (1 + PARTS),
        compiler_params=params(),
        name="enter",
    )(ids, rank, tokens, modulation)


def attend_forward_kernel(size, heads, tile, diagonal, one_ref, rank_ref, *refs):
    count = PARTS * (2 * size - 1)
    pieces = refs[:count]
    w_any, idk_ref, idq_ref = refs[count : count + 3]
    o_refs = refs[count + 3 : count + 3 + size]
    (x_any, qkv_any, lse_ref, x_ref, qkv_ref, w_ref, k_ref, o_all_ref, sem, w_sem, out_sem) = refs[count + 3 + size :]
    tok = pieces[0].shape[1]
    total = x_ref.shape[1]
    rows = pieces[0].shape[0]
    rank = rank_ref[0]
    w_copy = pltpu.make_async_copy(w_any, w_ref, w_sem.at[0])
    w_copy.start()

    def piece_copy(d, part, source):
        at = 0 if d == 0 else 2 * d - 2 + source
        return pltpu.make_async_copy(
            pieces[at * PARTS + part],
            x_ref.at[part * rows : (part + 1) * rows, d * tok : (d + 1) * tok],
            sem.at[d, part],
        )

    for part in range(PARTS):
        piece_copy(0, part, 0).start()
    for d in range(1, size):
        for part in range(PARTS):

            @pl.when(rank + d < size)
            def _():
                piece_copy(d, part, 1).start()

            @pl.when(rank + d >= size)
            def _():
                piece_copy(d, part, 2).start()

    w_copy.wait()
    for d in range(size):
        for part in range(PARTS):
            piece_copy(d, part, 1).wait()
        at = slice(d * tok, (d + 1) * tok)
        qkv_ref[:, at] = matmul(w_ref[...], x_ref[:, at]).astype(BF)
    out_copies = [
        pltpu.make_async_copy(x_ref, x_any, out_sem.at[0]),
        pltpu.make_async_copy(qkv_ref, qkv_any, out_sem.at[1]),
    ]
    for copy in out_copies:
        copy.start()

    def head_step(head, carry):
        q_at = pl.ds(pl.multiple_of(head * HP, HP), HP)
        k_at = pl.ds(pl.multiple_of((heads + head) * HP, HP), HP)
        v_at = pl.ds(pl.multiple_of((2 * heads + head) * HP, HP), HP)
        o_at = pl.ds(pl.multiple_of(head * HD, 8), HD)
        k_ref[...] = jnp.transpose(qkv_ref[k_at, :])

        def block(at, keys, masked):
            s = matmul(k_ref[keys, :], qkv_ref[q_at, at]) * EXP2_SCALE
            if masked:
                s = jnp.where(idk_ref[...] == idq_ref[:, at], s, -1e30)
            top = jnp.max(s, axis=0, keepdims=True)
            e = jnp.exp2(s - top)
            tot = col_sum(e)
            o = matmul(qkv_ref[v_at, keys], e.astype(BF)) * (1.0 / tot)
            o_all_ref[o_at, at] = o[0:HD, :]
            lse_ref[pl.ds(head, 1), at] = top + jnp.log2(tot)

        def full(masked):
            def step(i, inner):
                block(pl.ds(pl.multiple_of(i * tile, tile), tile), pl.ds(0, total), masked)
                return inner

            lax.fori_loop(0, total // tile, step, 0, unroll=True)

        @pl.when(one_ref[0] == 1)
        def _():
            full(False)

        @pl.when(one_ref[0] == 0)
        def _():
            if diagonal:

                def step(i, inner):
                    at = pl.ds(pl.multiple_of(i * tile, tile), tile)
                    block(at, at, False)
                    return inner

                lax.fori_loop(0, total // tile, step, 0, unroll=True)
            else:
                full(True)

        return carry

    lax.fori_loop(0, heads, head_step, 0)
    for d in range(size):
        o_refs[d][...] = o_all_ref[:, d * tok : (d + 1) * tok].astype(BF)
    for copy in out_copies:
        copy.wait()


def attend_forward(one, rank, pieces, w, idk, idq, heads, tile, diagonal):
    size = (len(pieces) // PARTS + 1) // 2
    tok = pieces[0].shape[1]
    width, total = PARTS * pieces[0].shape[0], size * tok
    return pl.pallas_call(
        functools.partial(attend_forward_kernel, size, heads, tile, diagonal),
        out_shape=(shape((heads * HD, tok)),) * size
        + (
            shape((width, total)),
            shape((3 * heads * HP, total)),
            shape((heads, total), F32),
        ),
        in_specs=[SMEM, SMEM] + [ANY] * (len(pieces) + 1) + [VMEM, VMEM],
        out_specs=(VMEM,) * size + (ANY, ANY, VMEM),
        scratch_shapes=[
            pltpu.VMEM((width, total), BF),
            pltpu.VMEM((3 * heads * HP, total), BF),
            pltpu.VMEM(w.shape, BF),
            pltpu.VMEM((total, HP), BF),
            pltpu.VMEM((heads * HD, total), F32),
            pltpu.SemaphoreType.DMA((size, PARTS)),
            pltpu.SemaphoreType.DMA((1,)),
            pltpu.SemaphoreType.DMA((2,)),
        ],
        compiler_params=params(),
        name="attend_forward",
    )(one, rank, *pieces, w, idk, idq)


def attend_backward_kernel(size, heads, tile, diagonal, one_ref, rank_ref, *refs):
    o_refs, refs = refs[:size], refs[size:]
    dos_ref, qkv_ref, lse_ref, w_ref, idk_ref, idq_ref = refs[:6]
    dqkv_ref, dx_ref, k_ref, v_ref, do_ref, dk_ref, dv_ref, acc_ref, delta_ref = refs[6:]
    tok = dos_ref.shape[2]
    total = qkv_ref.shape[1]
    local = heads * HD
    for d in range(size):
        at = slice(d * tok, (d + 1) * tok)
        owner = lax.rem(rank_ref[0] + d, size)
        do = dos_ref[owner].astype(F32)
        do_ref[0:local, at] = do
        do_ref[local : local + HP - HD, at] = jnp.zeros((HP - HD, tok), F32)
        prod = do * o_refs[d][...].astype(F32)
        for head in range(heads):
            delta_ref[head : head + 1, at] = col_sum(prod[head * HD : (head + 1) * HD, :])

    def head_step(head, carry):
        q_at = pl.ds(pl.multiple_of(head * HP, HP), HP)
        k_at = pl.ds(pl.multiple_of((heads + head) * HP, HP), HP)
        v_at = pl.ds(pl.multiple_of((2 * heads + head) * HP, HP), HP)
        o_at = pl.ds(pl.multiple_of(head * HD, 8), HP)
        k_ref[...] = jnp.transpose(qkv_ref[k_at, :])
        v_ref[...] = jnp.transpose(qkv_ref[v_at, :])

        def out_at(part):
            return pl.ds(pl.multiple_of(part * local + head * HD, 8), HD)

        def block(at, keys, masked, fresh):
            q = qkv_ref[q_at, at]
            do = do_ref[o_at, at].astype(BF)
            p = jnp.exp2(matmul(k_ref[keys, :], q) * EXP2_SCALE - lse_ref[pl.ds(head, 1), at])
            if masked:
                p = jnp.where(idk_ref[...] == idq_ref[:, at], p, 0.0)
            ds = (p * (matmul(v_ref[keys, :], do) - delta_ref[pl.ds(head, 1), at])).astype(BF)
            dv = times_trans(do, p.astype(BF))
            dk = times_trans(q, ds)
            if fresh:
                dv_ref[:, keys] = dv
                dk_ref[:, keys] = dk
            else:
                dv_ref[:, keys] += dv
                dk_ref[:, keys] += dk
            dq = matmul(qkv_ref[k_at, keys], ds) * SCALE
            acc_ref[out_at(0), at] = dq[0:HD, :]

        def full(masked):
            dk_ref[...] = jnp.zeros_like(dk_ref)
            dv_ref[...] = jnp.zeros_like(dv_ref)

            def step(i, inner):
                block(pl.ds(pl.multiple_of(i * tile, tile), tile), pl.ds(0, total), masked, False)
                return inner

            lax.fori_loop(0, total // tile, step, 0, unroll=True)

        @pl.when(one_ref[0] == 1)
        def _():
            full(False)

        @pl.when(one_ref[0] == 0)
        def _():
            if diagonal:

                def step(i, inner):
                    at = pl.ds(pl.multiple_of(i * tile, tile), tile)
                    block(at, at, False, True)
                    return inner

                lax.fori_loop(0, total // tile, step, 0, unroll=True)
            else:
                full(True)

        acc_ref[out_at(1), :] = dk_ref[0:HD, :] * SCALE
        acc_ref[out_at(2), :] = dv_ref[0:HD, :]
        return carry

    lax.fori_loop(0, heads, head_step, 0)
    dqkv_ref[...] = acc_ref[...].astype(BF)
    for d in range(size):
        dx_ref[d] = trans_times(dqkv_ref[:, d * tok : (d + 1) * tok], w_ref[...]).astype(BF)


def attend_backward(one, rank, dos, qkv, o, lse, w, idk, idq, heads, tile, diagonal):
    size, local, tok = dos.shape
    total = size * tok
    width = w.shape[1]
    return pl.pallas_call(
        functools.partial(attend_backward_kernel, size, heads, tile, diagonal),
        out_shape=(shape((3 * local, total)), shape((size, tok, width))),
        in_specs=[SMEM, SMEM] + [VMEM] * (size + 6),
        out_specs=(VMEM, VMEM),
        scratch_shapes=[
            pltpu.VMEM((total, HP), BF),
            pltpu.VMEM((total, HP), BF),
            pltpu.VMEM((local + HP - HD, total), F32),
            pltpu.VMEM((HP, total), F32),
            pltpu.VMEM((HP, total), F32),
            pltpu.VMEM((3 * local, total), F32),
            pltpu.VMEM((heads, total), F32),
        ],
        compiler_params=params(),
        name="attend_backward",
    )(one, rank, *o, dos, qkv, lse, w, idk, idq)


STEP = 512
UP_STEP = 768
PROJECT_STEP = 1024


def middle_kernel(size, rank_ref, *refs):
    o_refs, refs = refs[:size], refs[size:]
    (tokens_ref, mods_ref, dino_ref, cot_ref, wo_any, w1_any, w2_any, p1_any, p2_any, p3_any) = refs[:10]
    (out_any, a1_any, dr2_any, left1_any, right1_ref, left2_any, gp_any, dmlp_ref, dy_ref, normed_any, inv_ref, attn_any,
     gate_ref) = refs[10:23]
    (wo_ref, w1_ref, w2_ref, p1_ref, p2_ref, p3_ref, act_ref, out_ref, a1_ref, dr2_ref, left1_ref, left2_ref, gp_ref,
     normed_ref, attn_ref, w1_sem, sems, out_sems) = refs[23:]
    flushes = []

    def flush(source, target):
        copy = pltpu.make_async_copy(source, target, out_sems.at[len(flushes)])
        copy.start()
        flushes.append(copy)

    local, tok = o_refs[0].shape
    width = size * local
    hidden = w1_any.shape[1]
    wide, narrow = p3_ref.shape
    steps = hidden // UP_STEP
    slots = w1_ref.shape[0]
    a2_ref, y_ref = left1_ref.at[0:wide, :], left1_ref.at[wide:, :]
    g_ref, b_ref = left2_ref.at[0:hidden, :], left2_ref.at[hidden : hidden + width, :]
    o_ref = left2_ref.at[hidden + width :, :]
    dr1_ref, dz_ref = right1_ref.at[:, 0:wide], right1_ref.at[:, wide:]
    wo_copy = pltpu.make_async_copy(wo_any, wo_ref, sems.at[4])
    wo_copy.start()

    def w1_copy(i):
        at = pl.ds(pl.multiple_of(i * UP_STEP, UP_STEP), UP_STEP)
        slot = lax.rem(i, slots)
        return pltpu.make_async_copy(w1_any.at[:, at], w1_ref.at[slot], w1_sem.at[slot])

    for i in range(slots):
        w1_copy(i).start()
    w2_copy = pltpu.make_async_copy(w2_any, w2_ref, sems.at[0])
    p1_copy = pltpu.make_async_copy(p1_any, p1_ref, sems.at[1])
    p2_copy = pltpu.make_async_copy(p2_any, p2_ref, sems.at[2])
    p3_copy = pltpu.make_async_copy(p3_any, p3_ref, sems.at[3])
    for copy in (w2_copy, p1_copy, p2_copy, p3_copy):
        copy.start()

    gate1, shift2, scale2, gate2 = [mods_ref[i : i + 1, :] for i in (2, 3, 4, 5)]
    for d in range(size):
        owner = lax.rem(rank_ref[0] + size - d, size)
        o_ref[pl.ds(pl.multiple_of(owner * local, 16), local), :] = o_refs[d][...]
    wo_copy.wait()
    attn = trans_times(o_ref[...], wo_ref[...])
    attn_ref[...] = attn
    flush(attn_ref, attn_any)
    h1 = tokens_ref[...].astype(F32) + gate1 * attn
    normed, inv = normalize(h1)
    normed_ref[...] = normed
    flush(normed_ref, normed_any)
    inv_ref[...] = inv
    b = (normed * (1.0 + scale2) + shift2).astype(BF)
    b_ref[...] = jnp.transpose(b)

    def up(i, carry):
        at = pl.ds(pl.multiple_of(i * UP_STEP, UP_STEP), UP_STEP)
        w1_copy(i).wait()
        u = matmul(b, w1_ref[lax.rem(i, slots)])

        @pl.when(i + slots < steps)
        def _():
            w1_copy(i + slots).start()

        sq = u * u
        t = jnp.tanh(u * (GELU_A + (GELU_A * GELU_B) * sq))
        half = 0.5 * (1.0 + t)
        g = (u * half).astype(BF)
        gp_ref[:, at] = (half + u * (1.0 - t * t) * (0.5 * GELU_A + (1.5 * GELU_A * GELU_B) * sq)).astype(BF)
        act_ref[:, at] = g
        g_ref[at, :] = jnp.transpose(g)
        return carry

    lax.fori_loop(0, steps, up, 0, unroll=True)
    flush(left2_ref, left2_any)
    flush(gp_ref, gp_any)
    w2_copy.wait()
    mlp = matmul(act_ref[...], w2_ref[...])
    y = (h1 + gate2 * mlp).astype(BF)
    out_ref[...] = y
    flush(out_ref, out_any)
    y_ref[...] = jnp.transpose(y)
    def project(source, w_ref, held, out_t_ref, slope_ref):
        def step(i, carry):
            at = pl.ds(pl.multiple_of(i * PROJECT_STEP, PROJECT_STEP), PROJECT_STEP)
            r = matmul(source, w_ref[:, at])
            sig = sigmoid(r)
            act = (r * sig).astype(BF)
            act_ref[:, pl.ds(pl.multiple_of(held + i * PROJECT_STEP, PROJECT_STEP), PROJECT_STEP)] = act
            out_t_ref[at, :] = jnp.transpose(act)
            slope_ref[:, at] = (sig * (1.0 + r * (1.0 - sig))).astype(BF)
            return carry

        lax.fori_loop(0, wide // PROJECT_STEP, step, 0, unroll=True)
        return act_ref[:, held : held + wide]

    def project_back(source, w_ref, slope_ref):
        def step(i, carry):
            at = pl.ds(pl.multiple_of(i * PROJECT_STEP, PROJECT_STEP), PROJECT_STEP)
            slope_ref[:, at] = (times_trans(source, w_ref[at, :]) * slope_ref[:, at].astype(F32)).astype(BF)
            return carry

        lax.fori_loop(0, wide // PROJECT_STEP, step, 0, unroll=True)
        return slope_ref[...]

    p1_copy.wait()
    a1 = project(y, p1_ref, 0, a1_ref, dr1_ref)
    flush(a1_ref, a1_any)
    p2_copy.wait()
    a2 = project(a1, p2_ref, wide, a2_ref, dr2_ref)
    flush(left1_ref, left1_any)
    p3_copy.wait()
    z = matmul(a2, p3_ref[...])
    t = dino_ref[...].astype(F32)
    nz = lax.rsqrt(jnp.sum(z * z, axis=-1, keepdims=True) + EPS_NORM)
    nt = lax.rsqrt(jnp.sum(t * t, axis=-1, keepdims=True) + EPS_NORM)
    cosine = jnp.sum(z * t, axis=-1, keepdims=True) * nz * nt
    dz = (-0.5 * (t * (nz * nt) - (cosine * nz * nz) * z)).astype(BF)
    dz_ref[...] = dz
    dr2 = project_back(dz, p3_ref, dr2_ref)
    flush(dr2_ref, dr2_any)
    dr1 = project_back(dr2, p2_ref, dr1_ref)
    dy = cot_ref[...].astype(F32) + times_trans(dr1, p1_ref[...])
    dy_ref[...] = dy
    dmlp_ref[...] = (gate2 * dy).astype(BF)
    gate_ref[...] = col_sum(dy * mlp)
    for copy in flushes:
        copy.wait()


def middle(rank, os, tokens, mods, dino, cot, wo, w1, w2, p1, p2, p3):
    tok, width = tokens.shape
    hidden, wide, narrow = w1.shape[1], p1.shape[1], p3.shape[1]
    return pl.pallas_call(
        functools.partial(middle_kernel, len(os)),
        out_shape=(
            shape((tok, width)), shape((wide, tok)), shape((tok, wide)), shape((wide + width, tok)),
            shape((tok, wide + narrow)), shape((hidden + 2 * width, tok)), shape((tok, hidden)), shape((tok, width)), shape((tok, width), F32),
            shape((tok, width), F32), shape((tok, 1), F32), shape((tok, width), F32), shape((1, width), F32),
        ),
        in_specs=[SMEM] + [VMEM] * (len(os) + 4) + [ANY] * 6,
        out_specs=(ANY, ANY, ANY, ANY, VMEM, ANY, ANY, VMEM, VMEM, ANY, VMEM, ANY, VMEM),
        scratch_shapes=[
            pltpu.VMEM(dims, BF)
            for dims in (wo.shape, (3, width, UP_STEP), w2.shape, p1.shape, p2.shape, p3.shape, (tok, hidden))
        ]
        + [
            pltpu.VMEM(dims, kind)
            for dims, kind in (
                ((tok, width), BF), ((wide, tok), BF), ((tok, wide), BF), ((wide + width, tok), BF),
                ((hidden + 2 * width, tok), BF), ((tok, hidden), BF), ((tok, width), F32), ((tok, width), F32),
            )
        ]
        + [pltpu.SemaphoreType.DMA((3,)), pltpu.SemaphoreType.DMA((5,)), pltpu.SemaphoreType.DMA((8,))],
        compiler_params=params(),
        name="middle",
    )(rank, *os, tokens, mods, dino, cot, wo, w1, w2, p1, p2, p3)


def descend_kernel(size, *refs):
    (dmlp_ref, gp_any, dy_any, normed_any, inv_ref, attn_any, mods_ref, w2_any, w1_any, wo_any) = refs[:10]
    (right2_ref, dh1_ref, do_ref, sums_ref) = refs[10:14]
    (w2_ref, w1_ref, wo_ref, gp_ref, dy_ref, normed_ref, attn_ref, w2_sem, w1_sem, wo_sem, in_sem) = refs[14:]
    hidden = w1_ref.shape[1]
    du_ref, dattn_ref = right2_ref.at[:, 0:hidden], right2_ref.at[:, hidden:]
    local = do_ref.shape[1]
    steps = hidden // STEP

    def w2_copy(i):
        at = pl.ds(pl.multiple_of(i * STEP, STEP), STEP)
        return pltpu.make_async_copy(w2_any.at[at, :], w2_ref.at[at, :], w2_sem.at[i])

    in_copies = [
        pltpu.make_async_copy(source, held, in_sem.at[i])
        for i, (source, held) in enumerate(
            ((gp_any, gp_ref), (dy_any, dy_ref), (normed_any, normed_ref), (attn_any, attn_ref))
        )
    ]
    in_copies[0].start()
    for i in range(steps):
        w2_copy(i).start()
    w1_copy = pltpu.make_async_copy(w1_any, w1_ref, w1_sem.at[0])
    w1_copy.start()
    wo_copy = pltpu.make_async_copy(wo_any, wo_ref, wo_sem.at[0])
    wo_copy.start()
    for copy in in_copies[1:]:
        copy.start()
    in_copies[0].wait()
    dmlp = dmlp_ref[...]

    def down(i, carry):
        at = pl.ds(pl.multiple_of(i * STEP, STEP), STEP)
        w2_copy(i).wait()
        du_ref[:, at] = (times_trans(dmlp, w2_ref[at, :]) * gp_ref[:, at].astype(F32)).astype(BF)
        return carry

    lax.fori_loop(0, steps, down, 0, unroll=True)
    w1_copy.wait()
    for copy in in_copies[1:]:
        copy.wait()
    db = times_trans(du_ref[...], w1_ref[...])
    gate1, scale2 = mods_ref[2:3, :], mods_ref[4:5, :]
    normed = normed_ref[...]
    dh1 = dy_ref[...] + norm_back(db * (1.0 + scale2), normed, inv_ref[...])
    dh1_ref[...] = dh1
    dattn = (gate1 * dh1).astype(BF)
    dattn_ref[...] = dattn
    sums_ref[...] = jnp.zeros_like(sums_ref)
    sums_ref[0:1, :] = col_sum(dh1 * attn_ref[...])
    sums_ref[1:2, :] = col_sum(db)
    sums_ref[2:3, :] = col_sum(db * normed)
    wo_copy.wait()
    for d in range(size):
        do_ref[d] = times_trans(wo_ref[d * local : (d + 1) * local, :], dattn).astype(BF)


def descend(size, dmlp, gp, dy, normed, inv, attn, mods, w2, w1, wo):
    tok, width = dmlp.shape
    hidden = w1.shape[1]
    return pl.pallas_call(
        functools.partial(descend_kernel, size),
        out_shape=(
            shape((tok, hidden + width)), shape((tok, width), F32),
            shape((size, width // size, tok)), shape((8, width), F32),
        ),
        in_specs=[VMEM, ANY, ANY, ANY, VMEM, ANY, VMEM] + [ANY] * 3,
        out_specs=(VMEM,) * 4,
        scratch_shapes=[pltpu.VMEM(w.shape, BF) for w in (w2, w1, wo, gp)]
        + [pltpu.VMEM(v.shape, F32) for v in (dy, normed, attn)]
        + [
            pltpu.SemaphoreType.DMA((hidden // STEP,)),
            pltpu.SemaphoreType.DMA((1,)),
            pltpu.SemaphoreType.DMA((1,)),
            pltpu.SemaphoreType.DMA((4,)),
        ],
        compiler_params=params(),
        name="descend",
    )(dmlp, gp, dy, normed, inv, attn, mods, w2, w1, wo)


def leave_kernel(part_ref, left_ref, right_ref, tokens_ref, dh1_ref, mods_ref, out_ref, sums_ref):
    da = part_ref[...].astype(F32) + left_ref[...].astype(F32) + right_ref[...].astype(F32)
    normed, inv = normalize(tokens_ref[...].astype(F32))
    out_ref[...] = (dh1_ref[...] + norm_back(da * (1.0 + mods_ref[1:2, :]), normed, inv)).astype(BF)
    sums_ref[...] = jnp.zeros_like(sums_ref)
    sums_ref[0:1, :] = col_sum(da)
    sums_ref[1:2, :] = col_sum(da * normed)


def leave(part, from_left, from_right, tokens, dh1, mods):
    return pl.pallas_call(
        leave_kernel,
        out_shape=(shape(tokens.shape), shape((8, tokens.shape[1]), F32)),
        in_specs=[VMEM] * 6,
        out_specs=(VMEM, VMEM),
        compiler_params=params(),
        name="leave",
    )(part, from_left, from_right, tokens, dh1, mods)


def weight_grad_kernel(count, flat, rows, packs, rows_ref, *refs):
    lefts = refs[:count]
    rights = refs[count : count * (1 + len(rows))]
    outs = refs[count * (1 + len(rows)) : -2]
    held_ref, sem = refs[-2:]
    blocks = sum(packs)
    part = lefts[0].shape[1]
    copies, held_at, held = [], [], 0
    for job, deep in enumerate(rows):
        held_at.append(held)
        for i in range(blocks):
            at = pl.ds(pl.multiple_of(rows_ref[job * blocks + i], 16), deep)
            for j in range(count):
                copies.append(
                    pltpu.make_async_copy(
                        lefts[j].at[at, :],
                        held_ref.at[held : held + deep, j * part : (j + 1) * part],
                        sem.at[len(copies)],
                    )
                )
            held += deep

    @pl.when(pl.program_id(0) == 0)
    def _():
        for copy in copies:
            copy.start()
        for copy in copies:
            copy.wait()

    dot = times_trans if flat else matmul
    for job, deep in enumerate(rows):
        base = held_at[job]
        for spot, pack in enumerate(packs):
            out_ref = outs[job * len(packs) + spot]
            total = None
            for j in range(count):
                term = dot(
                    held_ref[base : base + pack * deep, j * part : (j + 1) * part], rights[job * count + j][...]
                )
                total = term if total is None else total + term
            out_ref[...] = total.reshape(out_ref.shape).astype(BF)
            base += pack * deep


def weight_grad(lefts, rights, jobs, packs, wide, step, flat=False):
    count = len(lefts)
    part = lefts[0].shape[1]
    rows = tuple(job[1] for job in jobs)

    def right_spec(base):
        if flat:
            return pl.BlockSpec((step, part), lambda i, b: (i + base, 0))
        return pl.BlockSpec((part, step), lambda i, b: (0, i + base))

    outs = pl.pallas_call(
        functools.partial(weight_grad_kernel, count, flat, rows, packs),
        out_shape=tuple(shape((pack, deep, wide)) for deep in rows for pack in packs),
        grid_spec=pltpu.PrefetchScalarGridSpec(
            num_scalar_prefetch=1,
            grid=(wide // step,),
            in_specs=[ANY] * count + [right_spec(job[2]) for job in jobs for _ in range(count)],
            out_specs=tuple(
                pl.BlockSpec((pack, deep, step), lambda i, b: (0, 0, i)) for deep in rows for pack in packs
            ),
            scratch_shapes=[
                pltpu.VMEM((sum(packs) * sum(rows), part * count), BF),
                pltpu.SemaphoreType.DMA((sum(packs) * count * len(rows),)),
            ],
        ),
        compiler_params=params(dimension_semantics=("arbitrary",)),
        name="weight_grad",
    )(jnp.concatenate([job[0] for job in jobs]), *lefts, *(list(rights) * len(jobs)))
    return [outs[i * len(packs) : (i + 1) * len(packs)] for i in range(len(jobs))]


def weight_grad_seq_kernel(count, rows, order_ref, *refs):
    lefts, rights = refs[:count], refs[count : 2 * count]
    near_ref, far_ref, own_ref, held_ref, sem = refs[2 * count :]
    blocks = held_ref.shape[0] // rows
    part = lefts[0].shape[1]
    step = pl.program_id(0)
    copies = [
        pltpu.make_async_copy(
            lefts[j].at[pl.ds(pl.multiple_of(order_ref[4 + i], 16), rows), :],
            held_ref.at[i * rows : (i + 1) * rows, j * part : (j + 1) * part],
            sem.at[i * count + j],
        )
        for i in range(blocks)
        for j in range(count)
    ]

    @pl.when(step == 0)
    def _():
        for copy in copies:
            copy.start()
        for copy in copies:
            copy.wait()

    total = None
    for j in range(count):
        term = matmul(held_ref[:, j * part : (j + 1) * part], rights[j][...])
        total = term if total is None else total + term
    total = total.astype(BF)

    @pl.when(step < 2)
    def _():
        near_ref[0] = total

    @pl.when(step == 2)
    def _():
        far_ref[...] = total

    @pl.when(step == 3)
    def _():
        own_ref[...] = total


def weight_grad_seq(lefts, rights, row_starts, rows, columns, step):
    count = len(lefts)
    part = lefts[0].shape[1]
    blocks = row_starts.shape[0]
    return pl.pallas_call(
        functools.partial(weight_grad_seq_kernel, count, rows),
        out_shape=(shape((2, blocks * rows, step)), shape((blocks * rows, step)), shape((blocks * rows, step))),
        grid_spec=pltpu.PrefetchScalarGridSpec(
            num_scalar_prefetch=1,
            grid=(4,),
            in_specs=[ANY] * count + [pl.BlockSpec((part, step), lambda i, b: (0, b[i]))] * count,
            out_specs=(
                pl.BlockSpec((1, blocks * rows, step), lambda i, b: (jnp.minimum(i, 1), 0, 0)),
                pl.BlockSpec((blocks * rows, step), lambda i, b: (0, 0)),
                pl.BlockSpec((blocks * rows, step), lambda i, b: (0, 0)),
            ),
            scratch_shapes=[
                pltpu.VMEM((blocks * rows, part * count), BF),
                pltpu.SemaphoreType.DMA((blocks * count,)),
            ],
        ),
        compiler_params=params(dimension_semantics=("arbitrary",)),
        name="weight_grad_seq",
    )(jnp.concatenate([columns, row_starts]), *lefts, *rights)


def split_kernel(turned, rank_ref, keep_ref, got1_ref, got2_ref, near_ref, far_ref, own_ref):
    total = keep_ref[0].astype(F32) + got1_ref[got1_ref.shape[0] - 1].astype(F32) + got2_ref[0].astype(F32)
    total = total.astype(BF)
    if turned:
        total = jnp.transpose(total)
    size = 4
    block = total.shape[0 if turned else 1] // size
    for j in range(size):
        at = slice(j * block, (j + 1) * block)
        piece = total[at, :] if turned else total[:, at]
        mask = j ^ rank_ref[0]

        @pl.when(mask == 3)
        def _():
            near_ref[0] = piece

        @pl.when(mask == 1)
        def _():
            near_ref[1] = piece

        @pl.when(mask == 2)
        def _():
            far_ref[...] = piece

        @pl.when(mask == 0)
        def _():
            own_ref[...] = piece


def split(rank, keep, got1, got2, turned=False):
    rows, cols = keep.shape[1:]
    dims = (cols // 4, rows) if turned else (rows, cols // 4)
    return pl.pallas_call(
        functools.partial(split_kernel, turned),
        out_shape=(shape((2,) + dims), shape(dims), shape(dims)),
        in_specs=[SMEM, VMEM, VMEM, VMEM],
        out_specs=(VMEM,) * 3,
        compiler_params=params(),
        name="split",
    )(rank, keep, got1, got2)


def flip(x, axis, size, bit):
    return lax.ppermute(x, axis, [(i, i ^ bit) for i in range(size)])


def add(a, b):
    return (a.astype(F32) + b.astype(F32)).astype(BF)


def masks_of(bits):
    out = []
    for i in range(2 ** len(bits)):
        mask = 0
        for spot, bit in enumerate(bits):
            if not (i >> (len(bits) - 1 - spot)) & 1:
                mask |= bit
        out.append(mask)
    return out


def after(x, *others):
    return together(x, *others)[0]


def together(*values):
    leaves, tree = jax.tree.flatten(values)
    return jax.tree.unflatten(tree, lax.optimization_barrier(tuple(leaves)))


def exchange(blocks):
    return lax.all_to_all(blocks, "seq", split_axis=0, concat_axis=0, tiled=True)


def shards(
    tokens, modulation, image_ids, w_qkv, w_out, w_fc1, w_fc2, w_proj1, w_proj2, w_proj3, dino, cotangent,
):
    n_seq = lax.axis_size("seq")
    n_dp = lax.axis_size("dp")
    rank = lax.axis_index("seq")
    me = lax.axis_index("dp")
    tok_dev, width = tokens.shape
    group_tok = image_ids.shape[0]
    hidden, wide, narrow = w_fc1.shape[1], w_proj2.shape[0], w_proj3.shape[1]
    heads = H // n_seq
    local = heads * HD
    slots = modulation.shape[0]
    dp_bits = [1 << i for i in range(n_dp.bit_length() - 1)]
    rank_arg = rank.reshape(1).astype(jnp.int32)

    mods, *firsts = enter(image_ids, rank_arg, tokens, modulation)

    rights, lefts = [firsts], [firsts]
    for s in range(1, n_seq):
        up = [(i, i + 1) for i in range(s - 1, n_seq - 1)]
        low = [(i, i - 1) for i in range(1, n_seq - s + 1)]
        rights.append([lax.ppermute(v, "seq", up) for v in rights[-1]])
        lefts.append([lax.ppermute(v, "seq", low) for v in lefts[-1]])
    pieces = list(firsts)
    for d in range(1, n_seq):
        pieces += lefts[d] + rights[n_seq - d]

    columns = [lax.dynamic_slice_in_dim(w_qkv, i * width + rank * local, local, 1) for i in range(3)]
    w_rows = jnp.transpose(jnp.concatenate(columns, axis=1))
    w_pad = jnp.pad(w_rows.reshape(3 * heads, HD, width), ((0, 0), (0, HP - HD), (0, 0))).reshape(3 * heads * HP, width)
    ids_rel = lax.dynamic_slice_in_dim(jnp.concatenate([image_ids, image_ids]), rank * tok_dev, group_tok)
    idk, idq = ids_rel[:, None], ids_rel[None, :]
    one = (image_ids[0] == image_ids[group_tok - 1]).astype(jnp.int32).reshape(1)
    tile = group_tok // 4
    diagonal = tok_dev % tile == 0

    *heads_out, first_all, qkv, lse = attend_forward(
        one, rank_arg, pieces, w_pad, idk, idq, heads, tile, diagonal
    )
    attended = [heads_out[0]]
    for d in range(1, n_seq):
        attended.append(lax.ppermute(heads_out[d], "seq", [(i, (i + d) % n_seq) for i in range(n_seq)]))
    (rounded, act1, dr2, left1, right1, left2, gelu_slope, dmlp, dy, normed2, inv2, attn, sum_gate2) = middle(
        rank_arg, attended, tokens, mods, dino, cotangent, w_out, w_fc1, w_fc2, w_proj1, w_proj2, w_proj3
    )

    fast = all(k % (16 * n_dp) == 0 for k in (width, hidden, wide)) and n_dp == 8 and n_seq == 4

    def down(dmlp):
        return descend(n_seq, dmlp, gelu_slope, dy, normed2, inv2, attn, mods, w_fc2, w_fc1, w_out)

    def back(dos):
        return attend_backward(
            one, rank_arg, dos, qkv, heads_out, lse, w_rows, idk, idq, heads, tile, diagonal
        )

    def outgoing(g_heads, sums1):
        units = [g_heads[:, i * local : (i + 1) * local] for i in range(3)]
        rows = jnp.concatenate([sums1[0:2], sums2[0:3], sum_gate2], axis=0).astype(BF)
        rows = rows.reshape(n_seq, 6 * width // (n_seq * local), local)
        blocks = []
        for target in range(n_seq):
            mine = jnp.zeros_like(units[0])
            for i in range(3):
                mine = jnp.where((n_seq * i + rank) // 3 == target, units[i], mine)
            blocks.append(jnp.concatenate([mine, rows[target]], axis=0))
        return jnp.stack(blocks)

    if fast:
        swap = lambda x, bit: flip(x, "dp", n_dp, bit)
        core, x, y = dp_bits
        near = lambda v: flip(v, "seq", n_seq, 1)
        far = lambda v: flip(v, "seq", n_seq, 2)

        def job(base, deep, bits, column):
            starts = base + (me ^ jnp.array(masks_of(bits), jnp.int32)) * (deep // n_dp)
            return (starts, deep // n_dp, column)

        def right(v, step):
            return lax.ppermute(v, "seq", [(i, i + 1) for i in range(step)])

        def left(v, step):
            return lax.ppermute(v, "seq", [(i, i - 1) for i in range(n_seq - step, n_seq)])

        def row_starts(base, deep, bits):
            return base + (me ^ jnp.array(masks_of(bits), jnp.int32)) * (deep // n_dp)

        def row_starts(base, deep, bits):
            return base + (me ^ jnp.array(masks_of(bits), jnp.int32)) * (deep // n_dp)

        def last(*terms):
            return sum(v.astype(F32) for v in terms)

        quarter = (1, 1, 1, 1)
        lefts2, dmlps = [left2, swap(left2, core)], [dmlp, swap(dmlp, core)]
        act1_other, dr2_other = swap(act1, core), swap(dr2, core)
        right2, dhidden1, dheads, sums2 = down(dmlp)
        act1_other, dr2_other, lefts2, dmlps, left1, right1, right2, dheads = together(
            act1_other, dr2_other, lefts2, dmlps, left1, right1, right2, dheads
        )

        dheads_in = exchange(dheads)
        lefts1, rights1 = [left1, swap(left1, core)], [right1, swap(right1, core)]
        rights2 = [right2, swap(right2, core)]
        (p2,) = weight_grad([act1, act1_other], [dr2, dr2_other], [job(0, wide, (x, y), 0)], quarter, wide, STEP)
        (f2,) = weight_grad(lefts2, after(dmlps, p2), [job(0, hidden, (y, x), 0)], quarter, width, 384)
        p2, f2, lefts2, lefts1, rights1, rights2 = together(p2, f2, lefts2, lefts1, rights1, rights2)

        p2a, p2b, f2a = swap(p2[0], x), swap(p2[1], x), swap(f2[0], y)
        p1n, p1f, p1o = weight_grad_seq(
            lefts1, rights1, row_starts(wide, width, (y, x)), width // n_dp,
            rank ^ jnp.array(masks_of((1, 2)), jnp.int32), wide // n_seq,
        )
        p1z = near(p1n)
        (p3,) = weight_grad(
            lefts1, after(rights1, p1n), [job(0, wide, (y, x), wide // 256)], (2, 1, 1), narrow, 256
        )
        p3a = swap(p3[0], y)
        dqkv, dx = back(after(dheads_in, p3, p2a))
        f2s = add(f2[2], after(f2a, dqkv))
        p2, f2, p2a, p2b, f2s, p1f, p1o, p1z, p3, p3a, rights2, dqkv, dx = together(
            p2, f2, p2a, p2b, f2s, p1f, p1o, p1z, p3, p3a, rights2, dqkv, dx
        )

        f2c, f2b = swap(f2s, x), swap(f2[1], y)
        up, low = right(dx[3], 1), left(dx[1], 1)
        (f1,) = weight_grad(lefts2, rights2, [job(hidden, width, (x, y), 0)], quarter, hidden, 1152)
        p1y = far(add(p1f, p1z[0]))
        (fq,) = weight_grad(
            [first_all], [after(dqkv, f1)], [job(0, width, (core, y, x), 0)], (4, 2, 2), 3 * local, 3 * local,
            flat=True,
        )
        (fo,) = weight_grad(
            lefts2, after(rights2, fq), [job(hidden + width, width, (y, x), hidden // 384)], (2, 1, 1), width, 384
        )
        p2s, p3s, p1o = add(p2[2], p2a), add(p3[1], p3a[:1]), add(p1o, p1z[1])
        f2, f2c, f2b, up, low, p1y, p3s, f1, fq, fo, p2s, p1o = together(
            f2, f2c, f2b, up, low, p1y, p3s, f1, fq, fo, p2s, p1o
        )

        f1a, p2c = swap(f1[0], x), swap(p2s, y)
        up, low = right(add(dx[2], up), 2), left(add(dx[2], low), 2)
        fqa = swap(fq[0], core)
        f2n, f2f, f2o = split(rank_arg, after(f2[3], fqa), f2b, f2c, turned=True)
        f2z = near(f2n)
        p3c = swap(after(p3s, f2n), x)
        foa = swap(after(fo[0], p2c), y)
        p1d = add(p1o, p1y).reshape(4, width // n_dp, wide // n_seq)
        p2n, p2f, p2o = split(rank_arg, p2[3], p2b, p2c)
        up, low = add(dx[1], up), add(dx[3], low)
        f1s = add(f1[2], f1a)
        f1s, foa, fqa, p3c, p2n, p2f, p1d, f2z, f2f, up, low, f1 = together(
            f1s, foa, fqa, p3c, p2n, p2f, p1d, f2z, f2f, up, low, f1
        )

        f1b, f1c = swap(f1[1], x), swap(f1s, y)
        up, low = right(up, 3), left(low, 3)
        f2y = far(add(f2f, f2z[0]))
        p3n, p3f, p3o = split(rank_arg, p3[2], p3a, p3c, turned=True)
        p2z, foc = near(after(p2n, up, low)), swap(add(fo[1], after(foa, up, low)[:1]), x)
        fqb, fqk = swap(add(fq[1], after(fqa, up, low)[:2]), y), add(fq[2], fqa[2:])
        f1b, f1c, up, low, f2y, p2z, p2f, p3n, foc, fqb, fqk, p1d = together(
            f1b, f1c, up, low, f2y, p2z, p2f, p3n, foc, fqb, fqk, p1d
        )

        fqs, fqk = add(fqk[0], fqb[0]), add(fqk[1], fqb[1])
        fqc, p1e = swap(fqs, x), swap(p1d[0:2], y)
        p2y, p3z = far(add(p2f, p2z[0])), near(p3n)
        f1n, f1f, f1o = split(rank_arg, f1[3], f1b, f1c)
        f1z = near(f1n)
        fon, fof, foo = split(rank_arg, after(fo[2], f1n), foa, foc)
        foz = near(fon)
        grad_inputs, sums1 = leave(after(dx[0], fon, fqc), up, low, tokens, dhidden1, mods)
        fqk, fqc, sums1, p1e, f1z, f1f, p2y, p3z, foz, fof = together(
            fqk, fqc, sums1, p1e, f1z, f1f, p2y, p3z, foz, fof
        )

        f1s = add(f1f, f1z[0])
        f1y, p3y, foy = far(f1s), far(add(after(p3f, f1s), p3z[0])), far(add(after(fof, f1s), foz[0]))
        p1x = swap(add(after(p1d[2], f1s), p1e[0]), x)
        incoming = exchange(outgoing(add(fqk, after(fqc, f1s)), sums1))
        g_proj1 = last(p1d[3], p1e[1], p1x)
        g_proj2, g_fc1, g_fc2 = last(p2o, p2z[1], p2y), last(f1o, f1z[1], f1y), jnp.transpose(last(f2o, f2z[1], f2y))
        g_proj3, g_out = jnp.transpose(last(p3o, p3z[1], p3y)), last(foo, foz[1], foy)
    else:
        right2, dhidden1, dheads, sums2 = down(dmlp)
        dqkv, dx = back(exchange(dheads))
        up, low = None, None
        for s in range(1, n_seq):
            up = dx[n_seq - s] if up is None else add(dx[n_seq - s], up)
            low = dx[s] if low is None else add(dx[s], low)
            up = lax.ppermute(up, "seq", [(i, i + 1) for i in range(s)])
            low = lax.ppermute(low, "seq", [(i, i - 1) for i in range(n_seq - s, n_seq)])
        grad_inputs, sums1 = leave(dx[0], up, low, tokens, dhidden1, mods)

        def reduced(a, b):
            share = lax.psum_scatter(matmul(a, b).astype(BF), "dp", scatter_dimension=0, tiled=True)
            return lax.psum_scatter(share, "seq", scatter_dimension=1, tiled=True).astype(F32)

        g_proj3 = reduced(left1[:wide], right1[:, wide:])
        g_proj2 = reduced(act1, dr2)
        g_proj1 = reduced(left1[wide:], right1[:, :wide])
        g_fc2 = reduced(left2[:hidden], dmlp)
        g_fc1 = reduced(left2[hidden : hidden + width], right2[:, :hidden])
        g_out = reduced(left2[hidden + width :], right2[:, hidden:])
        g_heads = lax.psum_scatter(
            times_trans(first_all, dqkv).astype(BF), "dp", scatter_dimension=0, tiled=True
        )

    if not fast:
        incoming = exchange(outgoing(g_heads, sums1))
    held = width // n_dp
    slot = jnp.arange(slots, dtype=jnp.int32)[:, None, None]
    whose = image_ids[::tok_dev]
    dmods = incoming[:, held:].reshape(n_seq, 6 * width // n_seq).astype(F32)
    grad_mods = jnp.sum(jnp.where(slot == whose[None, :, None], dmods[None], 0.0), axis=1)
    incoming = incoming[:, :held]
    columns = [jnp.zeros(incoming.shape[1:], BF) for _ in range(3)]
    for source in range(n_seq):
        for i in range(3):
            unit = n_seq * i + source
            columns[unit % 3] = jnp.where(unit // 3 == rank, incoming[source], columns[unit % 3])
    g_qkv = jnp.concatenate(columns, axis=1).astype(F32)

    return (rounded, grad_inputs, grad_mods, g_qkv, g_out, g_fc1, g_fc2, g_proj1, g_proj2, g_proj3)


def solution(mesh):
    tok = P(("dp", "seq"), None)
    in_specs = (tok, P("dp", None), P("dp")) + (P(),) * 7 + (tok, tok)
    out_specs = (tok, tok) + (P("dp", "seq"),) * 8
    return jax.shard_map(shards, mesh=mesh, in_specs=in_specs, out_specs=out_specs, check_vma=False)
```
